32 devices in a mesh: lat: 8 (over y, x, core), lon: 4 (over z).
Axes of the slice: x: 2, y: 2, z: 4, core: 2. Of those that a mesh axis runs over, the one named last changes fastest.
Arguments:
- tracers: float32 [4, 4, 256, 720], P(None, None, 'lat', 'lon'), may hold values from -6 to 6
- courant: float32 [2, 4, 256, 720], P(None, None, 'lat', 'lon'), may hold values from -0.8 to 0.8
- cutoffs: int32 [256], replicated, may hold values from 1 to 360, as said below
Outputs:
- updated: float32 [4, 4, 256, 720], P(None, None, 'lat', 'lon')
- filtered_zonal: float32 [4, 256, 720], P(None, 'lat', 'lon')
The draws below stay inside these ranges and needn't reach their ends.
Inputs may be any that keep to these rules, and one draw needn't show every extreme that they name: cutoffs[j] is 360 for every row j with min(j, 255 - j) >= 64, below 360 for all other rows, and 1 at the two pole rows.
All inputs are finite; a program needn't handle non-finite values.
Results may differ from the reference program's by a relative error of at most 0.0003.
Values sent between devices are 32-bit elements; how exact they have to be, the bound alone decides.
A program may use at most 64 MiB of HBM per device.

```python
import math
import jax
import jax.numpy as jnp
from jax import lax

LEV = 4
TRAC = 4
NLAT = 256
NLON = 720


def draw_cutoffs(key, part):
    row_ids = jnp.arange(NLAT, dtype=jnp.int32)
    distance = jnp.minimum(row_ids, NLAT - 1 - row_ids)
    polar_band = NLAT // 4
    jitter = jax.random.randint(key, (NLAT,), -3, 4, dtype=jnp.int32)
    ramped = 1 + distance * (NLON // 2 - 2) // polar_band + jitter
    ramped = jnp.clip(ramped, 1, NLON // 2 - 1)
    ramped = jnp.where(distance == 0, 1, ramped)
    return jnp.where(distance < polar_band, ramped, NLON // 2).astype(jnp.int32)


def level_of(key, extent, cuts, least, top_value):
    def one(position, shards_of):
        steps = jax.random.uniform(jax.random.fold_in(jax.random.fold_in(key, 6), position), (shards_of,), jnp.float32, least / len(cuts), top_value / len(cuts))
        return jnp.repeat(jnp.exp(steps), extent[position] // shards_of).reshape((-1,) + (1,) * (len(extent) - position - 1))

    gain = one(*cuts[0])
    for cut in cuts[1:]:
        gain = gain * one(*cut)
    return gain


def bell_draw(rng, shape, width, most, shards=(), kind=jnp.bfloat16):
    factor_of = level_of(rng, shape, shards, -0.22, 0.18) if shards else 1.0
    array = jax.random.normal(rng, shape, jnp.float32) * width * factor_of
    return jnp.minimum(jnp.maximum(array, -most), most).astype(kind)


def setup_inputs(seed: int = 0) -> dict:
    arg_keys = jax.random.split(jax.random.key(seed), 4)
    return {
        "tracers": bell_draw(arg_keys[0], (LEV, TRAC, NLAT, NLON), 1.0, 6.0, ((2, 8), (3, 4)), jnp.float32),
        "courant": jnp.clip(jax.random.uniform(arg_keys[1], (2, LEV, NLAT, NLON), jnp.float32, -0.8, 0.8) * level_of(arg_keys[1], (2, LEV, NLAT, NLON), ((2, 8), (3, 4)), -0.4, 0.0), -0.8, 0.8),
        "cutoffs": draw_cutoffs(jax.random.fold_in(arg_keys[3], 71), 0),
    }


def take_range(values, start, count, axis_index):
    return lax.slice_in_dim(values, start, start + count, axis=axis_index)


def ppm_flux(extended, courant_faces, axis_index):
    cell_count = extended.shape[axis_index] - 6
    edge_values = (7.0 / 12.0) * (take_range(extended, 1, cell_count + 3, axis_index) + take_range(extended, 2, cell_count + 3, axis_index)) - (1.0 / 12.0) * (take_range(extended, 0, cell_count + 3, axis_index) + take_range(extended, 3, cell_count + 3, axis_index))
    left_edge = take_range(edge_values, 0, cell_count + 2, axis_index)
    right_edge = take_range(edge_values, 1, cell_count + 2, axis_index)
    centre = take_range(extended, 2, cell_count + 2, axis_index)
    slopes = right_edge - left_edge
    curvature = 6.0 * centre - 3.0 * (left_edge + right_edge)
    upwind = take_range(right_edge, 0, cell_count + 1, axis_index) - 0.5 * courant_faces * (take_range(slopes, 0, cell_count + 1, axis_index) - (1.0 - courant_faces * (2.0 / 3.0)) * take_range(curvature, 0, cell_count + 1, axis_index))
    downwind = take_range(left_edge, 1, cell_count + 1, axis_index) - 0.5 * courant_faces * (take_range(slopes, 1, cell_count + 1, axis_index) + (1.0 + courant_faces * (2.0 / 3.0)) * take_range(curvature, 1, cell_count + 1, axis_index))
    return courant_faces * jnp.where(courant_faces > 0, upwind, downwind)


def metric_weights(first_row, row_count, grid_rows):
    faces = first_row + jnp.arange(-1, row_count, dtype=jnp.int32)
    centres = first_row + jnp.arange(row_count, dtype=jnp.int32)
    face_weight = jnp.sin(jnp.minimum(faces + 1, grid_rows - 1 - faces).astype(jnp.float32) * (math.pi / grid_rows))
    cell_weight = jnp.sin((jnp.minimum(centres, grid_rows - 1 - centres).astype(jnp.float32) + 0.5) * (math.pi / grid_rows))
    return face_weight, cell_weight


def reference(tracers, courant, cutoffs):
    zonal = courant[0]
    meridional = courant[1]
    spectrum = jnp.fft.rfft(zonal, axis=2)
    waves = jnp.arange(NLON // 2 + 1, dtype=jnp.int32)
    keep_mask = waves[None, None, :] <= cutoffs[None, :, None]
    lowpass = jnp.fft.irfft(jnp.where(keep_mask, spectrum, 0.0), n=NLON, axis=2).astype(jnp.float32)
    filtered_zonal = jnp.where((cutoffs < NLON // 2)[None, :, None], lowpass, zonal)
    face_weight, cell_weight = metric_weights(jnp.int32(0), NLAT, NLAT)

    def one_level(items):
        level_tracers, zonal_level, merid_level = items
        lon_ext = jnp.concatenate([level_tracers[:, :, -3:], level_tracers, level_tracers[:, :, :3]], axis=2)
        zonal_faces = jnp.concatenate([zonal_level[:, -1:], zonal_level], axis=1)[None]
        flux_east = ppm_flux(lon_ext, zonal_faces, 2)
        lat_ext = jnp.pad(level_tracers, ((0, 0), (3, 3), (0, 0)))
        merid_faces = jnp.pad(merid_level, ((1, 0), (0, 0)))[None]
        flux_north = ppm_flux(lat_ext, merid_faces, 1) * face_weight[None, :, None]
        change = (flux_east[:, :, 1:] - flux_east[:, :, :-1]) + (flux_north[:, 1:, :] - flux_north[:, :-1, :]) / cell_weight[None, :, None]
        return level_tracers - change

    updated = lax.map(one_level, (tracers, filtered_zonal, meridional))
    return updated, filtered_zonal
```

```python
import functools
import math

import jax
import numpy as np
import jax.numpy as jnp
from jax import lax
from jax.experimental import pallas as pl
from jax.experimental.pallas import tpu as pltpu
from jax.sharding import PartitionSpec as P


def padded(cells, sides, width, closed):
    for axis, dim in sides:
        count = lax.axis_size(axis)
        ends = count if closed else count - 1
        head = lax.slice_in_dim(cells, 0, width, axis=dim)
        tail = lax.slice_in_dim(cells, cells.shape[dim] - width, cells.shape[dim], axis=dim)
        cells = jnp.concatenate(
            [
                lax.ppermute(tail, axis, [(i, (i + 1) % count) for i in range(ends)]),
                cells,
                lax.ppermute(head, axis, [((i + 1) % count, i) for i in range(ends)]),
            ],
            axis=dim,
        )
    return cells


def take_range(values, start, count, axis_index):
    return lax.slice_in_dim(values, start, start + count, axis=axis_index)


def ppm_flux(extended, courant_faces, axis_index):
    cell_count = extended.shape[axis_index] - 6
    edge_values = 7.0 / 12.0 * (
        take_range(extended, 1, cell_count + 3, axis_index)
        + take_range(extended, 2, cell_count + 3, axis_index)
    ) - 1.0 / 12.0 * (
        take_range(extended, 0, cell_count + 3, axis_index)
        + take_range(extended, 3, cell_count + 3, axis_index)
    )
    left_edge = take_range(edge_values, 0, cell_count + 2, axis_index)
    right_edge = take_range(edge_values, 1, cell_count + 2, axis_index)
    centre = take_range(extended, 2, cell_count + 2, axis_index)
    slopes = right_edge - left_edge
    curvature = 6.0 * centre - 3.0 * (left_edge + right_edge)
    upwind = take_range(right_edge, 0, cell_count + 1, axis_index) - 0.5 * courant_faces * (
        take_range(slopes, 0, cell_count + 1, axis_index)
        - (1.0 - courant_faces * (2.0 / 3.0)) * take_range(curvature, 0, cell_count + 1, axis_index)
    )
    downwind = take_range(left_edge, 1, cell_count + 1, axis_index) - 0.5 * courant_faces * (
        take_range(slopes, 1, cell_count + 1, axis_index)
        + (1.0 + courant_faces * (2.0 / 3.0)) * take_range(curvature, 1, cell_count + 1, axis_index)
    )
    return courant_faces * jnp.where(courant_faces > 0, upwind, downwind)


def metric_weights(first_row, row_count, grid_rows):
    faces = first_row + jnp.arange(-1, row_count, dtype=jnp.int32)
    centres = first_row + jnp.arange(row_count, dtype=jnp.int32)
    face_weight = jnp.sin(
        jnp.minimum(faces + 1, grid_rows - 1 - faces).astype(jnp.float32) * (math.pi / grid_rows)
    )
    cell_weight = jnp.sin(
        (jnp.minimum(centres, grid_rows - 1 - centres).astype(jnp.float32) + 0.5)
        * (math.pi / grid_rows)
    )
    return (face_weight, cell_weight)


def angle_table(first_ids, second_ids, period):
    product = first_ids[:, None] * second_ids[None, :] % period
    angles = product.astype(jnp.float32) * (2.0 * math.pi / period)
    return (jnp.cos(angles), jnp.sin(angles))


def spectral_lowpass(row_block, limits, outer_count):
    row_count, circle = row_block.shape
    inner_count = circle // outer_count
    highest = lax.Precision.HIGHEST
    grid_values = row_block.reshape(row_count, outer_count, inner_count)
    outer_ids = jnp.arange(outer_count, dtype=jnp.int32)
    inner_ids = jnp.arange(inner_count, dtype=jnp.int32)
    outer_cos, outer_sin = angle_table(outer_ids, outer_ids, outer_count)
    inner_cos, inner_sin = angle_table(inner_ids, inner_ids, inner_count)
    twiddle_cos, twiddle_sin = angle_table(inner_ids, outer_ids, circle)
    first_real = jnp.einsum("rab,ak->rbk", grid_values, outer_cos, precision=highest)
    first_imag = -jnp.einsum("rab,ak->rbk", grid_values, outer_sin, precision=highest)
    turned_real = first_real * twiddle_cos + first_imag * twiddle_sin
    turned_imag = first_imag * twiddle_cos - first_real * twiddle_sin
    coeff_real = jnp.einsum("rbk,bj->rjk", turned_real, inner_cos, precision=highest) + jnp.einsum(
        "rbk,bj->rjk", turned_imag, inner_sin, precision=highest
    )
    coeff_imag = jnp.einsum("rbk,bj->rjk", turned_imag, inner_cos, precision=highest) - jnp.einsum(
        "rbk,bj->rjk", turned_real, inner_sin, precision=highest
    )
    wavenumber = inner_ids[:, None] * outer_count + outer_ids[None, :]
    folded = jnp.minimum(wavenumber, circle - wavenumber)
    keep_mask = folded[None, :, :] <= limits[:, None, None]
    coeff_real = jnp.where(keep_mask, coeff_real, 0.0)
    coeff_imag = jnp.where(keep_mask, coeff_imag, 0.0)
    back_real = jnp.einsum("rjk,jb->rbk", coeff_real, inner_cos, precision=highest) - jnp.einsum(
        "rjk,jb->rbk", coeff_imag, inner_sin, precision=highest
    )
    back_imag = jnp.einsum("rjk,jb->rbk", coeff_imag, inner_cos, precision=highest) + jnp.einsum(
        "rjk,jb->rbk", coeff_real, inner_sin, precision=highest
    )
    reverted_real = back_real * twiddle_cos - back_imag * twiddle_sin
    reverted_imag = back_imag * twiddle_cos + back_real * twiddle_sin
    signal = jnp.einsum("rbk,ka->rab", reverted_real, outer_cos, precision=highest) - jnp.einsum(
        "rbk,ka->rab", reverted_imag, outer_sin, precision=highest
    )
    return (signal / circle).reshape(row_count, circle)


def general_body(tracers, courant, cutoffs):
    levels, tracer_count, lat_rows, lon_cols = tracers.shape
    lon_groups = lax.axis_size("lon")
    lon_index = lax.axis_index("lon")
    lat_bands = lax.axis_size("lat")
    band_index = lax.axis_index("lat")
    grid_rows = lat_rows * lat_bands
    zonal = courant[0]
    meridional = courant[1]
    lat_stack = jnp.concatenate([tracers, meridional[:, None]], axis=1)
    lat_ext = padded(lat_stack, (("lat", 2),), 3, False)
    flat_count = levels * lat_rows
    flat_zonal = zonal.reshape(flat_count, lon_cols)
    edges = jnp.concatenate([tracers[..., :3], tracers[..., lon_cols - 3 :]], axis=-1)
    west_index = (lon_index + lon_groups - 1) % lon_groups
    east_index = (lon_index + 1) % lon_groups
    local_limits = lax.dynamic_slice_in_dim(cutoffs, band_index * lat_rows, lat_rows)
    limits = jnp.tile(local_limits, levels)
    circle = lon_cols * lon_groups
    gathered = lax.all_gather(flat_zonal, "lon", axis=0)
    gathered_edges = lax.all_gather(edges, "lon", axis=0)
    west = lax.dynamic_index_in_dim(gathered_edges, west_index, 0, keepdims=False)[..., 3:]
    east = lax.dynamic_index_in_dim(gathered_edges, east_index, 0, keepdims=False)[..., :3]
    west_raw = lax.dynamic_index_in_dim(gathered, west_index, 0, keepdims=False)[:, -1:]
    raw_ext = jnp.concatenate([west_raw, flat_zonal], axis=1)
    whole_rows = jnp.transpose(gathered, (1, 0, 2)).reshape(flat_count, circle)
    lowpass = spectral_lowpass(whole_rows, limits, lon_groups)
    lowpass = jnp.concatenate([lowpass[:, -1:], lowpass], axis=1)
    lowpass_ext = lax.dynamic_slice_in_dim(lowpass, lon_index * lon_cols, lon_cols + 1, axis=1)
    lon_ext = jnp.concatenate([west, tracers, east], axis=-1)
    filtered_flat = jnp.where((limits < circle // 2)[:, None], lowpass_ext, raw_ext)
    zonal_faces = filtered_flat.reshape(levels, 1, lat_rows, lon_cols + 1)
    filtered_zonal = zonal_faces[:, 0, :, 1:]
    flux_east = ppm_flux(lon_ext, zonal_faces, 3)
    face_weight, cell_weight = metric_weights(band_index * lat_rows, lat_rows, grid_rows)
    flux_north = (
    ppm_flux(lat_ext[:, :tracer_count], lat_ext[:, tracer_count:, 2 : lat_rows + 3, :], 2)
    * face_weight[None, None, :, None]
    )
    change = (
    flux_east[:, :, :, 1:]
    - flux_east[:, :, :, :-1]
    + (flux_north[:, :, 1:, :] - flux_north[:, :, :-1, :]) / cell_weight[None, None, :, None]
    )
    return (tracers - change, filtered_zonal)


MESH = pl.DeviceIdType.MESH
RINGS = 4
LANES = 128
DEPTH = 192
SENT = 184
EAST, WEST, ACROSS, PACK_EAST, PACK_WEST, NORTH, SOUTH, NORTH_C = range(8)


def split_halves(values):
    high = values.astype(jnp.bfloat16)
    low = (values - high.astype(jnp.float32)).astype(jnp.bfloat16)
    return high, low


def filter_tables(circle, cols):
    half = circle // 2
    cells = np.arange(circle, dtype=np.int64)
    cos_ids = np.arange(half + 1, dtype=np.int64)
    sin_ids = np.arange(1, half, dtype=np.int64)

    def waves(ids):
        return np.concatenate(
            [
                np.cos(2.0 * np.pi * ((cos_ids[:, None] * ids[None, :]) % circle) / circle),
                np.sin(2.0 * np.pi * ((sin_ids[:, None] * ids[None, :]) % circle) / circle),
            ],
            axis=0,
        )

    def halves(table):
        high = table.astype(jnp.bfloat16)
        low = (table - high.astype(np.float64)).astype(jnp.bfloat16)
        return high, low

    forward = np.zeros((circle // cols, circle, DEPTH))
    forward[:, :, :cols] = waves(cells).reshape(circle, circle // cols, cols).transpose(1, 0, 2)
    wavenumber = np.concatenate([cos_ids, sin_ids])
    scale = np.where((wavenumber == 0) | (wavenumber == half), 1.0, 2.0) / circle
    inverse = np.zeros((DEPTH, circle))
    inverse[:cols] = waves(np.arange(cols)).T * scale
    inverse[DEPTH - 1] = waves(np.array([-1]))[:, 0] * scale
    return halves(forward) + halves(inverse)


def weight_tables(bands, rows, cols):
    grid_rows = bands * rows
    faces = np.arange(bands)[:, None] * rows + np.arange(-8, rows)[None, :]
    cells = np.arange(bands)[:, None] * rows + np.arange(rows)[None, :]
    face = np.sin(np.minimum(faces + 1, grid_rows - 1 - faces) * (np.pi / grid_rows))
    cell = 1.0 / np.sin((np.minimum(cells, grid_rows - 1 - cells) + 0.5) * (np.pi / grid_rows))
    face = np.broadcast_to(face[:, :, None], face.shape + (cols,))
    cell = np.broadcast_to(cell[:, :, None], cell.shape + (cols,))
    return face.astype(np.float32), cell.astype(np.float32)


def flux_factors(courant, scale):
    size = jnp.abs(courant)
    steep = size - size * size
    middle = 3.0 * size - 2.0 * size * size
    scaled = courant * scale
    return (
        scaled * (1.0 + steep - middle) * (1.0 / 12.0),
        scaled * steep * (-1.0 / 12.0),
        scaled * middle,
    )


def kernel(
    sizes,
    tracers, courant, cutoffs, ahead_hi, ahead_lo, back_hi, back_lo, face_w, cell_w,
    updated, filtered,
    zonal, cells, merid, blocks, total, table_hi, table_lo, inv_hi, inv_lo, limit_v, face_v, cell_v,
    pack, packs, border, wide, turned, edges, rest,
    load_sem, send_sem, recv_sem, ready,
):
    levels, count, rows, cols, bands, polar_bands, circle = sizes
    flat = levels * rows
    z = lax.axis_index("lon")
    band = lax.axis_index("lat")
    polar = (band < polar_bands) | (band >= bands - polar_bands)
    has_south = band > 0
    has_north = band < bands - 1
    tail = cols - LANES
    barrier = pltpu.get_barrier_semaphore()

    def load(index, source, target):
        return pltpu.make_async_copy(source, target, load_sem.at[index])

    own_cells = cells.at[:, :, pl.ds(8, rows), :]
    load_zonal = load(0, courant.at[0], zonal)
    load_cells = load(1, tracers, own_cells)
    load_merid = load(2, courant.at[1], merid.at[:, pl.ds(8, rows), :])
    load_limit = load(3, cutoffs, limit_v)
    load_face = load(4, face_w.at[band], face_v)
    load_cell = load(5, cell_w.at[band], cell_v)
    load_tables = [
        load(6, ahead_hi, table_hi),
        load(7, ahead_lo, table_lo),
        load(8, back_hi, inv_hi),
        load(9, back_lo, inv_lo),
    ]
    load_zonal.start()
    for other in range(1, RINGS):
        @pl.when(z < other)
        def _():
            pl.semaphore_signal(barrier, inc=1, device_id={"lon": other}, device_id_type=MESH)

    @pl.when(has_south)
    def _():
        pl.semaphore_signal(barrier, inc=1, device_id={"lat": band - 1}, device_id_type=MESH)

    @pl.when(has_north)
    def _():
        pl.semaphore_signal(barrier, inc=1, device_id={"lat": band + 1}, device_id_type=MESH)

    load_cells.start()
    load_merid.start()
    load_face.start()
    load_cell.start()

    @pl.when(polar)
    def _():
        load_limit.start()
        for copy in load_tables:
            copy.start()

    blocks[0, SENT - 8 : DEPTH] = jnp.zeros((DEPTH - SENT + 8, LANES), jnp.float32)
    for slot in range(1, RINGS):
        blocks[slot, SENT:DEPTH] = jnp.zeros((DEPTH - SENT, LANES), jnp.float32)
    border[...] = jnp.zeros_like(border)
    turned[DEPTH:, :] = jnp.zeros((2 * LANES - DEPTH, LANES), jnp.float32)

    @pl.when(jnp.logical_not(has_south))
    def _():
        cells[:, :, 0:8, :] = jnp.zeros((levels, count, 8, cols), jnp.float32)
        merid[:, 0:8, :] = jnp.zeros((levels, 8, cols), jnp.float32)

    @pl.when(jnp.logical_not(has_north))
    def _():
        cells[:, :, rows + 8 :, :] = jnp.zeros((levels, count, 8, cols), jnp.float32)

    load_zonal.wait()
    blocks[0, :LANES] = zonal[:, :, :LANES].reshape(flat, LANES).T
    blocks[0, LANES:cols] = zonal[:, :, LANES:].reshape(flat, tail).T

    def remote(index, source, target, where):
        return pltpu.make_async_remote_copy(
            src_ref=source,
            dst_ref=target,
            send_sem=send_sem.at[index],
            recv_sem=recv_sem.at[index],
            device_id=where,
            device_id_type=MESH,
        )

    east = lax.rem(z + 1, RINGS)
    west = lax.rem(z + 3, RINGS)
    across = lax.rem(z + 2, RINGS)
    own = blocks.at[0, pl.ds(0, SENT)]
    send_east = remote(EAST, own, blocks.at[3, pl.ds(0, SENT)], {"lon": east})
    send_west = remote(WEST, own, blocks.at[1, pl.ds(0, SENT)], {"lon": west})
    send_across = remote(ACROSS, own, blocks.at[2, pl.ds(0, SENT)], {"lon": across})
    pack_east = remote(PACK_EAST, pack.at[0], packs.at[0], {"lon": east})
    pack_west = remote(PACK_WEST, pack.at[1], packs.at[1], {"lon": west})
    send_north = remote(
        NORTH, tracers.at[:, :, pl.ds(rows - 8, 8), :], cells.at[:, :, pl.ds(0, 8), :], {"lat": band + 1}
    )
    send_south = remote(
        SOUTH, tracers.at[:, :, pl.ds(0, 8), :], cells.at[:, :, pl.ds(rows + 8, 8), :], {"lat": band - 1}
    )
    send_north_c = remote(
        NORTH_C, courant.at[1, :, pl.ds(rows - 8, 8), :], merid.at[:, pl.ds(0, 8), :], {"lat": band + 1}
    )

    pl.semaphore_wait(barrier, z + has_south.astype(jnp.int32) + has_north.astype(jnp.int32))
    for other in range(RINGS - 1):
        @pl.when(z > other)
        def _():
            pl.semaphore_signal(ready.at[z], inc=1, device_id={"lon": other}, device_id_type=MESH)

    def send_zonal(chosen):
        for copy, where in ((send_east, east), (send_west, west), (send_across, across)):
            @pl.when(polar & chosen(where))
            def _():
                copy.start()

    def send_packs(chosen):
        for copy, where in ((pack_east, east), (pack_west, west)):
            @pl.when(chosen(where))
            def _():
                copy.start()

    send_zonal(lambda where: where < z)

    @pl.when(has_north)
    def _():
        send_north.start()
        send_north_c.start()

    @pl.when(has_south)
    def _():
        send_south.start()

    load_cells.wait()
    for t in range(count):
        first = cells[:, t, 8 : rows + 8, :LANES].reshape(flat, LANES).T
        last = cells[:, t, 8 : rows + 8, LANES:].reshape(flat, tail).T
        pack[0, t, 0:3] = last[tail - 3 : tail]
        pack[1, t, 0:3] = first[0:3]
    pack[0, count, 0:1] = blocks[0, cols - 1 : cols]
    send_packs(lambda where: where < z)

    def forward(slot):
        high, low = split_halves(blocks[slot])
        both = jnp.dot(
            table_hi[slot], jnp.concatenate([high, low], axis=1), preferred_element_type=jnp.float32
        )
        rest_term = jnp.dot(table_lo[slot], high, preferred_element_type=jnp.float32)
        return both[:, :LANES] + (both[:, LANES:] + rest_term)

    @pl.when(polar)
    def _():
        for copy in load_tables:
            copy.wait()
        load_limit.wait()
        total[...] = forward(0)

    for other in range(1, RINGS):
        @pl.when(z < other)
        def _():
            pl.semaphore_wait(ready.at[other], 1)
            send_zonal(lambda where: where == other)
            send_packs(lambda where: where == other)

    load_merid.wait()
    load_face.wait()
    load_cell.wait()

    @pl.when(has_south)
    def _():
        send_north.wait_recv()
        send_north_c.wait_recv()

    @pl.when(has_north)
    def _():
        send_south.wait_recv()

    for level in range(levels):
        speed = merid[level, 7 : rows + 8]
        speed_row = lax.broadcasted_iota(jnp.int32, speed.shape, 0)
        speed = jnp.where((speed_row == 0) & jnp.logical_not(has_south), 0.0, speed)
        by_face, by_edge, by_cell = flux_factors(speed, face_v[7 : rows + 8])
        upward = speed > 0
        inverse_cell = cell_v[...]

        def merid_step(t, carry):
            def shifted(offset):
                return cells[level, t, pl.ds(7 + offset, rows + 1), :]

            below, here, above, beyond = shifted(-1), shifted(0), shifted(1), shifted(2)
            edge_here = 7.0 * (below + here) - (shifted(-2) + above)
            edge_face = 7.0 * (here + above) - (below + beyond)
            edge_next = 7.0 * (above + beyond) - (here + shifted(3))
            flux = (
                by_face * edge_face
                + by_edge * jnp.where(upward, edge_here, edge_next)
                + by_cell * jnp.where(upward, here, above)
            )
            change = (flux[1:] - flux[:-1]) * inverse_cell
            rest[level, t] = cells[level, t, 8 : rows + 8, :] - change
            return carry

        lax.fori_loop(0, count, merid_step, 0)

    pack_east.wait_recv()
    pack_west.wait_recv()
    for t in range(count):
        border[t, tail : tail + 3] = packs[1, t, 0:3]
        border[t, LANES - 3 : LANES] = packs[0, t, 0:3]
        halo = border[t].T.reshape(levels, rows, LANES)
        wide[:, t, :, :LANES] = cells[:, t, 8 : rows + 8, :LANES]
        wide[:, t, :, LANES:] = halo
        wide[:, t, :, LANES:cols] = cells[:, t, 8 : rows + 8, LANES:]

    def zonal_edges(index, carry):
        level, t = index // count, index % count
        here = wide[level, t]
        pair = here + pltpu.roll(here, 1, 1)
        edges[level, t] = 8.0 * pair - (pltpu.roll(pair, 1, 1) + pltpu.roll(pair, 2 * LANES - 1, 1))
        return carry

    lax.fori_loop(0, levels * count, zonal_edges, 0)

    @pl.when(jnp.logical_not(polar))
    def _():
        turned[:cols] = blocks[0, :cols]

    @pl.when(polar)
    def _():
        send_west.wait_recv()
        total[...] += forward(1)
        send_across.wait_recv()
        total[...] += forward(2)
        lane = lax.broadcasted_iota(jnp.int32, (8, 2 * LANES), 1)
        spread = jnp.broadcast_to(limit_v[...].reshape(1, bands * rows), (8, bands * rows))
        spread = pltpu.roll(spread, lax.rem((bands - band) * rows, bands * rows), 1)
        limit = jnp.where(lane < rows, spread, 0)
        copies = 1
        while copies < levels:
            limit = limit + pltpu.roll(limit, copies * rows, 1)
            copies *= 2
        limit = limit[0:1, :LANES]
        wave = lax.broadcasted_iota(jnp.int32, (circle, LANES), 0)
        wave = jnp.where(wave <= circle // 2, wave, wave - circle // 2)
        send_east.wait_recv()
        coeff = jnp.where(wave <= limit, total[...] + forward(3), 0.0)
        high, low = split_halves(coeff)
        both = jnp.dot(
            inv_hi[...], jnp.concatenate([high, low], axis=1), preferred_element_type=jnp.float32
        )
        rest_term = jnp.dot(inv_lo[...], high, preferred_element_type=jnp.float32)
        smooth = both[:, :LANES] + (both[:, LANES:] + rest_term)
        kept = limit < circle // 2
        turned[:cols] = jnp.where(kept, smooth[:cols], blocks[0, :cols])
        turned[2 * LANES - 8 :] = jnp.broadcast_to(
            jnp.where(kept, smooth[DEPTH - 1 :], packs[0, count, 0:1]), (8, LANES)
        )

    @pl.when(jnp.logical_not(polar))
    def _():
        turned[2 * LANES - 8 :] = jnp.broadcast_to(packs[0, count, 0:1], (8, LANES))

    for level in range(levels):
        speed = turned[:, level * rows : (level + 1) * rows]
        border_speed = jnp.concatenate([speed[:LANES].T, speed[LANES:].T], axis=1)
        filtered[level] = border_speed[:, :cols]
        by_face, by_edge, by_cell = flux_factors(border_speed, 1.0)
        eastward = border_speed > 0

        def zonal_step(t, carry):
            edge = edges[level, t]
            here = wide[level, t]
            flux = (
                by_face * pltpu.roll(edge, 2 * LANES - 1, 1)
                + by_edge * jnp.where(eastward, edge, pltpu.roll(edge, 2 * LANES - 2, 1))
                + by_cell * jnp.where(eastward, here, pltpu.roll(here, 2 * LANES - 1, 1))
            )
            change = flux - pltpu.roll(flux, 1, 1)
            updated[level, t] = rest[level, t] - change[:, :cols]
            return carry

        lax.fori_loop(0, count, zonal_step, 0)

    pack_east.wait_send()
    pack_west.wait_send()

    @pl.when(polar)
    def _():
        send_east.wait_send()
        send_west.wait_send()
        send_across.wait_send()

    @pl.when(has_north)
    def _():
        send_north.wait_send()
        send_north_c.wait_send()

    @pl.when(has_south)
    def _():
        send_south.wait_send()


def ring_body(bands, tracers, courant, cutoffs):
    levels, count, rows, cols = tracers.shape
    circle = cols * RINGS
    sizes = (levels, count, rows, cols, bands, bands // 4, circle)
    ahead_hi, ahead_lo, back_hi, back_lo = filter_tables(circle, cols)
    face_w, cell_w = weight_tables(bands, rows, cols)
    any_space = pl.BlockSpec(memory_space=pl.ANY)
    vmem = pl.BlockSpec(memory_space=pltpu.VMEM)
    f32, half = jnp.float32, jnp.bfloat16
    slab = (levels, count, rows)
    return pl.pallas_call(
        functools.partial(kernel, sizes),
        out_shape=(
            jax.ShapeDtypeStruct(tracers.shape, f32),
            jax.ShapeDtypeStruct((levels, rows, cols), f32),
        ),
        in_specs=[any_space] * 9,
        out_specs=(vmem, vmem),
        scratch_shapes=[
            pltpu.VMEM((levels, rows, cols), f32),
            pltpu.VMEM((levels, count, rows + 16, cols), f32),
            pltpu.VMEM((levels, rows + 8, cols), f32),
            pltpu.VMEM((RINGS, DEPTH, LANES), f32),
            pltpu.VMEM((circle, LANES), f32),
            pltpu.VMEM((RINGS, circle, DEPTH), half),
            pltpu.VMEM((RINGS, circle, DEPTH), half),
            pltpu.VMEM((DEPTH, circle), half),
            pltpu.VMEM((DEPTH, circle), half),
            pltpu.VMEM((bands * rows,), jnp.int32),
            pltpu.VMEM((rows + 8, cols), f32),
            pltpu.VMEM((rows, cols), f32),
            pltpu.VMEM((2, count + 1, 8, LANES), f32),
            pltpu.VMEM((2, count + 1, 8, LANES), f32),
            pltpu.VMEM((count, LANES, LANES), f32),
            pltpu.VMEM(slab + (2 * LANES,), f32),
            pltpu.VMEM((2 * LANES, LANES), f32),
            pltpu.VMEM(slab + (2 * LANES,), f32),
            pltpu.VMEM(slab + (cols,), f32),
            pltpu.SemaphoreType.DMA((10,)),
            pltpu.SemaphoreType.DMA((8,)),
            pltpu.SemaphoreType.DMA((8,)),
            pltpu.SemaphoreType.REGULAR((RINGS,)),
        ],
        compiler_params=pltpu.CompilerParams(
            collective_id=0, has_side_effects=True, vmem_limit_bytes=60 * 2**20
        ),
    )(
        tracers, courant, cutoffs,
        jnp.asarray(ahead_hi), jnp.asarray(ahead_lo), jnp.asarray(back_hi), jnp.asarray(back_lo),
        jnp.asarray(face_w), jnp.asarray(cell_w),
    )


def body(bands, tracers, courant, cutoffs):
    levels, _, rows, cols = tracers.shape
    fits = (
        lax.axis_size("lon") == RINGS
        and bands % 4 == 0
        and bands * rows == 2 * LANES
        and levels * rows == LANES
        and LANES < cols <= SENT
        and cols % 4 == 0
    )
    if fits:
        return ring_body(bands, tracers, courant, cutoffs)
    return general_body(tracers, courant, cutoffs)


def solution(mesh):
    in_specs = (P(None, None, "lat", "lon"), P(None, None, "lat", "lon"), P())
    out_specs = (P(None, None, "lat", "lon"), P(None, "lat", "lon"))
    return jax.shard_map(
        functools.partial(body, mesh.shape["lat"]),
        mesh=mesh,
        in_specs=in_specs,
        out_specs=out_specs,
        check_vma=False,
    )
```

```python
import functools
import math

import jax
import numpy as np
import jax.numpy as jnp
from jax import lax
from jax.experimental import pallas as pl
from jax.experimental.pallas import tpu as pltpu
from jax.sharding import PartitionSpec as P


def padded(cells, sides, width, closed):
    for axis, dim in sides:
        count = lax.axis_size(axis)
        ends = count if closed else count - 1
        head = lax.slice_in_dim(cells, 0, width, axis=dim)
        tail = lax.slice_in_dim(cells, cells.shape[dim] - width, cells.shape[dim], axis=dim)
        cells = jnp.concatenate(
            [
                lax.ppermute(tail, axis, [(i, (i + 1) % count) for i in range(ends)]),
                cells,
                lax.ppermute(head, axis, [((i + 1) % count, i) for i in range(ends)]),
            ],
            axis=dim,
        )
    return cells


def take_range(values, start, count, axis_index):
    return lax.slice_in_dim(values, start, start + count, axis=axis_index)


def ppm_flux(extended, courant_faces, axis_index):
    cell_count = extended.shape[axis_index] - 6
    edge_values = 7.0 / 12.0 * (
        take_range(extended, 1, cell_count + 3, axis_index)
        + take_range(extended, 2, cell_count + 3, axis_index)
    ) - 1.0 / 12.0 * (
        take_range(extended, 0, cell_count + 3, axis_index)
        + take_range(extended, 3, cell_count + 3, axis_index)
    )
    left_edge = take_range(edge_values, 0, cell_count + 2, axis_index)
    right_edge = take_range(edge_values, 1, cell_count + 2, axis_index)
    centre = take_range(extended, 2, cell_count + 2, axis_index)
    slopes = right_edge - left_edge
    curvature = 6.0 * centre - 3.0 * (left_edge + right_edge)
    upwind = take_range(right_edge, 0, cell_count + 1, axis_index) - 0.5 * courant_faces * (
        take_range(slopes, 0, cell_count + 1, axis_index)
        - (1.0 - courant_faces * (2.0 / 3.0)) * take_range(curvature, 0, cell_count + 1, axis_index)
    )
    downwind = take_range(left_edge, 1, cell_count + 1, axis_index) - 0.5 * courant_faces * (
        take_range(slopes, 1, cell_count + 1, axis_index)
        + (1.0 + courant_faces * (2.0 / 3.0)) * take_range(curvature, 1, cell_count + 1, axis_index)
    )
    return courant_faces * jnp.where(courant_faces > 0, upwind, downwind)


def metric_weights(first_row, row_count, grid_rows):
    faces = first_row + jnp.arange(-1, row_count, dtype=jnp.int32)
    centres = first_row + jnp.arange(row_count, dtype=jnp.int32)
    face_weight = jnp.sin(
        jnp.minimum(faces + 1, grid_rows - 1 - faces).astype(jnp.float32) * (math.pi / grid_rows)
    )
    cell_weight = jnp.sin(
        (jnp.minimum(centres, grid_rows - 1 - centres).astype(jnp.float32) + 0.5)
        * (math.pi / grid_rows)
    )
    return (face_weight, cell_weight)


def angle_table(first_ids, second_ids, period):
    product = first_ids[:, None] * second_ids[None, :] % period
    angles = product.astype(jnp.float32) * (2.0 * math.pi / period)
    return (jnp.cos(angles), jnp.sin(angles))


def spectral_lowpass(row_block, limits, outer_count):
    row_count, circle = row_block.shape
    inner_count = circle // outer_count
    highest = lax.Precision.HIGHEST
    grid_values = row_block.reshape(row_count, outer_count, inner_count)
    outer_ids = jnp.arange(outer_count, dtype=jnp.int32)
    inner_ids = jnp.arange(inner_count, dtype=jnp.int32)
    outer_cos, outer_sin = angle_table(outer_ids, outer_ids, outer_count)
    inner_cos, inner_sin = angle_table(inner_ids, inner_ids, inner_count)
    twiddle_cos, twiddle_sin = angle_table(inner_ids, outer_ids, circle)
    first_real = jnp.einsum("rab,ak->rbk", grid_values, outer_cos, precision=highest)
    first_imag = -jnp.einsum("rab,ak->rbk", grid_values, outer_sin, precision=highest)
    turned_real = first_real * twiddle_cos + first_imag * twiddle_sin
    turned_imag = first_imag * twiddle_cos - first_real * twiddle_sin
    coeff_real = jnp.einsum("rbk,bj->rjk", turned_real, inner_cos, precision=highest) + jnp.einsum(
        "rbk,bj->rjk", turned_imag, inner_sin, precision=highest
    )
    coeff_imag = jnp.einsum("rbk,bj->rjk", turned_imag, inner_cos, precision=highest) - jnp.einsum(
        "rbk,bj->rjk", turned_real, inner_sin, precision=highest
    )
    wavenumber = inner_ids[:, None] * outer_count + outer_ids[None, :]
    folded = jnp.minimum(wavenumber, circle - wavenumber)
    keep_mask = folded[None, :, :] <= limits[:, None, None]
    coeff_real = jnp.where(keep_mask, coeff_real, 0.0)
    coeff_imag = jnp.where(keep_mask, coeff_imag, 0.0)
    back_real = jnp.einsum("rjk,jb->rbk", coeff_real, inner_cos, precision=highest) - jnp.einsum(
        "rjk,jb->rbk", coeff_imag, inner_sin, precision=highest
    )
    back_imag = jnp.einsum("rjk,jb->rbk", coeff_imag, inner_cos, precision=highest) + jnp.einsum(
        "rjk,jb->rbk", coeff_real, inner_sin, precision=highest
    )
    reverted_real = back_real * twiddle_cos - back_imag * twiddle_sin
    reverted_imag = back_imag * twiddle_cos + back_real * twiddle_sin
    signal = jnp.einsum("rbk,ka->rab", reverted_real, outer_cos, precision=highest) - jnp.einsum(
        "rbk,ka->rab", reverted_imag, outer_sin, precision=highest
    )
    return (signal / circle).reshape(row_count, circle)


def general_body(tracers, courant, cutoffs):
    levels, tracer_count, lat_rows, lon_cols = tracers.shape
    lon_groups = lax.axis_size("lon")
    lon_index = lax.axis_index("lon")
    lat_bands = lax.axis_size("lat")
    band_index = lax.axis_index("lat")
    grid_rows = lat_rows * lat_bands
    zonal = courant[0]
    meridional = courant[1]
    lat_stack = jnp.concatenate([tracers, meridional[:, None]], axis=1)
    lat_ext = padded(lat_stack, (("lat", 2),), 3, False)
    flat_count = levels * lat_rows
    flat_zonal = zonal.reshape(flat_count, lon_cols)
    edges = jnp.concatenate([tracers[..., :3], tracers[..., lon_cols - 3 :]], axis=-1)
    west_index = (lon_index + lon_groups - 1) % lon_groups
    east_index = (lon_index + 1) % lon_groups
    local_limits = lax.dynamic_slice_in_dim(cutoffs, band_index * lat_rows, lat_rows)
    limits = jnp.tile(local_limits, levels)
    circle = lon_cols * lon_groups
    gathered = lax.all_gather(flat_zonal, "lon", axis=0)
    gathered_edges = lax.all_gather(edges, "lon", axis=0)
    west = lax.dynamic_index_in_dim(gathered_edges, west_index, 0, keepdims=False)[..., 3:]
    east = lax.dynamic_index_in_dim(gathered_edges, east_index, 0, keepdims=False)[..., :3]
    west_raw = lax.dynamic_index_in_dim(gathered, west_index, 0, keepdims=False)[:, -1:]
    raw_ext = jnp.concatenate([west_raw, flat_zonal], axis=1)
    whole_rows = jnp.transpose(gathered, (1, 0, 2)).reshape(flat_count, circle)
    lowpass = spectral_lowpass(whole_rows, limits, lon_groups)
    lowpass = jnp.concatenate([lowpass[:, -1:], lowpass], axis=1)
    lowpass_ext = lax.dynamic_slice_in_dim(lowpass, lon_index * lon_cols, lon_cols + 1, axis=1)
    lon_ext = jnp.concatenate([west, tracers, east], axis=-1)
    filtered_flat = jnp.where((limits < circle // 2)[:, None], lowpass_ext, raw_ext)
    zonal_faces = filtered_flat.reshape(levels, 1, lat_rows, lon_cols + 1)
    filtered_zonal = zonal_faces[:, 0, :, 1:]
    flux_east = ppm_flux(lon_ext, zonal_faces, 3)
    face_weight, cell_weight = metric_weights(band_index * lat_rows, lat_rows, grid_rows)
    flux_north = (
    ppm_flux(lat_ext[:, :tracer_count], lat_ext[:, tracer_count:, 2 : lat_rows + 3, :], 2)
    * face_weight[None, None, :, None]
    )
    change = (
    flux_east[:, :, :, 1:]
    - flux_east[:, :, :, :-1]
    + (flux_north[:, :, 1:, :] - flux_north[:, :, :-1, :]) / cell_weight[None, None, :, None]
    )
    return (tracers - change, filtered_zonal)


MESH = pl.DeviceIdType.MESH
RINGS = 4
LANES = 128
DEPTH = 192
SENT = 184
EAST, WEST, ACROSS, PACK_EAST, PACK_WEST, NORTH, SOUTH, NORTH_C = range(8)


def split_halves(values):
    high = values.astype(jnp.bfloat16)
    low = (values - high.astype(jnp.float32)).astype(jnp.bfloat16)
    return high, low


def filter_tables(circle, cols):
    half = circle // 2
    cells = np.arange(circle, dtype=np.int64)
    cos_ids = np.arange(half + 1, dtype=np.int64)
    sin_ids = np.arange(1, half, dtype=np.int64)

    def waves(ids):
        return np.concatenate(
            [
                np.cos(2.0 * np.pi * ((cos_ids[:, None] * ids[None, :]) % circle) / circle),
                np.sin(2.0 * np.pi * ((sin_ids[:, None] * ids[None, :]) % circle) / circle),
            ],
            axis=0,
        )

    def halves(table):
        high = table.astype(jnp.bfloat16)
        low = (table - high.astype(np.float64)).astype(jnp.bfloat16)
        return high, low

    forward = np.zeros((circle // cols, circle, DEPTH))
    forward[:, :, :cols] = waves(cells).reshape(circle, circle // cols, cols).transpose(1, 0, 2)
    wavenumber = np.concatenate([cos_ids, sin_ids])
    scale = np.where((wavenumber == 0) | (wavenumber == half), 1.0, 2.0) / circle
    inverse = np.zeros((DEPTH, circle))
    inverse[:cols] = waves(np.arange(cols)).T * scale
    inverse[DEPTH - 1] = waves(np.array([-1]))[:, 0] * scale
    return halves(forward) + halves(inverse)


def weight_tables(bands, rows, cols):
    grid_rows = bands * rows
    faces = np.arange(bands)[:, None] * rows + np.arange(-8, rows)[None, :]
    cells = np.arange(bands)[:, None] * rows + np.arange(rows)[None, :]
    face = np.sin(np.minimum(faces + 1, grid_rows - 1 - faces) * (np.pi / grid_rows))
    cell = 1.0 / np.sin((np.minimum(cells, grid_rows - 1 - cells) + 0.5) * (np.pi / grid_rows))
    face = np.broadcast_to(face[:, :, None], face.shape + (cols,))
    cell = np.broadcast_to(cell[:, :, None], cell.shape + (cols,))
    return face.astype(np.float32), cell.astype(np.float32)


def flux_factors(courant, scale):
    size = jnp.abs(courant)
    steep = size - size * size
    middle = 3.0 * size - 2.0 * size * size
    scaled = courant * scale
    return (
        scaled * (1.0 + steep - middle) * (1.0 / 12.0),
        scaled * steep * (-1.0 / 12.0),
        scaled * middle,
    )


def gather_kernel(
    sizes,
    tracers, courant, cutoffs, ahead_hi, ahead_lo, back_hi, back_lo, face_w, cell_w,
    faces, here_out, next_out, edge_out, face_out, beyond_out, rest,
    zonal, cells, merid, blocks, total, table_hi, table_lo, inv_hi, inv_lo, limit_v, face_v, cell_v,
    pack, packs, border, turned,
    load_sem, send_sem, recv_sem, ready,
):
    levels, count, rows, cols, bands, polar_bands, circle = sizes
    flat = levels * rows
    z = lax.axis_index("lon")
    band = lax.axis_index("lat")
    polar = (band < polar_bands) | (band >= bands - polar_bands)
    has_south = band > 0
    has_north = band < bands - 1
    tail = cols - LANES
    barrier = pltpu.get_barrier_semaphore()

    def load(index, source, target):
        return pltpu.make_async_copy(source, target, load_sem.at[index])

    load_zonal = load(0, courant.at[0], zonal)
    load_cells = load(1, tracers, cells.at[:, :, pl.ds(8, rows), :])
    load_merid = load(2, courant.at[1], merid.at[:, pl.ds(8, rows), :])
    load_limit = load(3, cutoffs, limit_v)
    load_face = load(4, face_w.at[band], face_v)
    load_cell = load(5, cell_w.at[band], cell_v)
    load_tables = [
        load(6, ahead_hi, table_hi),
        load(7, ahead_lo, table_lo),
        load(8, back_hi, inv_hi),
        load(9, back_lo, inv_lo),
    ]
    load_zonal.start()
    for other in range(1, RINGS):
        @pl.when(z < other)
        def _():
            pl.semaphore_signal(barrier, inc=1, device_id={"lon": other}, device_id_type=MESH)

    @pl.when(has_south)
    def _():
        pl.semaphore_signal(barrier, inc=1, device_id={"lat": band - 1}, device_id_type=MESH)

    @pl.when(has_north)
    def _():
        pl.semaphore_signal(barrier, inc=1, device_id={"lat": band + 1}, device_id_type=MESH)

    load_cells.start()
    pl.semaphore_wait(barrier, z + has_south.astype(jnp.int32) + has_north.astype(jnp.int32))
    for other in range(RINGS - 1):
        @pl.when(z > other)
        def _():
            pl.semaphore_signal(ready.at[z], inc=1, device_id={"lon": other}, device_id_type=MESH)

    blocks[0, SENT - 8 : DEPTH] = jnp.zeros((DEPTH - SENT + 8, LANES), jnp.float32)
    load_zonal.wait()
    blocks[0, :LANES] = zonal[:, :, :LANES].reshape(flat, LANES).T
    blocks[0, LANES:cols] = zonal[:, :, LANES:].reshape(flat, tail).T

    def remote(index, source, target, where):
        return pltpu.make_async_remote_copy(
            src_ref=source,
            dst_ref=target,
            send_sem=send_sem.at[index],
            recv_sem=recv_sem.at[index],
            device_id=where,
            device_id_type=MESH,
        )

    east = lax.rem(z + 1, RINGS)
    west = lax.rem(z + 3, RINGS)
    across = lax.rem(z + 2, RINGS)
    own = blocks.at[0, pl.ds(0, SENT)]
    send_east = remote(EAST, own, blocks.at[3, pl.ds(0, SENT)], {"lon": east})
    send_west = remote(WEST, own, blocks.at[1, pl.ds(0, SENT)], {"lon": west})
    send_across = remote(ACROSS, own, blocks.at[2, pl.ds(0, SENT)], {"lon": across})
    pack_east = remote(PACK_EAST, pack.at[0], packs.at[0], {"lon": east})
    pack_west = remote(PACK_WEST, pack.at[1], packs.at[1], {"lon": west})
    send_north = remote(
        NORTH, tracers.at[:, :, pl.ds(rows - 8, 8), :], cells.at[:, :, pl.ds(0, 8), :], {"lat": band + 1}
    )
    send_south = remote(
        SOUTH, tracers.at[:, :, pl.ds(0, 8), :], cells.at[:, :, pl.ds(rows + 8, 8), :], {"lat": band - 1}
    )
    send_north_c = remote(
        NORTH_C, courant.at[1, :, pl.ds(rows - 8, 8), :], merid.at[:, pl.ds(0, 8), :], {"lat": band + 1}
    )
    last_ring = z == RINGS - 1

    @pl.when(polar & (east < z))
    def _():
        send_east.start()

    @pl.when(polar & (west < z))
    def _():
        send_west.start()

    @pl.when(polar & (across < z) & jnp.logical_not(last_ring))
    def _():
        send_across.start()

    @pl.when(has_north)
    def _():
        send_north.start()
        send_north_c.start()

    @pl.when(has_south)
    def _():
        send_south.start()

    load_merid.start()
    load_face.start()
    load_cell.start()

    @pl.when(polar)
    def _():
        load_limit.start()
        for copy in load_tables:
            copy.start()

    load_cells.wait()
    for t in range(count):
        first = cells[:, t, 8 : rows + 8, :LANES].reshape(flat, LANES).T
        last = cells[:, t, 8 : rows + 8, LANES:].reshape(flat, tail).T
        pack[0, t, 0:3] = last[tail - 3 : tail]
        pack[1, t, 0:3] = first[0:3]
    pack[0, count, 0:1] = blocks[0, cols - 1 : cols]

    @pl.when(east < z)
    def _():
        pack_east.start()

    @pl.when(west < z)
    def _():
        pack_west.start()

    for slot in range(1, RINGS):
        blocks[slot, SENT:DEPTH] = jnp.zeros((DEPTH - SENT, LANES), jnp.float32)

    def forward(slot):
        high, low = split_halves(blocks[slot])
        both = jnp.dot(
            table_hi[slot], jnp.concatenate([high, low], axis=1), preferred_element_type=jnp.float32
        )
        rest_term = jnp.dot(table_lo[slot], high, preferred_element_type=jnp.float32)
        return both[:, :LANES] + (both[:, LANES:] + rest_term)

    @pl.when(polar)
    def _():
        for copy in load_tables:
            copy.wait()
        load_limit.wait()
        total[...] = forward(0)

    @pl.when(polar & last_ring)
    def _():
        send_east.wait_send()
        send_across.start()

    for other in range(1, RINGS):
        @pl.when(z < other)
        def _():
            pl.semaphore_wait(ready.at[other], 1)
            for copy, where in ((send_east, east), (send_west, west), (send_across, across)):
                @pl.when(polar & (where == other))
                def _():
                    copy.start()
            for copy, where in ((pack_east, east), (pack_west, west)):
                @pl.when(where == other)
                def _():
                    copy.start()

    load_merid.wait()
    load_face.wait()
    load_cell.wait()

    @pl.when(has_south)
    def _():
        send_north.wait_recv()
        send_north_c.wait_recv()

    @pl.when(has_north)
    def _():
        send_south.wait_recv()

    @pl.when(jnp.logical_not(has_south))
    def _():
        cells[:, :, 0:8, :] = jnp.zeros((levels, count, 8, cols), jnp.float32)
        merid[:, 0:8, :] = jnp.zeros((levels, 8, cols), jnp.float32)

    @pl.when(jnp.logical_not(has_north))
    def _():
        cells[:, :, rows + 8 :, :] = jnp.zeros((levels, count, 8, cols), jnp.float32)

    for level in range(levels):
        speed = merid[level, 7 : rows + 8]
        by_face, by_edge, by_cell = flux_factors(speed, face_v[7 : rows + 8])
        upward = (speed > 0)[None]

        def shifted(offset):
            return cells[level, :, 7 + offset : 8 + offset + rows, :]

        below, here, above, beyond = shifted(-1), shifted(0), shifted(1), shifted(2)
        edge_here = 7.0 * (below + here) - (shifted(-2) + above)
        edge_face = 7.0 * (here + above) - (below + beyond)
        edge_next = 7.0 * (above + beyond) - (here + shifted(3))
        flux = (
            by_face[None] * edge_face
            + by_edge[None] * jnp.where(upward, edge_here, edge_next)
            + by_cell[None] * jnp.where(upward, here, above)
        )
        change = (flux[:, 1:] - flux[:, :-1]) * cell_v[...][None]
        rest[level] = cells[level, :, 8 : rows + 8, :] - change

    border[...] = jnp.zeros_like(border)
    pack_east.wait_recv()
    pack_west.wait_recv()
    for t in range(count):
        border[t, tail : tail + 3] = packs[1, t, 0:3]
        border[t, LANES - 3 : LANES] = packs[0, t, 0:3]
        here_out[:, t, :, :LANES] = cells[:, t, 8 : rows + 8, :LANES]
        here_out[:, t, :, LANES:] = border[t].T.reshape(levels, rows, LANES)
        here_out[:, t, :, LANES:cols] = cells[:, t, 8 : rows + 8, LANES:]

    for level in range(levels):
        here = here_out[level]
        pair = here + pltpu.roll(here, 1, 2)
        edge = 8.0 * pair - (pltpu.roll(pair, 1, 2) + pltpu.roll(pair, 2 * LANES - 1, 2))
        next_out[level] = pltpu.roll(here, 2 * LANES - 1, 2)
        edge_out[level] = edge
        face_out[level] = pltpu.roll(edge, 2 * LANES - 1, 2)
        beyond_out[level] = pltpu.roll(edge, 2 * LANES - 2, 2)

    def finish(body_rows, west_row):
        turned[:cols] = body_rows
        turned[2 * LANES - 8 :] = jnp.broadcast_to(west_row, (8, LANES))

    turned[LANES:, :] = jnp.zeros((LANES, LANES), jnp.float32)

    @pl.when(jnp.logical_not(polar))
    def _():
        finish(blocks[0, :cols], packs[0, count, 0:1])

    @pl.when(polar)
    def _():
        send_west.wait_recv()
        total[...] += forward(1)
        send_across.wait_recv()
        total[...] += forward(2)
        lane = lax.broadcasted_iota(jnp.int32, (8, 2 * LANES), 1)
        spread = jnp.broadcast_to(limit_v[...].reshape(1, bands * rows), (8, bands * rows))
        spread = pltpu.roll(spread, lax.rem((bands - band) * rows, bands * rows), 1)
        limit = jnp.where(lane < rows, spread, 0)
        copies = 1
        while copies < levels:
            limit = limit + pltpu.roll(limit, copies * rows, 1)
            copies *= 2
        limit = limit[0:1, :LANES]
        wave = lax.broadcasted_iota(jnp.int32, (circle, LANES), 0)
        wave = jnp.where(wave <= circle // 2, wave, wave - circle // 2)
        send_east.wait_recv()
        coeff = jnp.where(wave <= limit, total[...] + forward(3), 0.0)
        high, low = split_halves(coeff)
        both = jnp.dot(
            inv_hi[...], jnp.concatenate([high, low], axis=1), preferred_element_type=jnp.float32
        )
        rest_term = jnp.dot(inv_lo[...], high, preferred_element_type=jnp.float32)
        smooth = both[:, :LANES] + (both[:, LANES:] + rest_term)
        kept = limit < circle // 2
        finish(
            jnp.where(kept, smooth[:cols], blocks[0, :cols]),
            jnp.where(kept, smooth[DEPTH - 1 :], packs[0, count, 0:1]),
        )

    faces[:, :, :LANES] = turned[:LANES].T.reshape(levels, rows, LANES)
    faces[:, :, LANES:] = turned[LANES:].T.reshape(levels, rows, LANES)

    pack_east.wait_send()
    pack_west.wait_send()

    @pl.when(polar)
    def _():
        @pl.when(jnp.logical_not(last_ring))
        def _():
            send_east.wait_send()

        send_west.wait_send()
        send_across.wait_send()

    @pl.when(has_north)
    def _():
        send_north.wait_send()
        send_north_c.wait_send()

    @pl.when(has_south)
    def _():
        send_south.wait_send()


def flux_kernel(
    faces, here, following, edge, face_edge, beyond, rest, updated, filtered, result, smooth, sem
):
    levels, _, _, cols = rest.shape
    smooth[...] = faces[:, :, :cols]
    store = pltpu.make_async_copy(smooth, filtered, sem.at[levels])
    store.start()
    for level in range(levels):
        speed = faces[level]
        by_face, by_edge, by_cell = flux_factors(speed, 1.0)
        eastward = (speed > 0)[None]
        flux = (
            by_face[None] * face_edge[level]
            + by_edge[None] * jnp.where(eastward, edge[level], beyond[level])
            + by_cell[None] * jnp.where(eastward, here[level], following[level])
        )
        change = flux - pltpu.roll(flux, 1, 2)
        result[level] = rest[level] - change[:, :, :cols]
        pltpu.make_async_copy(result.at[level], updated.at[level], sem.at[level]).start()
    for level in range(levels):
        pltpu.make_async_copy(result.at[level], updated.at[level], sem.at[level]).wait()
    store.wait()


def ring_body(bands, tracers, courant, cutoffs):
    levels, count, rows, cols = tracers.shape
    circle = cols * RINGS
    sizes = (levels, count, rows, cols, bands, bands // 4, circle)
    ahead_hi, ahead_lo, back_hi, back_lo = filter_tables(circle, cols)
    face_w, cell_w = weight_tables(bands, rows, cols)
    hbm = pl.BlockSpec(memory_space=pltpu.HBM)
    vmem = pl.BlockSpec(memory_space=pltpu.VMEM)
    f32, half = jnp.float32, jnp.bfloat16
    slab = (levels, count, rows)
    wide = jax.ShapeDtypeStruct(slab + (2 * LANES,), f32)
    parts = pl.pallas_call(
        functools.partial(gather_kernel, sizes),
        out_shape=(jax.ShapeDtypeStruct((levels, rows, 2 * LANES), f32),)
        + (wide,) * 5
        + (jax.ShapeDtypeStruct(tracers.shape, f32),),
        in_specs=[hbm] * 9,
        out_specs=(vmem,) * 7,
        scratch_shapes=[
            pltpu.VMEM((levels, rows, cols), f32),
            pltpu.VMEM((levels, count, rows + 16, cols), f32),
            pltpu.VMEM((levels, rows + 8, cols), f32),
            pltpu.VMEM((RINGS, DEPTH, LANES), f32),
            pltpu.VMEM((circle, LANES), f32),
            pltpu.VMEM((RINGS, circle, DEPTH), half),
            pltpu.VMEM((RINGS, circle, DEPTH), half),
            pltpu.VMEM((DEPTH, circle), half),
            pltpu.VMEM((DEPTH, circle), half),
            pltpu.VMEM((bands * rows,), jnp.int32),
            pltpu.VMEM((rows + 8, cols), f32),
            pltpu.VMEM((rows, cols), f32),
            pltpu.VMEM((2, count + 1, 8, LANES), f32),
            pltpu.VMEM((2, count + 1, 8, LANES), f32),
            pltpu.VMEM((count, LANES, LANES), f32),
            pltpu.VMEM((2 * LANES, LANES), f32),
            pltpu.SemaphoreType.DMA((10,)),
            pltpu.SemaphoreType.DMA((8,)),
            pltpu.SemaphoreType.DMA((8,)),
            pltpu.SemaphoreType.REGULAR((RINGS,)),
        ],
        compiler_params=pltpu.CompilerParams(
            collective_id=0, has_side_effects=True, vmem_limit_bytes=24 * 2**20
        ),
    )(
        *(
            pltpu.with_memory_space_constraint(jnp.asarray(operand), pltpu.HBM)
            for operand in (
                tracers, courant, cutoffs, ahead_hi, ahead_lo, back_hi, back_lo, face_w, cell_w
            )
        )
    )
    return pl.pallas_call(
        flux_kernel,
        out_shape=(
            jax.ShapeDtypeStruct(tracers.shape, f32),
            jax.ShapeDtypeStruct((levels, rows, cols), f32),
        ),
        in_specs=[vmem] * 7,
        out_specs=(hbm, hbm),
        scratch_shapes=[
            pltpu.VMEM(tracers.shape, f32),
            pltpu.VMEM((levels, rows, cols), f32),
            pltpu.SemaphoreType.DMA((levels + 1,)),
        ],
        compiler_params=pltpu.CompilerParams(vmem_limit_bytes=16 * 2**20),
    )(*parts)


def body(bands, tracers, courant, cutoffs):
    levels, _, rows, cols = tracers.shape
    fits = (
        lax.axis_size("lon") == RINGS
        and bands % 4 == 0
        and bands * rows == 2 * LANES
        and levels * rows == LANES
        and LANES < cols <= SENT
        and cols % 4 == 0
    )
    if fits:
        return ring_body(bands, tracers, courant, cutoffs)
    return general_body(tracers, courant, cutoffs)


def solution(mesh):
    in_specs = (P(None, None, "lat", "lon"), P(None, None, "lat", "lon"), P())
    out_specs = (P(None, None, "lat", "lon"), P(None, "lat", "lon"))
    return jax.shard_map(
        functools.partial(body, mesh.shape["lat"]),
        mesh=mesh,
        in_specs=in_specs,
        out_specs=out_specs,
        check_vma=False,
    )
```

```python
import functools
import math

import jax
import numpy as np
import jax.numpy as jnp
from jax import lax
from jax.experimental import pallas as pl
from jax.experimental.pallas import tpu as pltpu
from jax.sharding import PartitionSpec as P


def padded(cells, sides, width, closed):
    for axis, dim in sides:
        count = lax.axis_size(axis)
        ends = count if closed else count - 1
        head = lax.slice_in_dim(cells, 0, width, axis=dim)
        tail = lax.slice_in_dim(cells, cells.shape[dim] - width, cells.shape[dim], axis=dim)
        cells = jnp.concatenate(
            [
                lax.ppermute(tail, axis, [(i, (i + 1) % count) for i in range(ends)]),
                cells,
                lax.ppermute(head, axis, [((i + 1) % count, i) for i in range(ends)]),
            ],
            axis=dim,
        )
    return cells


def take_range(values, start, count, axis_index):
    return lax.slice_in_dim(values, start, start + count, axis=axis_index)


def ppm_flux(extended, courant_faces, axis_index):
    cell_count = extended.shape[axis_index] - 6
    edge_values = 7.0 / 12.0 * (
        take_range(extended, 1, cell_count + 3, axis_index)
        + take_range(extended, 2, cell_count + 3, axis_index)
    ) - 1.0 / 12.0 * (
        take_range(extended, 0, cell_count + 3, axis_index)
        + take_range(extended, 3, cell_count + 3, axis_index)
    )
    left_edge = take_range(edge_values, 0, cell_count + 2, axis_index)
    right_edge = take_range(edge_values, 1, cell_count + 2, axis_index)
    centre = take_range(extended, 2, cell_count + 2, axis_index)
    slopes = right_edge - left_edge
    curvature = 6.0 * centre - 3.0 * (left_edge + right_edge)
    upwind = take_range(right_edge, 0, cell_count + 1, axis_index) - 0.5 * courant_faces * (
        take_range(slopes, 0, cell_count + 1, axis_index)
        - (1.0 - courant_faces * (2.0 / 3.0)) * take_range(curvature, 0, cell_count + 1, axis_index)
    )
    downwind = take_range(left_edge, 1, cell_count + 1, axis_index) - 0.5 * courant_faces * (
        take_range(slopes, 1, cell_count + 1, axis_index)
        + (1.0 + courant_faces * (2.0 / 3.0)) * take_range(curvature, 1, cell_count + 1, axis_index)
    )
    return courant_faces * jnp.where(courant_faces > 0, upwind, downwind)


def metric_weights(first_row, row_count, grid_rows):
    faces = first_row + jnp.arange(-1, row_count, dtype=jnp.int32)
    centres = first_row + jnp.arange(row_count, dtype=jnp.int32)
    face_weight = jnp.sin(
        jnp.minimum(faces + 1, grid_rows - 1 - faces).astype(jnp.float32) * (math.pi / grid_rows)
    )
    cell_weight = jnp.sin(
        (jnp.minimum(centres, grid_rows - 1 - centres).astype(jnp.float32) + 0.5)
        * (math.pi / grid_rows)
    )
    return (face_weight, cell_weight)


def angle_table(first_ids, second_ids, period):
    product = first_ids[:, None] * second_ids[None, :] % period
    angles = product.astype(jnp.float32) * (2.0 * math.pi / period)
    return (jnp.cos(angles), jnp.sin(angles))


def spectral_lowpass(row_block, limits, outer_count):
    row_count, circle = row_block.shape
    inner_count = circle // outer_count
    highest = lax.Precision.HIGHEST
    grid_values = row_block.reshape(row_count, outer_count, inner_count)
    outer_ids = jnp.arange(outer_count, dtype=jnp.int32)
    inner_ids = jnp.arange(inner_count, dtype=jnp.int32)
    outer_cos, outer_sin = angle_table(outer_ids, outer_ids, outer_count)
    inner_cos, inner_sin = angle_table(inner_ids, inner_ids, inner_count)
    twiddle_cos, twiddle_sin = angle_table(inner_ids, outer_ids, circle)
    first_real = jnp.einsum("rab,ak->rbk", grid_values, outer_cos, precision=highest)
    first_imag = -jnp.einsum("rab,ak->rbk", grid_values, outer_sin, precision=highest)
    turned_real = first_real * twiddle_cos + first_imag * twiddle_sin
    turned_imag = first_imag * twiddle_cos - first_real * twiddle_sin
    coeff_real = jnp.einsum("rbk,bj->rjk", turned_real, inner_cos, precision=highest) + jnp.einsum(
        "rbk,bj->rjk", turned_imag, inner_sin, precision=highest
    )
    coeff_imag = jnp.einsum("rbk,bj->rjk", turned_imag, inner_cos, precision=highest) - jnp.einsum(
        "rbk,bj->rjk", turned_real, inner_sin, precision=highest
    )
    wavenumber = inner_ids[:, None] * outer_count + outer_ids[None, :]
    folded = jnp.minimum(wavenumber, circle - wavenumber)
    keep_mask = folded[None, :, :] <= limits[:, None, None]
    coeff_real = jnp.where(keep_mask, coeff_real, 0.0)
    coeff_imag = jnp.where(keep_mask, coeff_imag, 0.0)
    back_real = jnp.einsum("rjk,jb->rbk", coeff_real, inner_cos, precision=highest) - jnp.einsum(
        "rjk,jb->rbk", coeff_imag, inner_sin, precision=highest
    )
    back_imag = jnp.einsum("rjk,jb->rbk", coeff_imag, inner_cos, precision=highest) + jnp.einsum(
        "rjk,jb->rbk", coeff_real, inner_sin, precision=highest
    )
    reverted_real = back_real * twiddle_cos - back_imag * twiddle_sin
    reverted_imag = back_imag * twiddle_cos + back_real * twiddle_sin
    signal = jnp.einsum("rbk,ka->rab", reverted_real, outer_cos, precision=highest) - jnp.einsum(
        "rbk,ka->rab", reverted_imag, outer_sin, precision=highest
    )
    return (signal / circle).reshape(row_count, circle)


def general_body(tracers, courant, cutoffs):
    levels, tracer_count, lat_rows, lon_cols = tracers.shape
    lon_groups = lax.axis_size("lon")
    lon_index = lax.axis_index("lon")
    lat_bands = lax.axis_size("lat")
    band_index = lax.axis_index("lat")
    grid_rows = lat_rows * lat_bands
    zonal = courant[0]
    meridional = courant[1]
    lat_stack = jnp.concatenate([tracers, meridional[:, None]], axis=1)
    lat_ext = padded(lat_stack, (("lat", 2),), 3, False)
    flat_count = levels * lat_rows
    flat_zonal = zonal.reshape(flat_count, lon_cols)
    edges = jnp.concatenate([tracers[..., :3], tracers[..., lon_cols - 3 :]], axis=-1)
    west_index = (lon_index + lon_groups - 1) % lon_groups
    east_index = (lon_index + 1) % lon_groups
    local_limits = lax.dynamic_slice_in_dim(cutoffs, band_index * lat_rows, lat_rows)
    limits = jnp.tile(local_limits, levels)
    circle = lon_cols * lon_groups
    gathered = lax.all_gather(flat_zonal, "lon", axis=0)
    gathered_edges = lax.all_gather(edges, "lon", axis=0)
    west = lax.dynamic_index_in_dim(gathered_edges, west_index, 0, keepdims=False)[..., 3:]
    east = lax.dynamic_index_in_dim(gathered_edges, east_index, 0, keepdims=False)[..., :3]
    west_raw = lax.dynamic_index_in_dim(gathered, west_index, 0, keepdims=False)[:, -1:]
    raw_ext = jnp.concatenate([west_raw, flat_zonal], axis=1)
    whole_rows = jnp.transpose(gathered, (1, 0, 2)).reshape(flat_count, circle)
    lowpass = spectral_lowpass(whole_rows, limits, lon_groups)
    lowpass = jnp.concatenate([lowpass[:, -1:], lowpass], axis=1)
    lowpass_ext = lax.dynamic_slice_in_dim(lowpass, lon_index * lon_cols, lon_cols + 1, axis=1)
    lon_ext = jnp.concatenate([west, tracers, east], axis=-1)
    filtered_flat = jnp.where((limits < circle // 2)[:, None], lowpass_ext, raw_ext)
    zonal_faces = filtered_flat.reshape(levels, 1, lat_rows, lon_cols + 1)
    filtered_zonal = zonal_faces[:, 0, :, 1:]
    flux_east = ppm_flux(lon_ext, zonal_faces, 3)
    face_weight, cell_weight = metric_weights(band_index * lat_rows, lat_rows, grid_rows)
    flux_north = (
    ppm_flux(lat_ext[:, :tracer_count], lat_ext[:, tracer_count:, 2 : lat_rows + 3, :], 2)
    * face_weight[None, None, :, None]
    )
    change = (
    flux_east[:, :, :, 1:]
    - flux_east[:, :, :, :-1]
    + (flux_north[:, :, 1:, :] - flux_north[:, :, :-1, :]) / cell_weight[None, None, :, None]
    )
    return (tracers - change, filtered_zonal)


MESH = pl.DeviceIdType.MESH
RINGS = 4
LANES = 128
DEPTH = 192
TAIL = 64
TAIL_SENT = 56
EAST, WEST, ACROSS, EAST_TAIL, WEST_TAIL, ACROSS_TAIL, PACK_EAST, PACK_WEST, NORTH, SOUTH = range(10)


def split_halves(values):
    high = values.astype(jnp.bfloat16)
    low = (values - high.astype(jnp.float32)).astype(jnp.bfloat16)
    return high, low


def filter_tables(circle, cols):
    half = circle // 2
    cells = np.arange(circle, dtype=np.int64)
    cos_ids = np.arange(half + 1, dtype=np.int64)
    sin_ids = np.arange(1, half, dtype=np.int64)

    def waves(ids):
        return np.concatenate(
            [
                np.cos(2.0 * np.pi * ((cos_ids[:, None] * ids[None, :]) % circle) / circle),
                np.sin(2.0 * np.pi * ((sin_ids[:, None] * ids[None, :]) % circle) / circle),
            ],
            axis=0,
        )

    def halves(table):
        high = table.astype(jnp.bfloat16)
        low = (table - high.astype(np.float64)).astype(jnp.bfloat16)
        return high, low

    forward = np.zeros((circle // cols, circle, DEPTH))
    forward[:, :, :cols] = waves(cells).reshape(circle, circle // cols, cols).transpose(1, 0, 2)
    wavenumber = np.concatenate([cos_ids, sin_ids])
    scale = np.where((wavenumber == 0) | (wavenumber == half), 1.0, 2.0) / circle
    inverse = np.zeros((DEPTH, circle))
    inverse[:cols] = waves(np.arange(cols)).T * scale
    inverse[DEPTH - 1] = waves(np.array([-1]))[:, 0] * scale
    return halves(forward) + halves(inverse)


def weight_tables(bands, rows, cols):
    grid_rows = bands * rows
    faces = np.arange(bands)[:, None] * rows + np.arange(-8, rows)[None, :]
    cells = np.arange(bands)[:, None] * rows + np.arange(rows)[None, :]
    face = np.sin(np.minimum(faces + 1, grid_rows - 1 - faces) * (np.pi / grid_rows))
    cell = 1.0 / np.sin((np.minimum(cells, grid_rows - 1 - cells) + 0.5) * (np.pi / grid_rows))
    face = np.broadcast_to(face[:, :, None], face.shape + (cols,))
    cell = np.broadcast_to(cell[:, :, None], cell.shape + (cols,))
    return face.astype(np.float32), cell.astype(np.float32)


def flux_factors(courant, scale):
    size = jnp.abs(courant)
    steep = size - size * size
    middle = 3.0 * size - 2.0 * size * size
    scaled = courant * scale
    return (
        scaled * (1.0 + steep - middle) * (1.0 / 12.0),
        scaled * steep * (-1.0 / 12.0),
        scaled * middle,
    )


def gather_kernel(
    sizes,
    tracers, courant, cutoffs, ahead_hi, ahead_lo, back_hi, back_lo, face_w, cell_w,
    faces, here_out, next_out, edge_out, face_out, beyond_out, rest,
    zonal, cells, merid, heads, tails, own, total, table_hi, table_lo, inv_hi, inv_lo, limit_v, face_v, cell_v,
    pack, packs, sides, near, border, turned,
    load_sem, send_sem, recv_sem, ready, beside_in, beside_ok,
):
    levels, count, rows, cols, bands, polar_bands, circle = sizes
    flat = levels * rows
    z = lax.axis_index("lon")
    band = lax.axis_index("lat")
    polar = (band < polar_bands) | (band >= bands - polar_bands)
    has_south = band > 0
    has_north = band < bands - 1
    tail = cols - LANES
    barrier = pltpu.get_barrier_semaphore()

    def load(index, source, target):
        return pltpu.make_async_copy(source, target, load_sem.at[index])

    load_zonal = load(0, courant.at[0], zonal)
    load_cells = load(1, tracers, cells.at[:, :, pl.ds(8, rows), :])
    load_merid = load(2, courant.at[1], merid.at[:, pl.ds(8, rows), :])
    load_limit = load(3, cutoffs, limit_v)
    load_face = load(4, face_w.at[band], face_v)
    load_cell = load(5, cell_w.at[band], cell_v)
    load_tables = [
        load(6, ahead_hi, table_hi),
        load(7, ahead_lo, table_lo),
        load(8, back_hi, inv_hi),
        load(9, back_lo, inv_lo),
    ]
    load_zonal.start()
    for other in range(1, RINGS):
        @pl.when(z < other)
        def _():
            pl.semaphore_signal(barrier, inc=1, device_id={"lon": other}, device_id_type=MESH)

    near_ring = z < 2

    @pl.when(near_ring & has_south)
    def _():
        pl.semaphore_signal(barrier, inc=1, device_id={"lat": band - 1}, device_id_type=MESH)

    @pl.when(near_ring & has_north)
    def _():
        pl.semaphore_signal(barrier, inc=1, device_id={"lat": band + 1}, device_id_type=MESH)

    beside = has_south.astype(jnp.int32) + has_north.astype(jnp.int32)
    pl.semaphore_wait(barrier, z + jnp.where(near_ring, beside, 0))
    load_cells.start()
    load_merid.start()
    def remote(index, source, target, where):
        return pltpu.make_async_remote_copy(
            src_ref=source,
            dst_ref=target,
            send_sem=send_sem.at[index],
            recv_sem=recv_sem.at[index],
            device_id=where,
            device_id_type=MESH,
        )

    east = lax.rem(z + 1, RINGS)
    west = lax.rem(z + 3, RINGS)
    across = lax.rem(z + 2, RINGS)
    head = courant.at[0, :, :, pl.ds(0, LANES)]
    tail_rows = pl.ds(0, TAIL_SENT)
    own_tail = tails.at[0, tail_rows]

    class Pair:
        def __init__(self, first, second, sources, slot, where):
            self.head = remote(first, sources[0], heads.at[slot], {"lon": where})
            self.tail = remote(second, sources[1], tails.at[slot, tail_rows], {"lon": where})

        def start(self):
            self.head.start()
            self.tail.start()

        def wait_recv(self):
            self.head.wait_recv()
            self.tail.wait_recv()

        def wait_send(self):
            self.head.wait_send()
            self.tail.wait_send()

    mine = (head, own_tail)
    send_east = Pair(EAST, EAST_TAIL, mine, 3, east)
    send_west = Pair(WEST, WEST_TAIL, mine, 1, west)
    send_across = Pair(ACROSS, ACROSS_TAIL, mine, 2, across)
    pass_west = Pair(ACROSS, ACROSS_TAIL, (heads.at[1], tails.at[1, tail_rows]), 2, west)
    pass_east = Pair(ACROSS, ACROSS_TAIL, (heads.at[3], tails.at[3, tail_rows]), 2, east)
    pack_east = remote(PACK_EAST, pack.at[0], packs.at[0], {"lon": east})
    pack_west = remote(PACK_WEST, pack.at[1], packs.at[1], {"lon": west})
    send_north = remote(NORTH, sides.at[0], near.at[0], {"lat": band + 1})
    send_south = remote(SOUTH, sides.at[1], near.at[1], {"lat": band - 1})
    patient = (lax.rem(band, 2) == 1) & (z == 3)
    firsts = ((send_west, polar & ((z == 1) | (z == 2))), (send_east, polar & (z == 3)))
    early = [(copy, chosen & jnp.logical_not(patient)) for copy, chosen in firsts]
    late = [(copy, chosen & patient) for copy, chosen in firsts]

    for copy, chosen in early:
        @pl.when(chosen)
        def _():
            copy.head.start()

    for other in range(RINGS - 1):
        @pl.when(z > other)
        def _():
            pl.semaphore_signal(ready.at[z], inc=1, device_id={"lon": other}, device_id_type=MESH)

    tails[0, TAIL_SENT - 8 :] = jnp.zeros((TAIL - TAIL_SENT + 8, LANES), jnp.float32)
    load_zonal.wait()
    tails[0, :tail] = zonal[:, :, LANES:].reshape(flat, tail).T
    for copy, chosen in early:
        @pl.when(chosen)
        def _():
            copy.tail.start()

    for copy, chosen in late:
        @pl.when(chosen)
        def _():
            copy.start()

    own[:LANES] = zonal[:, :, :LANES].reshape(flat, LANES).T
    own[LANES:] = tails[0]
    load_face.start()
    load_cell.start()

    @pl.when(polar)
    def _():
        load_limit.start()
        for copy in load_tables:
            copy.start()

    load_cells.wait()
    for t in range(count):
        first = cells[:, t, 8 : rows + 8, :LANES].reshape(flat, LANES).T
        last = cells[:, t, 8 : rows + 8, LANES:].reshape(flat, tail).T
        pack[0, t, 0:3] = last[tail - 3 : tail]
        pack[1, t, 0:3] = first[0:3]
    pack[0, count, 0:1] = own[cols - 1 : cols]

    @pl.when(east < z)
    def _():
        pack_east.start()

    @pl.when(west < z)
    def _():
        pack_west.start()

    load_merid.wait()
    planes = [(level, t) for level in range(levels) for t in range(count)]
    for k, (level, t) in enumerate(planes):
        sides[0, 3 * k : 3 * k + 3, :cols] = cells[level, t, rows + 5 : rows + 8]
        sides[1, 3 * k : 3 * k + 3, :cols] = cells[level, t, 8:11]
    first_speed = 3 * len(planes)
    for level in range(levels):
        sides[0, first_speed + level, :cols] = merid[level, rows + 7]

    def send_sides(chosen):
        @pl.when(chosen & has_north)
        def _():
            send_north.start()

        @pl.when(chosen & has_south)
        def _():
            send_south.start()

    send_sides(near_ring)
    for slot in range(1, RINGS):
        tails[slot, TAIL_SENT:] = jnp.zeros((TAIL - TAIL_SENT, LANES), jnp.float32)
    border[...] = jnp.zeros_like(border)
    turned[LANES:, :] = jnp.zeros((LANES, LANES), jnp.float32)

    def signal_beside(semaphore):
        @pl.when(has_south)
        def _():
            pl.semaphore_signal(semaphore, inc=1, device_id={"lat": band - 1}, device_id_type=MESH)

        @pl.when(has_north)
        def _():
            pl.semaphore_signal(semaphore, inc=1, device_id={"lat": band + 1}, device_id_type=MESH)

    def greet(other):
        @pl.when(z < other)
        def _():
            pl.semaphore_wait(ready.at[other], 1)
            for copy, chosen in (
                (send_east, east == other),
                (send_west, west == other),
                (send_across, (across == other) & (z == 0)),
            ):
                @pl.when(polar & chosen)
                def _():
                    copy.start()
            for copy, where in ((pack_east, east), (pack_west, west)):
                @pl.when(where == other)
                def _():
                    copy.start()

        if other >= 2:
            @pl.when(z == 1)
            def _():
                signal_beside(beside_in.at[other])

    def block(slot):
        return jnp.concatenate([heads[slot].reshape(flat, LANES).T, tails[slot]], axis=0)

    def forward(slot, values):
        high, low = split_halves(values)
        both = jnp.dot(
            table_hi[slot], jnp.concatenate([high, low], axis=1), preferred_element_type=jnp.float32
        )
        rest_term = jnp.dot(table_lo[slot], high, preferred_element_type=jnp.float32)
        return both[:, :LANES] + (both[:, LANES:] + rest_term)

    greet(1)

    @pl.when(polar & (z == 3))
    def _():
        send_east.wait_send()
        send_across.start()
        send_west.start()

    greet(2)

    @pl.when(polar)
    def _():
        for copy in load_tables:
            copy.wait()
        load_limit.wait()
        total[...] = forward(0, own[...])

    greet(3)

    @pl.when(z == 1)
    def _():
        for other in (2, 3):
            pl.semaphore_wait(beside_in.at[other], beside)
            pl.semaphore_signal(beside_ok, inc=1, device_id={"lon": other}, device_id_type=MESH)

    @pl.when(z >= 2)
    def _():
        pl.semaphore_wait(beside_ok, 1)

    send_sides(z >= 2)

    @pl.when(polar & (z == 1))
    def _():
        send_west.head.wait_recv()
        pass_west.head.start()
        send_west.tail.wait_recv()
        pass_west.tail.start()

    @pl.when(polar & (z == 2))
    def _():
        send_east.head.wait_recv()
        pass_east.head.start()
        send_east.tail.wait_recv()
        pass_east.tail.start()

    load_face.wait()
    load_cell.wait()

    @pl.when(has_south)
    def _():
        send_north.wait_recv()
        for k, (level, t) in enumerate(planes):
            cells[level, t, 5:8] = near[0, 3 * k : 3 * k + 3, :cols]
        for level in range(levels):
            merid[level, 7] = near[0, first_speed + level, :cols]

    @pl.when(has_north)
    def _():
        send_south.wait_recv()
        for k, (level, t) in enumerate(planes):
            cells[level, t, rows + 8 : rows + 11] = near[1, 3 * k : 3 * k + 3, :cols]

    @pl.when(jnp.logical_not(has_south))
    def _():
        cells[:, :, 0:8, :] = jnp.zeros((levels, count, 8, cols), jnp.float32)
        merid[:, 0:8, :] = jnp.zeros((levels, 8, cols), jnp.float32)

    @pl.when(jnp.logical_not(has_north))
    def _():
        cells[:, :, rows + 8 :, :] = jnp.zeros((levels, count, 8, cols), jnp.float32)

    for level in range(levels):
        speed = merid[level, 7 : rows + 8]
        by_face, by_edge, by_cell = flux_factors(speed, face_v[7 : rows + 8])
        upward = speed > 0
        inverse_cell = cell_v[...]
        for t in range(count):
            def shifted(offset):
                return cells[level, t, 7 + offset : 8 + offset + rows, :]

            below, here, above, beyond = shifted(-1), shifted(0), shifted(1), shifted(2)
            edge_here = 7.0 * (below + here) - (shifted(-2) + above)
            edge_face = 7.0 * (here + above) - (below + beyond)
            edge_next = 7.0 * (above + beyond) - (here + shifted(3))
            flux = (
                by_face * edge_face
                + by_edge * jnp.where(upward, edge_here, edge_next)
                + by_cell * jnp.where(upward, here, above)
            )
            change = (flux[1:] - flux[:-1]) * inverse_cell
            rest[level, t] = cells[level, t, 8 : rows + 8, :] - change

    @pl.when(polar)
    def _():
        @pl.when(z == 0)
        def _():
            send_west.wait_recv()

        @pl.when((z == 1) | (z == 3))
        def _():
            send_east.wait_recv()

        slot = jnp.where(z == 0, 1, 3)
        total[...] += forward(slot, block(slot))

    pack_east.wait_recv()
    pack_west.wait_recv()
    for t in range(count):
        border[t, tail : tail + 3] = packs[1, t, 0:3]
        border[t, LANES - 3 : LANES] = packs[0, t, 0:3]
        here_out[:, t, :, :LANES] = cells[:, t, 8 : rows + 8, :LANES]
        here_out[:, t, :, LANES:] = border[t].T.reshape(levels, rows, LANES)
        here_out[:, t, :, LANES:cols] = cells[:, t, 8 : rows + 8, LANES:]

    for level in range(levels):
        here = here_out[level]

        def moved(offset):
            return pltpu.roll(here, (-offset) % (2 * LANES), 2)

        back_two, back_one, ahead_one, ahead_two = moved(-2), moved(-1), moved(1), moved(2)
        next_out[level] = ahead_one
        edge_out[level] = 7.0 * (back_one + here) - (back_two + ahead_one)
        face_out[level] = 7.0 * (here + ahead_one) - (back_one + ahead_two)
        beyond_out[level] = 7.0 * (ahead_one + ahead_two) - (here + moved(3))

    def finish(body_rows, west_row):
        turned[:cols] = body_rows
        turned[2 * LANES - 8 :] = jnp.broadcast_to(west_row, (8, LANES))

    @pl.when(jnp.logical_not(polar))
    def _():
        finish(own[:cols], packs[0, count, 0:1])

    @pl.when(polar)
    def _():
        lane = lax.broadcasted_iota(jnp.int32, (8, 2 * LANES), 1)
        spread = jnp.broadcast_to(limit_v[...].reshape(1, bands * rows), (8, bands * rows))
        spread = pltpu.roll(spread, lax.rem((bands - band) * rows, bands * rows), 1)
        limit = jnp.where(lane < rows, spread, 0)
        copies = 1
        while copies < levels:
            limit = limit + pltpu.roll(limit, copies * rows, 1)
            copies *= 2
        limit = limit[0:1, :LANES]
        wave = lax.broadcasted_iota(jnp.int32, (circle, LANES), 0)
        wave = jnp.where(wave <= circle // 2, wave, wave - circle // 2)

        @pl.when(z == 0)
        def _():
            send_east.wait_recv()

        @pl.when(z >= 2)
        def _():
            send_west.wait_recv()

        slot = jnp.where(z == 0, 3, 1)
        total[...] += forward(slot, block(slot))
        send_across.wait_recv()
        coeff = jnp.where(wave <= limit, total[...] + forward(2, block(2)), 0.0)
        high, low = split_halves(coeff)
        both = jnp.dot(
            inv_hi[...], jnp.concatenate([high, low], axis=1), preferred_element_type=jnp.float32
        )
        rest_term = jnp.dot(inv_lo[...], high, preferred_element_type=jnp.float32)
        smooth = both[:, :LANES] + (both[:, LANES:] + rest_term)
        kept = limit < circle // 2
        finish(
            jnp.where(kept, smooth[:cols], own[:cols]),
            jnp.where(kept, smooth[DEPTH - 1 :], packs[0, count, 0:1]),
        )

    faces[:, :, :LANES] = turned[:LANES].T.reshape(levels, rows, LANES)
    faces[:, :, LANES:] = turned[LANES:].T.reshape(levels, rows, LANES)

    pack_east.wait_send()
    pack_west.wait_send()

    @pl.when(polar)
    def _():
        @pl.when(z != 3)
        def _():
            send_east.wait_send()

        send_west.wait_send()
        send_across.wait_send()

    @pl.when(has_north)
    def _():
        send_north.wait_send()

    @pl.when(has_south)
    def _():
        send_south.wait_send()


def flux_kernel(
    faces, here, following, edge, face_edge, beyond, rest, updated, filtered, result, smooth, sem
):
    levels, _, _, cols = rest.shape
    smooth[...] = faces[:, :, :cols]
    store = pltpu.make_async_copy(smooth, filtered, sem.at[levels])
    store.start()
    for level in range(levels):
        speed = faces[level]
        by_face, by_edge, by_cell = flux_factors(speed, 1.0)
        eastward = speed > 0
        flux = (
            by_face[None] * face_edge[level]
            + by_edge[None] * jnp.where(eastward[None], edge[level], beyond[level])
            + by_cell[None] * jnp.where(eastward[None], here[level], following[level])
        )
        change = flux - pltpu.roll(flux, 1, 2)
        result[level] = rest[level] - change[:, :, :cols]
        pltpu.make_async_copy(result.at[level], updated.at[level], sem.at[level]).start()
    for level in range(levels):
        pltpu.make_async_copy(result.at[level], updated.at[level], sem.at[level]).wait()
    store.wait()


def ring_body(bands, tracers, courant, cutoffs):
    levels, count, rows, cols = tracers.shape
    circle = cols * RINGS
    sizes = (levels, count, rows, cols, bands, bands // 4, circle)
    ahead_hi, ahead_lo, back_hi, back_lo = filter_tables(circle, cols)
    face_w, cell_w = weight_tables(bands, rows, cols)
    hbm = pl.BlockSpec(memory_space=pltpu.HBM)
    vmem = pl.BlockSpec(memory_space=pltpu.VMEM)
    f32, half = jnp.float32, jnp.bfloat16
    slab = (levels, count, rows)
    strip = -(-(3 * levels * count + levels) // 8) * 8
    wide = jax.ShapeDtypeStruct(slab + (2 * LANES,), f32)
    parts = pl.pallas_call(
        functools.partial(gather_kernel, sizes),
        out_shape=(jax.ShapeDtypeStruct((levels, rows, 2 * LANES), f32),)
        + (wide,) * 5
        + (jax.ShapeDtypeStruct(tracers.shape, f32),),
        in_specs=[hbm] * 9,
        out_specs=(vmem,) * 7,
        scratch_shapes=[
            pltpu.VMEM((levels, rows, cols), f32),
            pltpu.VMEM((levels, count, rows + 16, cols), f32),
            pltpu.VMEM((levels, rows + 8, cols), f32),
            pltpu.VMEM((RINGS, levels, rows, LANES), f32),
            pltpu.VMEM((RINGS, TAIL, LANES), f32),
            pltpu.VMEM((DEPTH, LANES), f32),
            pltpu.VMEM((circle, LANES), f32),
            pltpu.VMEM((RINGS, circle, DEPTH), half),
            pltpu.VMEM((RINGS, circle, DEPTH), half),
            pltpu.VMEM((DEPTH, circle), half),
            pltpu.VMEM((DEPTH, circle), half),
            pltpu.VMEM((bands * rows,), jnp.int32),
            pltpu.VMEM((rows + 8, cols), f32),
            pltpu.VMEM((rows, cols), f32),
            pltpu.VMEM((2, count + 1, 8, LANES), f32),
            pltpu.VMEM((2, count + 1, 8, LANES), f32),
            pltpu.VMEM((2, strip, 2 * LANES), f32),
            pltpu.VMEM((2, strip, 2 * LANES), f32),
            pltpu.VMEM((count, LANES, LANES), f32),
            pltpu.VMEM((2 * LANES, LANES), f32),
            pltpu.SemaphoreType.DMA((10,)),
            pltpu.SemaphoreType.DMA((10,)),
            pltpu.SemaphoreType.DMA((10,)),
            pltpu.SemaphoreType.REGULAR((RINGS,)),
            pltpu.SemaphoreType.REGULAR((RINGS,)),
            pltpu.SemaphoreType.REGULAR,
        ],
        compiler_params=pltpu.CompilerParams(
            collective_id=0, has_side_effects=True, vmem_limit_bytes=24 * 2**20
        ),
    )(
        *(
            pltpu.with_memory_space_constraint(jnp.asarray(operand), pltpu.HBM)
            for operand in (
                tracers, courant, cutoffs, ahead_hi, ahead_lo, back_hi, back_lo, face_w, cell_w
            )
        )
    )
    return pl.pallas_call(
        flux_kernel,
        out_shape=(
            jax.ShapeDtypeStruct(tracers.shape, f32),
            jax.ShapeDtypeStruct((levels, rows, cols), f32),
        ),
        in_specs=[vmem] * 7,
        out_specs=(hbm, hbm),
        scratch_shapes=[
            pltpu.VMEM(tracers.shape, f32),
            pltpu.VMEM((levels, rows, cols), f32),
            pltpu.SemaphoreType.DMA((levels + 1,)),
        ],
        compiler_params=pltpu.CompilerParams(vmem_limit_bytes=16 * 2**20),
    )(*parts)


def body(bands, tracers, courant, cutoffs):
    levels, _, rows, cols = tracers.shape
    fits = (
        lax.axis_size("lon") == RINGS
        and bands % 4 == 0
        and bands * rows == 2 * LANES
        and levels * rows == LANES
        and LANES < cols <= LANES + TAIL_SENT - 4
        and cols % 4 == 0
    )
    if fits:
        return ring_body(bands, tracers, courant, cutoffs)
    return general_body(tracers, courant, cutoffs)


def solution(mesh):
    in_specs = (P(None, None, "lat", "lon"), P(None, None, "lat", "lon"), P())
    out_specs = (P(None, None, "lat", "lon"), P(None, "lat", "lon"))
    return jax.shard_map(
        functools.partial(body, mesh.shape["lat"]),
        mesh=mesh,
        in_specs=in_specs,
        out_specs=out_specs,
        check_vma=False,
    )
```

```python
import functools
import math

import jax
import numpy as np
import jax.numpy as jnp
from jax import lax
from jax.experimental import pallas as pl
from jax.experimental.pallas import tpu as pltpu
from jax.sharding import PartitionSpec as P


def padded(cells, sides, width, closed):
    for axis, dim in sides:
        count = lax.axis_size(axis)
        ends = count if closed else count - 1
        head = lax.slice_in_dim(cells, 0, width, axis=dim)
        tail = lax.slice_in_dim(cells, cells.shape[dim] - width, cells.shape[dim], axis=dim)
        cells = jnp.concatenate(
            [
                lax.ppermute(tail, axis, [(i, (i + 1) % count) for i in range(ends)]),
                cells,
                lax.ppermute(head, axis, [((i + 1) % count, i) for i in range(ends)]),
            ],
            axis=dim,
        )
    return cells


def take_range(values, start, count, axis_index):
    return lax.slice_in_dim(values, start, start + count, axis=axis_index)


def ppm_flux(extended, courant_faces, axis_index):
    cell_count = extended.shape[axis_index] - 6
    edge_values = 7.0 / 12.0 * (
        take_range(extended, 1, cell_count + 3, axis_index)
        + take_range(extended, 2, cell_count + 3, axis_index)
    ) - 1.0 / 12.0 * (
        take_range(extended, 0, cell_count + 3, axis_index)
        + take_range(extended, 3, cell_count + 3, axis_index)
    )
    left_edge = take_range(edge_values, 0, cell_count + 2, axis_index)
    right_edge = take_range(edge_values, 1, cell_count + 2, axis_index)
    centre = take_range(extended, 2, cell_count + 2, axis_index)
    slopes = right_edge - left_edge
    curvature = 6.0 * centre - 3.0 * (left_edge + right_edge)
    upwind = take_range(right_edge, 0, cell_count + 1, axis_index) - 0.5 * courant_faces * (
        take_range(slopes, 0, cell_count + 1, axis_index)
        - (1.0 - courant_faces * (2.0 / 3.0)) * take_range(curvature, 0, cell_count + 1, axis_index)
    )
    downwind = take_range(left_edge, 1, cell_count + 1, axis_index) - 0.5 * courant_faces * (
        take_range(slopes, 1, cell_count + 1, axis_index)
        + (1.0 + courant_faces * (2.0 / 3.0)) * take_range(curvature, 1, cell_count + 1, axis_index)
    )
    return courant_faces * jnp.where(courant_faces > 0, upwind, downwind)


def metric_weights(first_row, row_count, grid_rows):
    faces = first_row + jnp.arange(-1, row_count, dtype=jnp.int32)
    centres = first_row + jnp.arange(row_count, dtype=jnp.int32)
    face_weight = jnp.sin(
        jnp.minimum(faces + 1, grid_rows - 1 - faces).astype(jnp.float32) * (math.pi / grid_rows)
    )
    cell_weight = jnp.sin(
        (jnp.minimum(centres, grid_rows - 1 - centres).astype(jnp.float32) + 0.5)
        * (math.pi / grid_rows)
    )
    return (face_weight, cell_weight)


def angle_table(first_ids, second_ids, period):
    product = first_ids[:, None] * second_ids[None, :] % period
    angles = product.astype(jnp.float32) * (2.0 * math.pi / period)
    return (jnp.cos(angles), jnp.sin(angles))


def spectral_lowpass(row_block, limits, outer_count):
    row_count, circle = row_block.shape
    inner_count = circle // outer_count
    highest = lax.Precision.HIGHEST
    grid_values = row_block.reshape(row_count, outer_count, inner_count)
    outer_ids = jnp.arange(outer_count, dtype=jnp.int32)
    inner_ids = jnp.arange(inner_count, dtype=jnp.int32)
    outer_cos, outer_sin = angle_table(outer_ids, outer_ids, outer_count)
    inner_cos, inner_sin = angle_table(inner_ids, inner_ids, inner_count)
    twiddle_cos, twiddle_sin = angle_table(inner_ids, outer_ids, circle)
    first_real = jnp.einsum("rab,ak->rbk", grid_values, outer_cos, precision=highest)
    first_imag = -jnp.einsum("rab,ak->rbk", grid_values, outer_sin, precision=highest)
    turned_real = first_real * twiddle_cos + first_imag * twiddle_sin
    turned_imag = first_imag * twiddle_cos - first_real * twiddle_sin
    coeff_real = jnp.einsum("rbk,bj->rjk", turned_real, inner_cos, precision=highest) + jnp.einsum(
        "rbk,bj->rjk", turned_imag, inner_sin, precision=highest
    )
    coeff_imag = jnp.einsum("rbk,bj->rjk", turned_imag, inner_cos, precision=highest) - jnp.einsum(
        "rbk,bj->rjk", turned_real, inner_sin, precision=highest
    )
    wavenumber = inner_ids[:, None] * outer_count + outer_ids[None, :]
    folded = jnp.minimum(wavenumber, circle - wavenumber)
    keep_mask = folded[None, :, :] <= limits[:, None, None]
    coeff_real = jnp.where(keep_mask, coeff_real, 0.0)
    coeff_imag = jnp.where(keep_mask, coeff_imag, 0.0)
    back_real = jnp.einsum("rjk,jb->rbk", coeff_real, inner_cos, precision=highest) - jnp.einsum(
        "rjk,jb->rbk", coeff_imag, inner_sin, precision=highest
    )
    back_imag = jnp.einsum("rjk,jb->rbk", coeff_imag, inner_cos, precision=highest) + jnp.einsum(
        "rjk,jb->rbk", coeff_real, inner_sin, precision=highest
    )
    reverted_real = back_real * twiddle_cos - back_imag * twiddle_sin
    reverted_imag = back_imag * twiddle_cos + back_real * twiddle_sin
    signal = jnp.einsum("rbk,ka->rab", reverted_real, outer_cos, precision=highest) - jnp.einsum(
        "rbk,ka->rab", reverted_imag, outer_sin, precision=highest
    )
    return (signal / circle).reshape(row_count, circle)


def general_body(tracers, courant, cutoffs):
    levels, tracer_count, lat_rows, lon_cols = tracers.shape
    lon_groups = lax.axis_size("lon")
    lon_index = lax.axis_index("lon")
    lat_bands = lax.axis_size("lat")
    band_index = lax.axis_index("lat")
    grid_rows = lat_rows * lat_bands
    zonal = courant[0]
    meridional = courant[1]
    lat_stack = jnp.concatenate([tracers, meridional[:, None]], axis=1)
    lat_ext = padded(lat_stack, (("lat", 2),), 3, False)
    flat_count = levels * lat_rows
    flat_zonal = zonal.reshape(flat_count, lon_cols)
    edges = jnp.concatenate([tracers[..., :3], tracers[..., lon_cols - 3 :]], axis=-1)
    west_index = (lon_index + lon_groups - 1) % lon_groups
    east_index = (lon_index + 1) % lon_groups
    local_limits = lax.dynamic_slice_in_dim(cutoffs, band_index * lat_rows, lat_rows)
    limits = jnp.tile(local_limits, levels)
    circle = lon_cols * lon_groups
    gathered = lax.all_gather(flat_zonal, "lon", axis=0)
    gathered_edges = lax.all_gather(edges, "lon", axis=0)
    west = lax.dynamic_index_in_dim(gathered_edges, west_index, 0, keepdims=False)[..., 3:]
    east = lax.dynamic_index_in_dim(gathered_edges, east_index, 0, keepdims=False)[..., :3]
    west_raw = lax.dynamic_index_in_dim(gathered, west_index, 0, keepdims=False)[:, -1:]
    raw_ext = jnp.concatenate([west_raw, flat_zonal], axis=1)
    whole_rows = jnp.transpose(gathered, (1, 0, 2)).reshape(flat_count, circle)
    lowpass = spectral_lowpass(whole_rows, limits, lon_groups)
    lowpass = jnp.concatenate([lowpass[:, -1:], lowpass], axis=1)
    lowpass_ext = lax.dynamic_slice_in_dim(lowpass, lon_index * lon_cols, lon_cols + 1, axis=1)
    lon_ext = jnp.concatenate([west, tracers, east], axis=-1)
    filtered_flat = jnp.where((limits < circle // 2)[:, None], lowpass_ext, raw_ext)
    zonal_faces = filtered_flat.reshape(levels, 1, lat_rows, lon_cols + 1)
    filtered_zonal = zonal_faces[:, 0, :, 1:]
    flux_east = ppm_flux(lon_ext, zonal_faces, 3)
    face_weight, cell_weight = metric_weights(band_index * lat_rows, lat_rows, grid_rows)
    flux_north = (
    ppm_flux(lat_ext[:, :tracer_count], lat_ext[:, tracer_count:, 2 : lat_rows + 3, :], 2)
    * face_weight[None, None, :, None]
    )
    change = (
    flux_east[:, :, :, 1:]
    - flux_east[:, :, :, :-1]
    + (flux_north[:, :, 1:, :] - flux_north[:, :, :-1, :]) / cell_weight[None, None, :, None]
    )
    return (tracers - change, filtered_zonal)


MESH = pl.DeviceIdType.MESH
RINGS = 4
LANES = 128
DEPTH = 192
TAIL = 64
TAIL_SENT = 56
EAST, WEST, ACROSS, EAST_TAIL, WEST_TAIL, ACROSS_TAIL, PACK_EAST, PACK_WEST, NORTH, SOUTH, PASS, PASS_TAIL = range(12)


def split_halves(values):
    high = values.astype(jnp.bfloat16)
    low = (values - high.astype(jnp.float32)).astype(jnp.bfloat16)
    return high, low


def filter_tables(circle, cols):
    half = circle // 2
    cells = np.arange(circle, dtype=np.int64)
    cos_ids = np.arange(half + 1, dtype=np.int64)
    sin_ids = np.arange(1, half, dtype=np.int64)

    def waves(ids):
        return np.concatenate(
            [
                np.cos(2.0 * np.pi * ((cos_ids[:, None] * ids[None, :]) % circle) / circle),
                np.sin(2.0 * np.pi * ((sin_ids[:, None] * ids[None, :]) % circle) / circle),
            ],
            axis=0,
        )

    def halves(table):
        high = table.astype(jnp.bfloat16)
        low = (table - high.astype(np.float64)).astype(jnp.bfloat16)
        return high, low

    forward = np.zeros((circle // cols, circle, DEPTH))
    forward[:, :, :cols] = waves(cells).reshape(circle, circle // cols, cols).transpose(1, 0, 2)
    wavenumber = np.concatenate([cos_ids, sin_ids])
    scale = np.where((wavenumber == 0) | (wavenumber == half), 1.0, 2.0) / circle
    inverse = np.zeros((DEPTH, circle))
    inverse[:cols] = waves(np.arange(cols)).T * scale
    inverse[DEPTH - 1] = waves(np.array([-1]))[:, 0] * scale
    return halves(forward) + halves(inverse)


def weight_tables(bands, rows, cols):
    grid_rows = bands * rows
    faces = np.arange(bands)[:, None] * rows + np.arange(-8, rows)[None, :]
    cells = np.arange(bands)[:, None] * rows + np.arange(rows)[None, :]
    face = np.sin(np.minimum(faces + 1, grid_rows - 1 - faces) * (np.pi / grid_rows))
    cell = 1.0 / np.sin((np.minimum(cells, grid_rows - 1 - cells) + 0.5) * (np.pi / grid_rows))
    face = np.broadcast_to(face[:, :, None], face.shape + (cols,))
    cell = np.broadcast_to(cell[:, :, None], cell.shape + (cols,))
    return face.astype(np.float32), cell.astype(np.float32)


def flux_factors(courant, scale):
    size = jnp.abs(courant)
    steep = size - size * size
    middle = 3.0 * size - 2.0 * size * size
    scaled = courant * scale
    return (
        scaled * (1.0 + steep - middle) * (1.0 / 12.0),
        scaled * steep * (-1.0 / 12.0),
        scaled * middle,
    )


def gather_kernel(
    sizes,
    tracers, courant, cutoffs, ahead_hi, ahead_lo, back_hi, back_lo, face_w, cell_w,
    faces, here_out, next_out, edge_out, face_out, beyond_out, rest,
    zonal, cells, merid, heads, tails, own, total, table_hi, table_lo, inv_hi, inv_lo, limit_v, face_v, cell_v,
    pack, packs, sides, near, border, turned,
    load_sem, send_sem, recv_sem, ready, beside_in, beside_ok,
):
    levels, count, rows, cols, bands, polar_bands, circle = sizes
    flat = levels * rows
    z = lax.axis_index("lon")
    band = lax.axis_index("lat")
    polar = (band < polar_bands) | (band >= bands - polar_bands)
    has_south = band > 0
    has_north = band < bands - 1
    tail = cols - LANES
    barrier = pltpu.get_barrier_semaphore()

    def load(index, source, target):
        return pltpu.make_async_copy(source, target, load_sem.at[index])

    load_zonal = load(0, courant.at[0], zonal)
    load_cells = load(1, tracers, cells.at[:, :, pl.ds(8, rows), :])
    load_merid = load(2, courant.at[1], merid.at[:, pl.ds(8, rows), :])
    load_limit = load(3, cutoffs, limit_v)
    load_face = load(4, face_w.at[band], face_v)
    load_cell = load(5, cell_w.at[band], cell_v)
    load_tables = [
        load(6, ahead_hi, table_hi),
        load(7, ahead_lo, table_lo),
        load(8, back_hi, inv_hi),
        load(9, back_lo, inv_lo),
    ]
    load_zonal.start()
    for other in range(1, RINGS):
        @pl.when(z < other)
        def _():
            pl.semaphore_signal(barrier, inc=1, device_id={"lon": other}, device_id_type=MESH)

    near_ring = z < 2

    @pl.when(near_ring & has_south)
    def _():
        pl.semaphore_signal(barrier, inc=1, device_id={"lat": band - 1}, device_id_type=MESH)

    @pl.when(near_ring & has_north)
    def _():
        pl.semaphore_signal(barrier, inc=1, device_id={"lat": band + 1}, device_id_type=MESH)

    beside = has_south.astype(jnp.int32) + has_north.astype(jnp.int32)
    pl.semaphore_wait(barrier, z + jnp.where(near_ring, beside, 0))
    load_cells.start()
    load_merid.start()
    def remote(index, source, target, where, send_index=None):
        return pltpu.make_async_remote_copy(
            src_ref=source,
            dst_ref=target,
            send_sem=send_sem.at[index if send_index is None else send_index],
            recv_sem=recv_sem.at[index],
            device_id=where,
            device_id_type=MESH,
        )

    east = lax.rem(z + 1, RINGS)
    west = lax.rem(z + 3, RINGS)
    across = lax.rem(z + 2, RINGS)
    head = courant.at[0, :, :, pl.ds(0, LANES)]
    tail_rows = pl.ds(0, TAIL_SENT)
    own_tail = tails.at[0, tail_rows]

    class Pair:
        def __init__(self, first, second, sources, slot, where, sends=(None, None)):
            self.head = remote(first, sources[0], heads.at[slot], {"lon": where}, sends[0])
            self.tail = remote(second, sources[1], tails.at[slot, tail_rows], {"lon": where}, sends[1])

        def start(self):
            self.head.start()
            self.tail.start()

        def wait_recv(self):
            self.head.wait_recv()
            self.tail.wait_recv()

        def wait_send(self):
            self.head.wait_send()
            self.tail.wait_send()

    mine = (head, own_tail)
    send_east = Pair(EAST, EAST_TAIL, mine, 3, east)
    send_west = Pair(WEST, WEST_TAIL, mine, 1, west)
    send_across = Pair(ACROSS, ACROSS_TAIL, mine, 2, across)
    pass_west = Pair(ACROSS, ACROSS_TAIL, (heads.at[1], tails.at[1, tail_rows]), 2, west)
    pass_east = Pair(
        ACROSS, ACROSS_TAIL, (heads.at[3], tails.at[3, tail_rows]), 2, east, (PASS, PASS_TAIL)
    )
    pack_east = remote(PACK_EAST, pack.at[0], packs.at[0], {"lon": east})
    pack_west = remote(PACK_WEST, pack.at[1], packs.at[1], {"lon": west})
    send_north = remote(NORTH, sides.at[0], near.at[0], {"lat": band + 1})
    send_south = remote(SOUTH, sides.at[1], near.at[1], {"lat": band - 1})
    patient = (lax.rem(band, 2) == 1) & (z == 3)
    early = (
        (send_west, polar & ((z == 1) | (z == 2) | patient)),
        (send_east, polar & (z == 3) & jnp.logical_not(patient)),
    )
    late = ((send_east, polar & patient),)

    for copy, chosen in early:
        @pl.when(chosen)
        def _():
            copy.head.start()

    for other in range(RINGS - 1):
        @pl.when(z > other)
        def _():
            pl.semaphore_signal(ready.at[z], inc=1, device_id={"lon": other}, device_id_type=MESH)

    tails[0, TAIL_SENT - 8 :] = jnp.zeros((TAIL - TAIL_SENT + 8, LANES), jnp.float32)
    load_zonal.wait()
    tails[0, :tail] = zonal[:, :, LANES:].reshape(flat, tail).T
    for copy, chosen in early:
        @pl.when(chosen)
        def _():
            copy.tail.start()

    for copy, chosen in late:
        @pl.when(chosen)
        def _():
            copy.start()

    own[:LANES] = zonal[:, :, :LANES].reshape(flat, LANES).T
    own[LANES:] = tails[0]
    load_face.start()
    load_cell.start()

    @pl.when(polar)
    def _():
        load_limit.start()
        for copy in load_tables:
            copy.start()

    load_cells.wait()
    for t in range(count):
        first = cells[:, t, 8 : rows + 8, :LANES].reshape(flat, LANES).T
        last = cells[:, t, 8 : rows + 8, LANES:].reshape(flat, tail).T
        pack[0, t, 0:3] = last[tail - 3 : tail]
        pack[1, t, 0:3] = first[0:3]
    pack[0, count, 0:1] = own[cols - 1 : cols]

    @pl.when(east < z)
    def _():
        pack_east.start()

    @pl.when(west < z)
    def _():
        pack_west.start()

    load_merid.wait()
    planes = [(level, t) for level in range(levels) for t in range(count)]
    for k, (level, t) in enumerate(planes):
        sides[0, 3 * k : 3 * k + 3, :cols] = cells[level, t, rows + 5 : rows + 8]
        sides[1, 3 * k : 3 * k + 3, :cols] = cells[level, t, 8:11]
    first_speed = 3 * len(planes)
    for level in range(levels):
        sides[0, first_speed + level, :cols] = merid[level, rows + 7]

    def send_sides(chosen):
        @pl.when(chosen & has_north)
        def _():
            send_north.start()

        @pl.when(chosen & has_south)
        def _():
            send_south.start()

    send_sides(near_ring)
    for slot in range(1, RINGS):
        tails[slot, TAIL_SENT:] = jnp.zeros((TAIL - TAIL_SENT, LANES), jnp.float32)
    border[...] = jnp.zeros_like(border)
    turned[LANES:, :] = jnp.zeros((LANES, LANES), jnp.float32)

    def signal_beside(semaphore):
        @pl.when(has_south)
        def _():
            pl.semaphore_signal(semaphore, inc=1, device_id={"lat": band - 1}, device_id_type=MESH)

        @pl.when(has_north)
        def _():
            pl.semaphore_signal(semaphore, inc=1, device_id={"lat": band + 1}, device_id_type=MESH)

    def greet(other):
        @pl.when(z < other)
        def _():
            pl.semaphore_wait(ready.at[other], 1)
            for copy, where in ((pack_east, east), (pack_west, west)):
                @pl.when(where == other)
                def _():
                    copy.start()
            for copy, where in ((send_east, east), (send_west, west)):
                @pl.when(polar & (where == other))
                def _():
                    copy.start()

        if other >= 2:
            @pl.when(z == 1)
            def _():
                signal_beside(beside_in.at[other])

    def block(slot):
        return jnp.concatenate([heads[slot].reshape(flat, LANES).T, tails[slot]], axis=0)

    def forward(slot, values):
        high, low = split_halves(values)
        both = jnp.dot(
            table_hi[slot], jnp.concatenate([high, low], axis=1), preferred_element_type=jnp.float32
        )
        rest_term = jnp.dot(table_lo[slot], high, preferred_element_type=jnp.float32)
        return both[:, :LANES] + (both[:, LANES:] + rest_term)

    greet(1)

    @pl.when(polar & (z == 3))
    def _():
        send_east.wait_send()
        send_across.start()

        @pl.when(jnp.logical_not(patient))
        def _():
            send_west.start()

    greet(2)

    greet(3)

    @pl.when(z == 1)
    def _():
        for other in (2, 3):
            pl.semaphore_wait(beside_in.at[other], beside)
            pl.semaphore_signal(beside_ok, inc=1, device_id={"lon": other}, device_id_type=MESH)

    @pl.when(polar)
    def _():
        for copy in load_tables:
            copy.wait()
        load_limit.wait()
        total[...] = forward(0, own[...])

    @pl.when(z >= 2)
    def _():
        pl.semaphore_wait(beside_ok, 1)

    send_sides(z >= 2)

    @pl.when(polar & (z == 1))
    def _():
        send_west.head.wait_recv()
        pass_west.head.start()
        send_west.tail.wait_recv()
        pass_west.tail.start()

    @pl.when(polar & (z == 1))
    def _():
        send_east.head.wait_recv()
        pass_east.head.start()
        send_east.tail.wait_recv()
        pass_east.tail.start()

    load_face.wait()
    load_cell.wait()

    @pl.when(has_south)
    def _():
        send_north.wait_recv()
        for k, (level, t) in enumerate(planes):
            cells[level, t, 5:8] = near[0, 3 * k : 3 * k + 3, :cols]
        for level in range(levels):
            merid[level, 7] = near[0, first_speed + level, :cols]

    @pl.when(has_north)
    def _():
        send_south.wait_recv()
        for k, (level, t) in enumerate(planes):
            cells[level, t, rows + 8 : rows + 11] = near[1, 3 * k : 3 * k + 3, :cols]

    @pl.when(jnp.logical_not(has_south))
    def _():
        cells[:, :, 0:8, :] = jnp.zeros((levels, count, 8, cols), jnp.float32)
        merid[:, 0:8, :] = jnp.zeros((levels, 8, cols), jnp.float32)

    @pl.when(jnp.logical_not(has_north))
    def _():
        cells[:, :, rows + 8 :, :] = jnp.zeros((levels, count, 8, cols), jnp.float32)

    for level in range(levels):
        speed = merid[level, 7 : rows + 8]
        by_face, by_edge, by_cell = flux_factors(speed, face_v[7 : rows + 8])
        upward = speed > 0
        inverse_cell = cell_v[...]
        for t in range(count):
            def shifted(offset):
                return cells[level, t, 7 + offset : 8 + offset + rows, :]

            below, here, above, beyond = shifted(-1), shifted(0), shifted(1), shifted(2)
            edge_here = 7.0 * (below + here) - (shifted(-2) + above)
            edge_face = 7.0 * (here + above) - (below + beyond)
            edge_next = 7.0 * (above + beyond) - (here + shifted(3))
            flux = (
                by_face * edge_face
                + by_edge * jnp.where(upward, edge_here, edge_next)
                + by_cell * jnp.where(upward, here, above)
            )
            change = (flux[1:] - flux[:-1]) * inverse_cell
            rest[level, t] = cells[level, t, 8 : rows + 8, :] - change

    @pl.when(polar & (z == 2))
    def _():
        send_east.head.wait_recv()
        pass_east.head.start()
        send_east.tail.wait_recv()
        pass_east.tail.start()

    @pl.when(polar)
    def _():
        @pl.when(z == 0)
        def _():
            send_west.wait_recv()

        @pl.when(z == 3)
        def _():
            send_east.wait_recv()

        slot = jnp.where(z == 0, 1, 3)
        total[...] += forward(slot, block(slot))

    pack_east.wait_recv()
    pack_west.wait_recv()
    for t in range(count):
        border[t, tail : tail + 3] = packs[1, t, 0:3]
        border[t, LANES - 3 : LANES] = packs[0, t, 0:3]
        here_out[:, t, :, :LANES] = cells[:, t, 8 : rows + 8, :LANES]
        here_out[:, t, :, LANES:] = border[t].T.reshape(levels, rows, LANES)
        here_out[:, t, :, LANES:cols] = cells[:, t, 8 : rows + 8, LANES:]

    for level in range(levels):
        here = here_out[level]

        def moved(offset):
            return pltpu.roll(here, (-offset) % (2 * LANES), 2)

        back_two, back_one, ahead_one, ahead_two = moved(-2), moved(-1), moved(1), moved(2)
        next_out[level] = ahead_one
        edge_out[level] = 7.0 * (back_one + here) - (back_two + ahead_one)
        face_out[level] = 7.0 * (here + ahead_one) - (back_one + ahead_two)
        beyond_out[level] = 7.0 * (ahead_one + ahead_two) - (here + moved(3))

    def finish(body_rows, west_row):
        turned[:cols] = body_rows
        turned[2 * LANES - 8 :] = jnp.broadcast_to(west_row, (8, LANES))

    @pl.when(jnp.logical_not(polar))
    def _():
        finish(own[:cols], packs[0, count, 0:1])

    @pl.when(polar)
    def _():
        lane = lax.broadcasted_iota(jnp.int32, (8, 2 * LANES), 1)
        spread = jnp.broadcast_to(limit_v[...].reshape(1, bands * rows), (8, bands * rows))
        spread = pltpu.roll(spread, lax.rem((bands - band) * rows, bands * rows), 1)
        limit = jnp.where(lane < rows, spread, 0)
        copies = 1
        while copies < levels:
            limit = limit + pltpu.roll(limit, copies * rows, 1)
            copies *= 2
        limit = limit[0:1, :LANES]
        wave = lax.broadcasted_iota(jnp.int32, (circle, LANES), 0)
        wave = jnp.where(wave <= circle // 2, wave, wave - circle // 2)

        @pl.when(z == 0)
        def _():
            send_east.wait_recv()

        @pl.when(z >= 2)
        def _():
            send_west.wait_recv()

        slot = jnp.where(z == 0, 3, 1)
        total[...] += forward(slot, block(slot))
        send_across.wait_recv()
        coeff = jnp.where(wave <= limit, total[...] + forward(2, block(2)), 0.0)
        high, low = split_halves(coeff)
        both = jnp.dot(
            inv_hi[...], jnp.concatenate([high, low], axis=1), preferred_element_type=jnp.float32
        )
        rest_term = jnp.dot(inv_lo[...], high, preferred_element_type=jnp.float32)
        smooth = both[:, :LANES] + (both[:, LANES:] + rest_term)
        kept = limit < circle // 2
        finish(
            jnp.where(kept, smooth[:cols], own[:cols]),
            jnp.where(kept, smooth[DEPTH - 1 :], packs[0, count, 0:1]),
        )

    faces[:, :, :LANES] = turned[:LANES].T.reshape(levels, rows, LANES)
    faces[:, :, LANES:] = turned[LANES:].T.reshape(levels, rows, LANES)

    pack_east.wait_send()
    pack_west.wait_send()

    @pl.when(polar)
    def _():
        @pl.when(z != 3)
        def _():
            send_east.wait_send()

        send_west.wait_send()

        @pl.when(z == 3)
        def _():
            send_across.wait_send()

        @pl.when(z == 1)
        def _():
            pass_west.wait_send()

        @pl.when((z == 1) | (z == 2))
        def _():
            pass_east.wait_send()

    @pl.when(has_north)
    def _():
        send_north.wait_send()

    @pl.when(has_south)
    def _():
        send_south.wait_send()


def flux_kernel(
    faces, here, following, edge, face_edge, beyond, rest, updated, filtered, result, smooth, sem
):
    levels, _, _, cols = rest.shape
    smooth[...] = faces[:, :, :cols]
    store = pltpu.make_async_copy(smooth, filtered, sem.at[levels])
    store.start()
    for level in range(levels):
        speed = faces[level]
        by_face, by_edge, by_cell = flux_factors(speed, 1.0)
        eastward = speed > 0
        flux = (
            by_face[None] * face_edge[level]
            + by_edge[None] * jnp.where(eastward[None], edge[level], beyond[level])
            + by_cell[None] * jnp.where(eastward[None], here[level], following[level])
        )
        change = flux - pltpu.roll(flux, 1, 2)
        result[level] = rest[level] - change[:, :, :cols]
        pltpu.make_async_copy(result.at[level], updated.at[level], sem.at[level]).start()
    for level in range(levels):
        pltpu.make_async_copy(result.at[level], updated.at[level], sem.at[level]).wait()
    store.wait()


def ring_body(bands, tracers, courant, cutoffs):
    levels, count, rows, cols = tracers.shape
    circle = cols * RINGS
    sizes = (levels, count, rows, cols, bands, bands // 4, circle)
    ahead_hi, ahead_lo, back_hi, back_lo = filter_tables(circle, cols)
    face_w, cell_w = weight_tables(bands, rows, cols)
    hbm = pl.BlockSpec(memory_space=pltpu.HBM)
    vmem = pl.BlockSpec(memory_space=pltpu.VMEM)
    f32, half = jnp.float32, jnp.bfloat16
    slab = (levels, count, rows)
    strip = -(-(3 * levels * count + levels) // 8) * 8
    wide = jax.ShapeDtypeStruct(slab + (2 * LANES,), f32)
    parts = pl.pallas_call(
        functools.partial(gather_kernel, sizes),
        out_shape=(jax.ShapeDtypeStruct((levels, rows, 2 * LANES), f32),)
        + (wide,) * 5
        + (jax.ShapeDtypeStruct(tracers.shape, f32),),
        in_specs=[hbm] * 9,
        out_specs=(vmem,) * 7,
        scratch_shapes=[
            pltpu.VMEM((levels, rows, cols), f32),
            pltpu.VMEM((levels, count, rows + 16, cols), f32),
            pltpu.VMEM((levels, rows + 8, cols), f32),
            pltpu.VMEM((RINGS, levels, rows, LANES), f32),
            pltpu.VMEM((RINGS, TAIL, LANES), f32),
            pltpu.VMEM((DEPTH, LANES), f32),
            pltpu.VMEM((circle, LANES), f32),
            pltpu.VMEM((RINGS, circle, DEPTH), half),
            pltpu.VMEM((RINGS, circle, DEPTH), half),
            pltpu.VMEM((DEPTH, circle), half),
            pltpu.VMEM((DEPTH, circle), half),
            pltpu.VMEM((bands * rows,), jnp.int32),
            pltpu.VMEM((rows + 8, cols), f32),
            pltpu.VMEM((rows, cols), f32),
            pltpu.VMEM((2, count + 1, 8, LANES), f32),
            pltpu.VMEM((2, count + 1, 8, LANES), f32),
            pltpu.VMEM((2, strip, 2 * LANES), f32),
            pltpu.VMEM((2, strip, 2 * LANES), f32),
            pltpu.VMEM((count, LANES, LANES), f32),
            pltpu.VMEM((2 * LANES, LANES), f32),
            pltpu.SemaphoreType.DMA((10,)),
            pltpu.SemaphoreType.DMA((12,)),
            pltpu.SemaphoreType.DMA((10,)),
            pltpu.SemaphoreType.REGULAR((RINGS,)),
            pltpu.SemaphoreType.REGULAR((RINGS,)),
            pltpu.SemaphoreType.REGULAR,
        ],
        compiler_params=pltpu.CompilerParams(
            collective_id=0, has_side_effects=True, vmem_limit_bytes=24 * 2**20
        ),
    )(
        *(
            pltpu.with_memory_space_constraint(jnp.asarray(operand), pltpu.HBM)
            for operand in (
                tracers, courant, cutoffs, ahead_hi, ahead_lo, back_hi, back_lo, face_w, cell_w
            )
        )
    )
    return pl.pallas_call(
        flux_kernel,
        out_shape=(
            jax.ShapeDtypeStruct(tracers.shape, f32),
            jax.ShapeDtypeStruct((levels, rows, cols), f32),
        ),
        in_specs=[vmem] * 7,
        out_specs=(hbm, hbm),
        scratch_shapes=[
            pltpu.VMEM(tracers.shape, f32),
            pltpu.VMEM((levels, rows, cols), f32),
            pltpu.SemaphoreType.DMA((levels + 1,)),
        ],
        compiler_params=pltpu.CompilerParams(vmem_limit_bytes=16 * 2**20),
    )(*parts)


def body(bands, tracers, courant, cutoffs):
    levels, _, rows, cols = tracers.shape
    fits = (
        lax.axis_size("lon") == RINGS
        and bands % 4 == 0
        and bands * rows == 2 * LANES
        and levels * rows == LANES
        and LANES < cols <= LANES + TAIL_SENT - 4
        and cols % 4 == 0
    )
    if fits:
        return ring_body(bands, tracers, courant, cutoffs)
    return general_body(tracers, courant, cutoffs)


def solution(mesh):
    in_specs = (P(None, None, "lat", "lon"), P(None, None, "lat", "lon"), P())
    out_specs = (P(None, None, "lat", "lon"), P(None, "lat", "lon"))
    return jax.shard_map(
        functools.partial(body, mesh.shape["lat"]),
        mesh=mesh,
        in_specs=in_specs,
        out_specs=out_specs,
        check_vma=False,
    )
```

```python
import functools
import math

import jax
import numpy as np
import jax.numpy as jnp
from jax import lax
from jax.experimental import pallas as pl
from jax.experimental.pallas import tpu as pltpu
from jax.sharding import PartitionSpec as P


def padded(cells, sides, width, closed):
    for axis, dim in sides:
        count = lax.axis_size(axis)
        ends = count if closed else count - 1
        head = lax.slice_in_dim(cells, 0, width, axis=dim)
        tail = lax.slice_in_dim(cells, cells.shape[dim] - width, cells.shape[dim], axis=dim)
        cells = jnp.concatenate(
            [
                lax.ppermute(tail, axis, [(i, (i + 1) % count) for i in range(ends)]),
                cells,
                lax.ppermute(head, axis, [((i + 1) % count, i) for i in range(ends)]),
            ],
            axis=dim,
        )
    return cells


def take_range(values, start, count, axis_index):
    return lax.slice_in_dim(values, start, start + count, axis=axis_index)


def ppm_flux(extended, courant_faces, axis_index):
    cell_count = extended.shape[axis_index] - 6
    edge_values = 7.0 / 12.0 * (
        take_range(extended, 1, cell_count + 3, axis_index)
        + take_range(extended, 2, cell_count + 3, axis_index)
    ) - 1.0 / 12.0 * (
        take_range(extended, 0, cell_count + 3, axis_index)
        + take_range(extended, 3, cell_count + 3, axis_index)
    )
    left_edge = take_range(edge_values, 0, cell_count + 2, axis_index)
    right_edge = take_range(edge_values, 1, cell_count + 2, axis_index)
    centre = take_range(extended, 2, cell_count + 2, axis_index)
    slopes = right_edge - left_edge
    curvature = 6.0 * centre - 3.0 * (left_edge + right_edge)
    upwind = take_range(right_edge, 0, cell_count + 1, axis_index) - 0.5 * courant_faces * (
        take_range(slopes, 0, cell_count + 1, axis_index)
        - (1.0 - courant_faces * (2.0 / 3.0)) * take_range(curvature, 0, cell_count + 1, axis_index)
    )
    downwind = take_range(left_edge, 1, cell_count + 1, axis_index) - 0.5 * courant_faces * (
        take_range(slopes, 1, cell_count + 1, axis_index)
        + (1.0 + courant_faces * (2.0 / 3.0)) * take_range(curvature, 1, cell_count + 1, axis_index)
    )
    return courant_faces * jnp.where(courant_faces > 0, upwind, downwind)


def metric_weights(first_row, row_count, grid_rows):
    faces = first_row + jnp.arange(-1, row_count, dtype=jnp.int32)
    centres = first_row + jnp.arange(row_count, dtype=jnp.int32)
    face_weight = jnp.sin(
        jnp.minimum(faces + 1, grid_rows - 1 - faces).astype(jnp.float32) * (math.pi / grid_rows)
    )
    cell_weight = jnp.sin(
        (jnp.minimum(centres, grid_rows - 1 - centres).astype(jnp.float32) + 0.5)
        * (math.pi / grid_rows)
    )
    return (face_weight, cell_weight)


def angle_table(first_ids, second_ids, period):
    product = first_ids[:, None] * second_ids[None, :] % period
    angles = product.astype(jnp.float32) * (2.0 * math.pi / period)
    return (jnp.cos(angles), jnp.sin(angles))


def spectral_lowpass(row_block, limits, outer_count):
    row_count, circle = row_block.shape
    inner_count = circle // outer_count
    highest = lax.Precision.HIGHEST
    grid_values = row_block.reshape(row_count, outer_count, inner_count)
    outer_ids = jnp.arange(outer_count, dtype=jnp.int32)
    inner_ids = jnp.arange(inner_count, dtype=jnp.int32)
    outer_cos, outer_sin = angle_table(outer_ids, outer_ids, outer_count)
    inner_cos, inner_sin = angle_table(inner_ids, inner_ids, inner_count)
    twiddle_cos, twiddle_sin = angle_table(inner_ids, outer_ids, circle)
    first_real = jnp.einsum("rab,ak->rbk", grid_values, outer_cos, precision=highest)
    first_imag = -jnp.einsum("rab,ak->rbk", grid_values, outer_sin, precision=highest)
    turned_real = first_real * twiddle_cos + first_imag * twiddle_sin
    turned_imag = first_imag * twiddle_cos - first_real * twiddle_sin
    coeff_real = jnp.einsum("rbk,bj->rjk", turned_real, inner_cos, precision=highest) + jnp.einsum(
        "rbk,bj->rjk", turned_imag, inner_sin, precision=highest
    )
    coeff_imag = jnp.einsum("rbk,bj->rjk", turned_imag, inner_cos, precision=highest) - jnp.einsum(
        "rbk,bj->rjk", turned_real, inner_sin, precision=highest
    )
    wavenumber = inner_ids[:, None] * outer_count + outer_ids[None, :]
    folded = jnp.minimum(wavenumber, circle - wavenumber)
    keep_mask = folded[None, :, :] <= limits[:, None, None]
    coeff_real = jnp.where(keep_mask, coeff_real, 0.0)
    coeff_imag = jnp.where(keep_mask, coeff_imag, 0.0)
    back_real = jnp.einsum("rjk,jb->rbk", coeff_real, inner_cos, precision=highest) - jnp.einsum(
        "rjk,jb->rbk", coeff_imag, inner_sin, precision=highest
    )
    back_imag = jnp.einsum("rjk,jb->rbk", coeff_imag, inner_cos, precision=highest) + jnp.einsum(
        "rjk,jb->rbk", coeff_real, inner_sin, precision=highest
    )
    reverted_real = back_real * twiddle_cos - back_imag * twiddle_sin
    reverted_imag = back_imag * twiddle_cos + back_real * twiddle_sin
    signal = jnp.einsum("rbk,ka->rab", reverted_real, outer_cos, precision=highest) - jnp.einsum(
        "rbk,ka->rab", reverted_imag, outer_sin, precision=highest
    )
    return (signal / circle).reshape(row_count, circle)


def general_body(tracers, courant, cutoffs):
    levels, tracer_count, lat_rows, lon_cols = tracers.shape
    lon_groups = lax.axis_size("lon")
    lon_index = lax.axis_index("lon")
    lat_bands = lax.axis_size("lat")
    band_index = lax.axis_index("lat")
    grid_rows = lat_rows * lat_bands
    zonal = courant[0]
    meridional = courant[1]
    lat_stack = jnp.concatenate([tracers, meridional[:, None]], axis=1)
    lat_ext = padded(lat_stack, (("lat", 2),), 3, False)
    flat_count = levels * lat_rows
    flat_zonal = zonal.reshape(flat_count, lon_cols)
    edges = jnp.concatenate([tracers[..., :3], tracers[..., lon_cols - 3 :]], axis=-1)
    west_index = (lon_index + lon_groups - 1) % lon_groups
    east_index = (lon_index + 1) % lon_groups
    local_limits = lax.dynamic_slice_in_dim(cutoffs, band_index * lat_rows, lat_rows)
    limits = jnp.tile(local_limits, levels)
    circle = lon_cols * lon_groups
    gathered = lax.all_gather(flat_zonal, "lon", axis=0)
    gathered_edges = lax.all_gather(edges, "lon", axis=0)
    west = lax.dynamic_index_in_dim(gathered_edges, west_index, 0, keepdims=False)[..., 3:]
    east = lax.dynamic_index_in_dim(gathered_edges, east_index, 0, keepdims=False)[..., :3]
    west_raw = lax.dynamic_index_in_dim(gathered, west_index, 0, keepdims=False)[:, -1:]
    raw_ext = jnp.concatenate([west_raw, flat_zonal], axis=1)
    whole_rows = jnp.transpose(gathered, (1, 0, 2)).reshape(flat_count, circle)
    lowpass = spectral_lowpass(whole_rows, limits, lon_groups)
    lowpass = jnp.concatenate([lowpass[:, -1:], lowpass], axis=1)
    lowpass_ext = lax.dynamic_slice_in_dim(lowpass, lon_index * lon_cols, lon_cols + 1, axis=1)
    lon_ext = jnp.concatenate([west, tracers, east], axis=-1)
    filtered_flat = jnp.where((limits < circle // 2)[:, None], lowpass_ext, raw_ext)
    zonal_faces = filtered_flat.reshape(levels, 1, lat_rows, lon_cols + 1)
    filtered_zonal = zonal_faces[:, 0, :, 1:]
    flux_east = ppm_flux(lon_ext, zonal_faces, 3)
    face_weight, cell_weight = metric_weights(band_index * lat_rows, lat_rows, grid_rows)
    flux_north = (
    ppm_flux(lat_ext[:, :tracer_count], lat_ext[:, tracer_count:, 2 : lat_rows + 3, :], 2)
    * face_weight[None, None, :, None]
    )
    change = (
    flux_east[:, :, :, 1:]
    - flux_east[:, :, :, :-1]
    + (flux_north[:, :, 1:, :] - flux_north[:, :, :-1, :]) / cell_weight[None, None, :, None]
    )
    return (tracers - change, filtered_zonal)


MESH = pl.DeviceIdType.MESH
RINGS = 4
LANES = 128
DEPTH = 192
TAIL = 64
TAIL_SENT = 56
EAST, WEST, ACROSS, EAST_TAIL, WEST_TAIL, ACROSS_TAIL, PACK_EAST, PACK_WEST, NORTH, SOUTH, PASS, PASS_TAIL = range(12)


def split_halves(values):
    high = values.astype(jnp.bfloat16)
    low = (values - high.astype(jnp.float32)).astype(jnp.bfloat16)
    return high, low


def filter_tables(circle, cols):
    half = circle // 2
    cells = np.arange(circle, dtype=np.int64)
    cos_ids = np.arange(half + 1, dtype=np.int64)
    sin_ids = np.arange(1, half, dtype=np.int64)

    def waves(ids):
        return np.concatenate(
            [
                np.cos(2.0 * np.pi * ((cos_ids[:, None] * ids[None, :]) % circle) / circle),
                np.sin(2.0 * np.pi * ((sin_ids[:, None] * ids[None, :]) % circle) / circle),
            ],
            axis=0,
        )

    def halves(table):
        high = table.astype(jnp.bfloat16)
        low = (table - high.astype(np.float64)).astype(jnp.bfloat16)
        return high, low

    forward = np.zeros((circle // cols, circle, DEPTH))
    forward[:, :, :cols] = waves(cells).reshape(circle, circle // cols, cols).transpose(1, 0, 2)
    wavenumber = np.concatenate([cos_ids, sin_ids])
    scale = np.where((wavenumber == 0) | (wavenumber == half), 1.0, 2.0) / circle
    inverse = np.zeros((DEPTH, circle))
    inverse[:cols] = waves(np.arange(cols)).T * scale
    inverse[DEPTH - 1] = waves(np.array([-1]))[:, 0] * scale
    return halves(forward) + halves(inverse)


def weight_tables(bands, rows, cols):
    grid_rows = bands * rows
    faces = np.arange(bands)[:, None] * rows + np.arange(-8, rows)[None, :]
    cells = np.arange(bands)[:, None] * rows + np.arange(rows)[None, :]
    face = np.sin(np.minimum(faces + 1, grid_rows - 1 - faces) * (np.pi / grid_rows))
    cell = 1.0 / np.sin((np.minimum(cells, grid_rows - 1 - cells) + 0.5) * (np.pi / grid_rows))
    face = np.broadcast_to(face[:, :, None], face.shape + (cols,))
    cell = np.broadcast_to(cell[:, :, None], cell.shape + (cols,))
    return face.astype(np.float32), cell.astype(np.float32)


def flux_factors(courant, scale):
    size = jnp.abs(courant)
    steep = size - size * size
    middle = 3.0 * size - 2.0 * size * size
    scaled = courant * scale
    return (
        scaled * (1.0 + steep - middle) * (1.0 / 12.0),
        scaled * steep * (-1.0 / 12.0),
        scaled * middle,
    )


def gather_kernel(
    sizes,
    tracers, courant, cutoffs, ahead_hi, ahead_lo, back_hi, back_lo, face_w, cell_w,
    faces, here_out, next_out, edge_out, face_out, beyond_out, rest,
    zonal, cells, merid, heads, tails, own, total, table_hi, table_lo, inv_hi, inv_lo, limit_v, face_v, cell_v,
    pack, packs, sides, near, border, turned,
    load_sem, send_sem, recv_sem, ready, beside_in, beside_ok,
):
    levels, count, rows, cols, bands, polar_bands, circle = sizes
    flat = levels * rows
    z = lax.axis_index("lon")
    band = lax.axis_index("lat")
    polar = (band < polar_bands) | (band >= bands - polar_bands)
    has_south = band > 0
    has_north = band < bands - 1
    tail = cols - LANES
    barrier = pltpu.get_barrier_semaphore()

    def load(index, source, target):
        return pltpu.make_async_copy(source, target, load_sem.at[index])

    load_zonal = load(0, courant.at[0], zonal)
    load_cells = load(1, tracers, cells.at[:, :, pl.ds(8, rows), :])
    load_merid = load(2, courant.at[1], merid.at[:, pl.ds(8, rows), :])
    load_limit = load(3, cutoffs, limit_v)
    load_face = load(4, face_w.at[band], face_v)
    load_cell = load(5, cell_w.at[band], cell_v)
    load_tables = [
        load(6, ahead_hi, table_hi),
        load(7, ahead_lo, table_lo),
        load(8, back_hi, inv_hi),
        load(9, back_lo, inv_lo),
    ]
    load_zonal.start()
    for other in range(1, RINGS):
        @pl.when(z < other)
        def _():
            pl.semaphore_signal(barrier, inc=1, device_id={"lon": other}, device_id_type=MESH)

    near_ring = z == 0

    @pl.when(near_ring & has_south)
    def _():
        pl.semaphore_signal(barrier, inc=1, device_id={"lat": band - 1}, device_id_type=MESH)

    @pl.when(near_ring & has_north)
    def _():
        pl.semaphore_signal(barrier, inc=1, device_id={"lat": band + 1}, device_id_type=MESH)

    beside = has_south.astype(jnp.int32) + has_north.astype(jnp.int32)
    pl.semaphore_wait(barrier, z + jnp.where(near_ring, beside, 0))
    load_cells.start()
    load_merid.start()
    def remote(index, source, target, where, send_index=None):
        return pltpu.make_async_remote_copy(
            src_ref=source,
            dst_ref=target,
            send_sem=send_sem.at[index if send_index is None else send_index],
            recv_sem=recv_sem.at[index],
            device_id=where,
            device_id_type=MESH,
        )

    east = lax.rem(z + 1, RINGS)
    west = lax.rem(z + 3, RINGS)
    across = lax.rem(z + 2, RINGS)
    head = courant.at[0, :, :, pl.ds(0, LANES)]
    tail_rows = pl.ds(0, TAIL_SENT)
    own_tail = tails.at[0, tail_rows]

    class Pair:
        def __init__(self, first, second, sources, slot, where, sends=(None, None)):
            self.head = remote(first, sources[0], heads.at[slot], {"lon": where}, sends[0])
            self.tail = remote(second, sources[1], tails.at[slot, tail_rows], {"lon": where}, sends[1])

        def start(self):
            self.head.start()
            self.tail.start()

        def wait_recv(self):
            self.head.wait_recv()
            self.tail.wait_recv()

        def wait_send(self):
            self.head.wait_send()
            self.tail.wait_send()

    mine = (head, own_tail)
    send_east = Pair(EAST, EAST_TAIL, mine, 3, east)
    send_west = Pair(WEST, WEST_TAIL, mine, 1, west)
    send_across = Pair(ACROSS, ACROSS_TAIL, mine, 2, across)
    pass_west = Pair(ACROSS, ACROSS_TAIL, (heads.at[1], tails.at[1, tail_rows]), 2, west)
    pass_east = Pair(
        ACROSS, ACROSS_TAIL, (heads.at[3], tails.at[3, tail_rows]), 2, east, (PASS, PASS_TAIL)
    )
    pack_east = remote(PACK_EAST, pack.at[0], packs.at[0], {"lon": east})
    pack_west = remote(PACK_WEST, pack.at[1], packs.at[1], {"lon": west})
    send_north = remote(NORTH, sides.at[0], near.at[0], {"lat": band + 1})
    send_south = remote(SOUTH, sides.at[1], near.at[1], {"lat": band - 1})
    patient = (lax.rem(band, 2) == 1) & (z == 3)
    early = (
        (send_west, polar & ((z == 1) | (z == 2) | patient)),
        (send_east, polar & (z == 3) & jnp.logical_not(patient)),
    )
    late = ((send_east, polar & patient),)

    for copy, chosen in early:
        @pl.when(chosen)
        def _():
            copy.head.start()

    for other in range(RINGS - 1):
        @pl.when(z > other)
        def _():
            pl.semaphore_signal(ready.at[z], inc=1, device_id={"lon": other}, device_id_type=MESH)

    tails[0, TAIL_SENT - 8 :] = jnp.zeros((TAIL - TAIL_SENT + 8, LANES), jnp.float32)
    load_zonal.wait()
    tails[0, :tail] = zonal[:, :, LANES:].reshape(flat, tail).T
    for copy, chosen in early:
        @pl.when(chosen)
        def _():
            copy.tail.start()

    own[:LANES] = zonal[:, :, :LANES].reshape(flat, LANES).T
    own[LANES:] = tails[0]
    load_face.start()
    load_cell.start()

    @pl.when(polar)
    def _():
        load_limit.start()
        for copy in load_tables:
            copy.start()

    load_cells.wait()
    for t in range(count):
        first = cells[:, t, 8 : rows + 8, :LANES].reshape(flat, LANES).T
        last = cells[:, t, 8 : rows + 8, LANES:].reshape(flat, tail).T
        pack[0, t, 0:3] = last[tail - 3 : tail]
        pack[1, t, 0:3] = first[0:3]
    pack[0, count, 0:1] = own[cols - 1 : cols]

    @pl.when(east < z)
    def _():
        pack_east.start()

    @pl.when(west < z)
    def _():
        pack_west.start()

    for copy, chosen in late:
        @pl.when(chosen)
        def _():
            copy.start()

    load_merid.wait()
    planes = [(level, t) for level in range(levels) for t in range(count)]
    for k, (level, t) in enumerate(planes):
        sides[0, 3 * k : 3 * k + 3, :cols] = cells[level, t, rows + 5 : rows + 8]
        sides[1, 3 * k : 3 * k + 3, :cols] = cells[level, t, 8:11]
    first_speed = 3 * len(planes)
    for level in range(levels):
        sides[0, first_speed + level, :cols] = merid[level, rows + 7]

    def send_sides(chosen):
        @pl.when(chosen & has_north)
        def _():
            send_north.start()

        @pl.when(chosen & has_south)
        def _():
            send_south.start()

    send_sides(near_ring)
    for slot in range(1, RINGS):
        tails[slot, TAIL_SENT:] = jnp.zeros((TAIL - TAIL_SENT, LANES), jnp.float32)
    border[...] = jnp.zeros_like(border)
    turned[LANES:, :] = jnp.zeros((LANES, LANES), jnp.float32)

    def signal_beside(semaphore):
        @pl.when(has_south)
        def _():
            pl.semaphore_signal(semaphore, inc=1, device_id={"lat": band - 1}, device_id_type=MESH)

        @pl.when(has_north)
        def _():
            pl.semaphore_signal(semaphore, inc=1, device_id={"lat": band + 1}, device_id_type=MESH)

    def greet(other):
        @pl.when(z < other)
        def _():
            pl.semaphore_wait(ready.at[other], 1)
            for copy, where in ((pack_east, east), (pack_west, west)):
                @pl.when(where == other)
                def _():
                    copy.start()
            for copy, where in ((send_east, east), (send_west, west)):
                @pl.when(polar & (where == other))
                def _():
                    copy.start()

    def announce(others):
        for other in others:
            signal_beside(beside_in.at[other])

    def vouch(others):
        for other in others:
            pl.semaphore_wait(beside_in.at[other], beside)
            pl.semaphore_signal(beside_ok, inc=1, device_id={"lon": other}, device_id_type=MESH)

    def block(slot):
        return jnp.concatenate([heads[slot].reshape(flat, LANES).T, tails[slot]], axis=0)

    def forward(slot, values):
        high, low = split_halves(values)
        both = jnp.dot(
            table_hi[slot], jnp.concatenate([high, low], axis=1), preferred_element_type=jnp.float32
        )
        rest_term = jnp.dot(table_lo[slot], high, preferred_element_type=jnp.float32)
        return both[:, :LANES] + (both[:, LANES:] + rest_term)

    greet(1)

    @pl.when(z == 0)
    def _():
        announce((1,))
        vouch((1,))


    @pl.when(polar & (z == 3))
    def _():
        send_east.wait_send()
        send_across.start()

        @pl.when(jnp.logical_not(patient))
        def _():
            send_west.start()

    greet(2)

    greet(3)

    @pl.when(z == 1)
    def _():
        pl.semaphore_wait(beside_ok, 1)

    send_sides(z == 1)

    @pl.when(z == 1)
    def _():
        announce((2, 3))

    @pl.when(polar & (z == 1))
    def _():
        send_west.head.wait_recv()
        pass_west.head.start()
        send_west.tail.wait_recv()
        pass_west.tail.start()

    @pl.when(z == 1)
    def _():
        vouch((2, 3))

    @pl.when(polar)
    def _():
        for copy in load_tables:
            copy.wait()
        load_limit.wait()
        total[...] = forward(0, own[...])

    @pl.when(z >= 2)
    def _():
        pl.semaphore_wait(beside_ok, 1)

    send_sides(z >= 2)

    @pl.when(polar & (z == 1))
    def _():
        send_east.head.wait_recv()
        pass_east.head.start()
        send_east.tail.wait_recv()
        pass_east.tail.start()

    load_face.wait()
    load_cell.wait()

    @pl.when(has_south)
    def _():
        send_north.wait_recv()
        for k, (level, t) in enumerate(planes):
            cells[level, t, 5:8] = near[0, 3 * k : 3 * k + 3, :cols]
        for level in range(levels):
            merid[level, 7] = near[0, first_speed + level, :cols]

    @pl.when(has_north)
    def _():
        send_south.wait_recv()
        for k, (level, t) in enumerate(planes):
            cells[level, t, rows + 8 : rows + 11] = near[1, 3 * k : 3 * k + 3, :cols]

    @pl.when(jnp.logical_not(has_south))
    def _():
        cells[:, :, 0:8, :] = jnp.zeros((levels, count, 8, cols), jnp.float32)
        merid[:, 0:8, :] = jnp.zeros((levels, 8, cols), jnp.float32)

    @pl.when(jnp.logical_not(has_north))
    def _():
        cells[:, :, rows + 8 :, :] = jnp.zeros((levels, count, 8, cols), jnp.float32)

    for level in range(levels):
        speed = merid[level, 7 : rows + 8]
        by_face, by_edge, by_cell = flux_factors(speed, face_v[7 : rows + 8])
        upward = speed > 0
        inverse_cell = cell_v[...]
        for t in range(count):
            def shifted(offset):
                return cells[level, t, 7 + offset : 8 + offset + rows, :]

            below, here, above, beyond = shifted(-1), shifted(0), shifted(1), shifted(2)
            edge_here = 7.0 * (below + here) - (shifted(-2) + above)
            edge_face = 7.0 * (here + above) - (below + beyond)
            edge_next = 7.0 * (above + beyond) - (here + shifted(3))
            flux = (
                by_face * edge_face
                + by_edge * jnp.where(upward, edge_here, edge_next)
                + by_cell * jnp.where(upward, here, above)
            )
            change = (flux[1:] - flux[:-1]) * inverse_cell
            rest[level, t] = cells[level, t, 8 : rows + 8, :] - change

    @pl.when(polar & (z == 2))
    def _():
        send_east.head.wait_recv()
        pass_east.head.start()
        send_east.tail.wait_recv()
        pass_east.tail.start()

    @pl.when(polar)
    def _():
        @pl.when(z == 0)
        def _():
            send_west.wait_recv()

        @pl.when(z == 3)
        def _():
            send_east.wait_recv()

        slot = jnp.where(z == 0, 1, 3)
        total[...] += forward(slot, block(slot))

    pack_east.wait_recv()
    pack_west.wait_recv()
    for t in range(count):
        border[t, tail : tail + 3] = packs[1, t, 0:3]
        border[t, LANES - 3 : LANES] = packs[0, t, 0:3]
        here_out[:, t, :, :LANES] = cells[:, t, 8 : rows + 8, :LANES]
        here_out[:, t, :, LANES:] = border[t].T.reshape(levels, rows, LANES)
        here_out[:, t, :, LANES:cols] = cells[:, t, 8 : rows + 8, LANES:]

    for level in range(levels):
        here = here_out[level]

        def moved(offset):
            return pltpu.roll(here, (-offset) % (2 * LANES), 2)

        back_two, back_one, ahead_one, ahead_two = moved(-2), moved(-1), moved(1), moved(2)
        next_out[level] = ahead_one
        edge_out[level] = 7.0 * (back_one + here) - (back_two + ahead_one)
        face_out[level] = 7.0 * (here + ahead_one) - (back_one + ahead_two)
        beyond_out[level] = 7.0 * (ahead_one + ahead_two) - (here + moved(3))

    def finish(body_rows, west_row):
        turned[:cols] = body_rows
        turned[2 * LANES - 8 :] = jnp.broadcast_to(west_row, (8, LANES))

    @pl.when(jnp.logical_not(polar))
    def _():
        finish(own[:cols], packs[0, count, 0:1])

    @pl.when(polar)
    def _():
        lane = lax.broadcasted_iota(jnp.int32, (8, 2 * LANES), 1)
        spread = jnp.broadcast_to(limit_v[...].reshape(1, bands * rows), (8, bands * rows))
        spread = pltpu.roll(spread, lax.rem((bands - band) * rows, bands * rows), 1)
        limit = jnp.where(lane < rows, spread, 0)
        copies = 1
        while copies < levels:
            limit = limit + pltpu.roll(limit, copies * rows, 1)
            copies *= 2
        limit = limit[0:1, :LANES]
        wave = lax.broadcasted_iota(jnp.int32, (circle, LANES), 0)
        wave = jnp.where(wave <= circle // 2, wave, wave - circle // 2)

        @pl.when(z == 0)
        def _():
            send_east.wait_recv()

        @pl.when(z >= 2)
        def _():
            send_west.wait_recv()

        slot = jnp.where(z == 0, 3, 1)
        total[...] += forward(slot, block(slot))
        send_across.wait_recv()
        coeff = jnp.where(wave <= limit, total[...] + forward(2, block(2)), 0.0)
        high, low = split_halves(coeff)
        both = jnp.dot(
            inv_hi[...], jnp.concatenate([high, low], axis=1), preferred_element_type=jnp.float32
        )
        rest_term = jnp.dot(inv_lo[...], high, preferred_element_type=jnp.float32)
        smooth = both[:, :LANES] + (both[:, LANES:] + rest_term)
        kept = limit < circle // 2
        finish(
            jnp.where(kept, smooth[:cols], own[:cols]),
            jnp.where(kept, smooth[DEPTH - 1 :], packs[0, count, 0:1]),
        )

    faces[:, :, :LANES] = turned[:LANES].T.reshape(levels, rows, LANES)
    faces[:, :, LANES:] = turned[LANES:].T.reshape(levels, rows, LANES)

    pack_east.wait_send()
    pack_west.wait_send()

    @pl.when(polar)
    def _():
        @pl.when(z != 3)
        def _():
            send_east.wait_send()

        send_west.wait_send()

        @pl.when(z == 3)
        def _():
            send_across.wait_send()

        @pl.when(z == 1)
        def _():
            pass_west.wait_send()

        @pl.when((z == 1) | (z == 2))
        def _():
            pass_east.wait_send()

    @pl.when(has_north)
    def _():
        send_north.wait_send()

    @pl.when(has_south)
    def _():
        send_south.wait_send()


def flux_kernel(
    faces, here, following, edge, face_edge, beyond, rest, updated, filtered, result, smooth, sem
):
    levels, _, _, cols = rest.shape
    smooth[...] = faces[:, :, :cols]
    store = pltpu.make_async_copy(smooth, filtered, sem.at[levels])
    store.start()
    for level in range(levels):
        speed = faces[level]
        by_face, by_edge, by_cell = flux_factors(speed, 1.0)
        eastward = speed > 0
        flux = (
            by_face[None] * face_edge[level]
            + by_edge[None] * jnp.where(eastward[None], edge[level], beyond[level])
            + by_cell[None] * jnp.where(eastward[None], here[level], following[level])
        )
        change = flux - pltpu.roll(flux, 1, 2)
        result[level] = rest[level] - change[:, :, :cols]
        pltpu.make_async_copy(result.at[level], updated.at[level], sem.at[level]).start()
    for level in range(levels):
        pltpu.make_async_copy(result.at[level], updated.at[level], sem.at[level]).wait()
    store.wait()


def ring_body(bands, tracers, courant, cutoffs):
    levels, count, rows, cols = tracers.shape
    circle = cols * RINGS
    sizes = (levels, count, rows, cols, bands, bands // 4, circle)
    ahead_hi, ahead_lo, back_hi, back_lo = filter_tables(circle, cols)
    face_w, cell_w = weight_tables(bands, rows, cols)
    hbm = pl.BlockSpec(memory_space=pltpu.HBM)
    vmem = pl.BlockSpec(memory_space=pltpu.VMEM)
    f32, half = jnp.float32, jnp.bfloat16
    slab = (levels, count, rows)
    strip = -(-(3 * levels * count + levels) // 8) * 8
    wide = jax.ShapeDtypeStruct(slab + (2 * LANES,), f32)
    parts = pl.pallas_call(
        functools.partial(gather_kernel, sizes),
        out_shape=(jax.ShapeDtypeStruct((levels, rows, 2 * LANES), f32),)
        + (wide,) * 5
        + (jax.ShapeDtypeStruct(tracers.shape, f32),),
        in_specs=[hbm] * 9,
        out_specs=(vmem,) * 7,
        scratch_shapes=[
            pltpu.VMEM((levels, rows, cols), f32),
            pltpu.VMEM((levels, count, rows + 16, cols), f32),
            pltpu.VMEM((levels, rows + 8, cols), f32),
            pltpu.VMEM((RINGS, levels, rows, LANES), f32),
            pltpu.VMEM((RINGS, TAIL, LANES), f32),
            pltpu.VMEM((DEPTH, LANES), f32),
            pltpu.VMEM((circle, LANES), f32),
            pltpu.VMEM((RINGS, circle, DEPTH), half),
            pltpu.VMEM((RINGS, circle, DEPTH), half),
            pltpu.VMEM((DEPTH, circle), half),
            pltpu.VMEM((DEPTH, circle), half),
            pltpu.VMEM((bands * rows,), jnp.int32),
            pltpu.VMEM((rows + 8, cols), f32),
            pltpu.VMEM((rows, cols), f32),
            pltpu.VMEM((2, count + 1, 8, LANES), f32),
            pltpu.VMEM((2, count + 1, 8, LANES), f32),
            pltpu.VMEM((2, strip, 2 * LANES), f32),
            pltpu.VMEM((2, strip, 2 * LANES), f32),
            pltpu.VMEM((count, LANES, LANES), f32),
            pltpu.VMEM((2 * LANES, LANES), f32),
            pltpu.SemaphoreType.DMA((10,)),
            pltpu.SemaphoreType.DMA((12,)),
            pltpu.SemaphoreType.DMA((10,)),
            pltpu.SemaphoreType.REGULAR((RINGS,)),
            pltpu.SemaphoreType.REGULAR((RINGS,)),
            pltpu.SemaphoreType.REGULAR,
        ],
        compiler_params=pltpu.CompilerParams(
            collective_id=0, has_side_effects=True, vmem_limit_bytes=24 * 2**20
        ),
    )(
        *(
            pltpu.with_memory_space_constraint(jnp.asarray(operand), pltpu.HBM)
            for operand in (
                tracers, courant, cutoffs, ahead_hi, ahead_lo, back_hi, back_lo, face_w, cell_w
            )
        )
    )
    return pl.pallas_call(
        flux_kernel,
        out_shape=(
            jax.ShapeDtypeStruct(tracers.shape, f32),
            jax.ShapeDtypeStruct((levels, rows, cols), f32),
        ),
        in_specs=[vmem] * 7,
        out_specs=(hbm, hbm),
        scratch_shapes=[
            pltpu.VMEM(tracers.shape, f32),
            pltpu.VMEM((levels, rows, cols), f32),
            pltpu.SemaphoreType.DMA((levels + 1,)),
        ],
        compiler_params=pltpu.CompilerParams(vmem_limit_bytes=16 * 2**20),
    )(*parts)


def body(bands, tracers, courant, cutoffs):
    levels, _, rows, cols = tracers.shape
    fits = (
        lax.axis_size("lon") == RINGS
        and bands % 4 == 0
        and bands * rows == 2 * LANES
        and levels * rows == LANES
        and LANES < cols <= LANES + TAIL_SENT - 4
        and cols % 4 == 0
    )
    if fits:
        return ring_body(bands, tracers, courant, cutoffs)
    return general_body(tracers, courant, cutoffs)


def solution(mesh):
    in_specs = (P(None, None, "lat", "lon"), P(None, None, "lat", "lon"), P())
    out_specs = (P(None, None, "lat", "lon"), P(None, "lat", "lon"))
    return jax.shard_map(
        functools.partial(body, mesh.shape["lat"]),
        mesh=mesh,
        in_specs=in_specs,
        out_specs=out_specs,
        check_vma=False,
    )
```

```python
import functools
import math

import jax
import numpy as np
import jax.numpy as jnp
from jax import lax
from jax.experimental import pallas as pl
from jax.experimental.pallas import tpu as pltpu
from jax.sharding import PartitionSpec as P


def padded(cells, sides, width, closed):
    for axis, dim in sides:
        count = lax.axis_size(axis)
        ends = count if closed else count - 1
        head = lax.slice_in_dim(cells, 0, width, axis=dim)
        tail = lax.slice_in_dim(cells, cells.shape[dim] - width, cells.shape[dim], axis=dim)
        cells = jnp.concatenate(
            [
                lax.ppermute(tail, axis, [(i, (i + 1) % count) for i in range(ends)]),
                cells,
                lax.ppermute(head, axis, [((i + 1) % count, i) for i in range(ends)]),
            ],
            axis=dim,
        )
    return cells


def take_range(values, start, count, axis_index):
    return lax.slice_in_dim(values, start, start + count, axis=axis_index)


def ppm_flux(extended, courant_faces, axis_index):
    cell_count = extended.shape[axis_index] - 6
    edge_values = 7.0 / 12.0 * (
        take_range(extended, 1, cell_count + 3, axis_index)
        + take_range(extended, 2, cell_count + 3, axis_index)
    ) - 1.0 / 12.0 * (
        take_range(extended, 0, cell_count + 3, axis_index)
        + take_range(extended, 3, cell_count + 3, axis_index)
    )
    left_edge = take_range(edge_values, 0, cell_count + 2, axis_index)
    right_edge = take_range(edge_values, 1, cell_count + 2, axis_index)
    centre = take_range(extended, 2, cell_count + 2, axis_index)
    slopes = right_edge - left_edge
    curvature = 6.0 * centre - 3.0 * (left_edge + right_edge)
    upwind = take_range(right_edge, 0, cell_count + 1, axis_index) - 0.5 * courant_faces * (
        take_range(slopes, 0, cell_count + 1, axis_index)
        - (1.0 - courant_faces * (2.0 / 3.0)) * take_range(curvature, 0, cell_count + 1, axis_index)
    )
    downwind = take_range(left_edge, 1, cell_count + 1, axis_index) - 0.5 * courant_faces * (
        take_range(slopes, 1, cell_count + 1, axis_index)
        + (1.0 + courant_faces * (2.0 / 3.0)) * take_range(curvature, 1, cell_count + 1, axis_index)
    )
    return courant_faces * jnp.where(courant_faces > 0, upwind, downwind)


def metric_weights(first_row, row_count, grid_rows):
    faces = first_row + jnp.arange(-1, row_count, dtype=jnp.int32)
    centres = first_row + jnp.arange(row_count, dtype=jnp.int32)
    face_weight = jnp.sin(
        jnp.minimum(faces + 1, grid_rows - 1 - faces).astype(jnp.float32) * (math.pi / grid_rows)
    )
    cell_weight = jnp.sin(
        (jnp.minimum(centres, grid_rows - 1 - centres).astype(jnp.float32) + 0.5)
        * (math.pi / grid_rows)
    )
    return (face_weight, cell_weight)


def angle_table(first_ids, second_ids, period):
    product = first_ids[:, None] * second_ids[None, :] % period
    angles = product.astype(jnp.float32) * (2.0 * math.pi / period)
    return (jnp.cos(angles), jnp.sin(angles))


def spectral_lowpass(row_block, limits, outer_count):
    row_count, circle = row_block.shape
    inner_count = circle // outer_count
    highest = lax.Precision.HIGHEST
    grid_values = row_block.reshape(row_count, outer_count, inner_count)
    outer_ids = jnp.arange(outer_count, dtype=jnp.int32)
    inner_ids = jnp.arange(inner_count, dtype=jnp.int32)
    outer_cos, outer_sin = angle_table(outer_ids, outer_ids, outer_count)
    inner_cos, inner_sin = angle_table(inner_ids, inner_ids, inner_count)
    twiddle_cos, twiddle_sin = angle_table(inner_ids, outer_ids, circle)
    first_real = jnp.einsum("rab,ak->rbk", grid_values, outer_cos, precision=highest)
    first_imag = -jnp.einsum("rab,ak->rbk", grid_values, outer_sin, precision=highest)
    turned_real = first_real * twiddle_cos + first_imag * twiddle_sin
    turned_imag = first_imag * twiddle_cos - first_real * twiddle_sin
    coeff_real = jnp.einsum("rbk,bj->rjk", turned_real, inner_cos, precision=highest) + jnp.einsum(
        "rbk,bj->rjk", turned_imag, inner_sin, precision=highest
    )
    coeff_imag = jnp.einsum("rbk,bj->rjk", turned_imag, inner_cos, precision=highest) - jnp.einsum(
        "rbk,bj->rjk", turned_real, inner_sin, precision=highest
    )
    wavenumber = inner_ids[:, None] * outer_count + outer_ids[None, :]
    folded = jnp.minimum(wavenumber, circle - wavenumber)
    keep_mask = folded[None, :, :] <= limits[:, None, None]
    coeff_real = jnp.where(keep_mask, coeff_real, 0.0)
    coeff_imag = jnp.where(keep_mask, coeff_imag, 0.0)
    back_real = jnp.einsum("rjk,jb->rbk", coeff_real, inner_cos, precision=highest) - jnp.einsum(
        "rjk,jb->rbk", coeff_imag, inner_sin, precision=highest
    )
    back_imag = jnp.einsum("rjk,jb->rbk", coeff_imag, inner_cos, precision=highest) + jnp.einsum(
        "rjk,jb->rbk", coeff_real, inner_sin, precision=highest
    )
    reverted_real = back_real * twiddle_cos - back_imag * twiddle_sin
    reverted_imag = back_imag * twiddle_cos + back_real * twiddle_sin
    signal = jnp.einsum("rbk,ka->rab", reverted_real, outer_cos, precision=highest) - jnp.einsum(
        "rbk,ka->rab", reverted_imag, outer_sin, precision=highest
    )
    return (signal / circle).reshape(row_count, circle)


def general_body(tracers, courant, cutoffs):
    levels, tracer_count, lat_rows, lon_cols = tracers.shape
    lon_groups = lax.axis_size("lon")
    lon_index = lax.axis_index("lon")
    lat_bands = lax.axis_size("lat")
    band_index = lax.axis_index("lat")
    grid_rows = lat_rows * lat_bands
    zonal = courant[0]
    meridional = courant[1]
    lat_stack = jnp.concatenate([tracers, meridional[:, None]], axis=1)
    lat_ext = padded(lat_stack, (("lat", 2),), 3, False)
    flat_count = levels * lat_rows
    flat_zonal = zonal.reshape(flat_count, lon_cols)
    edges = jnp.concatenate([tracers[..., :3], tracers[..., lon_cols - 3 :]], axis=-1)
    west_index = (lon_index + lon_groups - 1) % lon_groups
    east_index = (lon_index + 1) % lon_groups
    local_limits = lax.dynamic_slice_in_dim(cutoffs, band_index * lat_rows, lat_rows)
    limits = jnp.tile(local_limits, levels)
    circle = lon_cols * lon_groups
    gathered = lax.all_gather(flat_zonal, "lon", axis=0)
    gathered_edges = lax.all_gather(edges, "lon", axis=0)
    west = lax.dynamic_index_in_dim(gathered_edges, west_index, 0, keepdims=False)[..., 3:]
    east = lax.dynamic_index_in_dim(gathered_edges, east_index, 0, keepdims=False)[..., :3]
    west_raw = lax.dynamic_index_in_dim(gathered, west_index, 0, keepdims=False)[:, -1:]
    raw_ext = jnp.concatenate([west_raw, flat_zonal], axis=1)
    whole_rows = jnp.transpose(gathered, (1, 0, 2)).reshape(flat_count, circle)
    lowpass = spectral_lowpass(whole_rows, limits, lon_groups)
    lowpass = jnp.concatenate([lowpass[:, -1:], lowpass], axis=1)
    lowpass_ext = lax.dynamic_slice_in_dim(lowpass, lon_index * lon_cols, lon_cols + 1, axis=1)
    lon_ext = jnp.concatenate([west, tracers, east], axis=-1)
    filtered_flat = jnp.where((limits < circle // 2)[:, None], lowpass_ext, raw_ext)
    zonal_faces = filtered_flat.reshape(levels, 1, lat_rows, lon_cols + 1)
    filtered_zonal = zonal_faces[:, 0, :, 1:]
    flux_east = ppm_flux(lon_ext, zonal_faces, 3)
    face_weight, cell_weight = metric_weights(band_index * lat_rows, lat_rows, grid_rows)
    flux_north = (
    ppm_flux(lat_ext[:, :tracer_count], lat_ext[:, tracer_count:, 2 : lat_rows + 3, :], 2)
    * face_weight[None, None, :, None]
    )
    change = (
    flux_east[:, :, :, 1:]
    - flux_east[:, :, :, :-1]
    + (flux_north[:, :, 1:, :] - flux_north[:, :, :-1, :]) / cell_weight[None, None, :, None]
    )
    return (tracers - change, filtered_zonal)


MESH = pl.DeviceIdType.MESH
RINGS = 4
LANES = 128
DEPTH = 192
TAIL = 64
TAIL_SENT = 56
EAST, WEST, ACROSS, EAST_TAIL, WEST_TAIL, ACROSS_TAIL, PACK_EAST, PACK_WEST, NORTH, SOUTH, PASS, PASS_TAIL, RESULT = range(13)


def split_halves(values):
    high = values.astype(jnp.bfloat16)
    low = (values - high.astype(jnp.float32)).astype(jnp.bfloat16)
    return high, low


def filter_tables(circle, cols):
    half = circle // 2
    cells = np.arange(circle, dtype=np.int64)
    cos_ids = np.arange(half + 1, dtype=np.int64)
    sin_ids = np.arange(1, half, dtype=np.int64)

    def waves(ids):
        return np.concatenate(
            [
                np.cos(2.0 * np.pi * ((cos_ids[:, None] * ids[None, :]) % circle) / circle),
                np.sin(2.0 * np.pi * ((sin_ids[:, None] * ids[None, :]) % circle) / circle),
            ],
            axis=0,
        )

    def halves(table):
        high = table.astype(jnp.bfloat16)
        low = (table - high.astype(np.float64)).astype(jnp.bfloat16)
        return high, low

    forward = np.zeros((circle // cols, circle, DEPTH))
    forward[:, :, :cols] = waves(cells).reshape(circle, circle // cols, cols).transpose(1, 0, 2)
    wavenumber = np.concatenate([cos_ids, sin_ids])
    scale = np.where((wavenumber == 0) | (wavenumber == half), 1.0, 2.0) / circle
    inverse = np.zeros((3, DEPTH, circle))
    for index, start in enumerate((0, -cols, cols)):
        inverse[index, :cols] = waves(start + np.arange(cols)).T * scale
        inverse[index, DEPTH - 1] = waves(np.array([start - 1]))[:, 0] * scale
    return halves(forward) + halves(inverse)


def weight_tables(bands, rows, cols):
    grid_rows = bands * rows
    faces = np.arange(bands)[:, None] * rows + np.arange(-8, rows)[None, :]
    cells = np.arange(bands)[:, None] * rows + np.arange(rows)[None, :]
    face = np.sin(np.minimum(faces + 1, grid_rows - 1 - faces) * (np.pi / grid_rows))
    cell = 1.0 / np.sin((np.minimum(cells, grid_rows - 1 - cells) + 0.5) * (np.pi / grid_rows))
    face = np.broadcast_to(face[:, :, None], face.shape + (cols,))
    cell = np.broadcast_to(cell[:, :, None], cell.shape + (cols,))
    return face.astype(np.float32), cell.astype(np.float32)


def flux_factors(courant, scale):
    size = jnp.abs(courant)
    steep = size - size * size
    middle = 3.0 * size - 2.0 * size * size
    scaled = courant * scale
    return (
        scaled * (1.0 + steep - middle) * (1.0 / 12.0),
        scaled * steep * (-1.0 / 12.0),
        scaled * middle,
    )


def gather_kernel(
    sizes,
    tracers, courant, cutoffs, ahead_hi, ahead_lo, back_hi, back_lo, face_w, cell_w,
    faces, here_out, next_out, edge_out, face_out, beyond_out, rest,
    zonal, cells, merid, heads, tails, own, total, table_hi, table_lo, inv_hi, inv_lo, far_hi, far_lo, result_out, result_in, limit_v, face_v, cell_v,
    pack, packs, sides, near, border, turned,
    load_sem, send_sem, recv_sem, ready, beside_in, beside_ok,
):
    levels, count, rows, cols, bands, polar_bands, circle = sizes
    flat = levels * rows
    z = lax.axis_index("lon")
    band = lax.axis_index("lat")
    polar = (band < polar_bands) | (band >= bands - polar_bands)
    has_south = band > 0
    has_north = band < bands - 1
    tail = cols - LANES
    barrier = pltpu.get_barrier_semaphore()

    def load(index, source, target):
        return pltpu.make_async_copy(source, target, load_sem.at[index])

    load_zonal = load(0, courant.at[0], zonal)
    load_cells = load(1, tracers, cells.at[:, :, pl.ds(8, rows), :])
    load_merid = load(2, courant.at[1], merid.at[:, pl.ds(8, rows), :])
    load_limit = load(3, cutoffs, limit_v)
    load_face = load(4, face_w.at[band], face_v)
    load_cell = load(5, cell_w.at[band], cell_v)
    load_tables = [
        load(6, ahead_hi, table_hi),
        load(7, ahead_lo, table_lo),
        load(8, back_hi.at[0], inv_hi),
        load(9, back_lo.at[0], inv_lo),
    ]
    load_far = [load(10, back_hi.at[z], far_hi), load(11, back_lo.at[z], far_lo)]
    load_zonal.start()
    load_cells.start()
    load_merid.start()
    for other in range(1, RINGS):
        @pl.when(z < other)
        def _():
            pl.semaphore_signal(barrier, inc=1, device_id={"lon": other}, device_id_type=MESH)

    near_ring = z == 0

    @pl.when(near_ring & has_south)
    def _():
        pl.semaphore_signal(barrier, inc=1, device_id={"lat": band - 1}, device_id_type=MESH)

    @pl.when(near_ring & has_north)
    def _():
        pl.semaphore_signal(barrier, inc=1, device_id={"lat": band + 1}, device_id_type=MESH)

    beside = has_south.astype(jnp.int32) + has_north.astype(jnp.int32)
    pl.semaphore_wait(barrier, z + jnp.where(near_ring, beside, 0))
    def remote(index, source, target, where, send_index=None):
        return pltpu.make_async_remote_copy(
            src_ref=source,
            dst_ref=target,
            send_sem=send_sem.at[index if send_index is None else send_index],
            recv_sem=recv_sem.at[index],
            device_id=where,
            device_id_type=MESH,
        )

    east = lax.rem(z + 1, RINGS)
    west = lax.rem(z + 3, RINGS)
    across = lax.rem(z + 2, RINGS)
    head = courant.at[0, :, :, pl.ds(0, LANES)]
    tail_rows = pl.ds(0, TAIL_SENT)
    own_tail = tails.at[0, tail_rows]

    class Pair:
        def __init__(self, first, second, sources, slot, where, sends=(None, None)):
            self.head = remote(first, sources[0], heads.at[slot], {"lon": where}, sends[0])
            self.tail = remote(second, sources[1], tails.at[slot, tail_rows], {"lon": where}, sends[1])

        def start(self):
            self.head.start()
            self.tail.start()

        def wait_recv(self):
            self.head.wait_recv()
            self.tail.wait_recv()

        def wait_send(self):
            self.head.wait_send()
            self.tail.wait_send()

    mine = (head, own_tail)
    send_east = Pair(EAST, EAST_TAIL, mine, 3, east)
    send_west = Pair(WEST, WEST_TAIL, mine, 1, west)
    send_across = Pair(ACROSS, ACROSS_TAIL, mine, 2, across)
    pass_west = Pair(ACROSS, ACROSS_TAIL, (heads.at[1], tails.at[1, tail_rows]), 2, west)
    pass_east = Pair(
        ACROSS, ACROSS_TAIL, (heads.at[3], tails.at[3, tail_rows]), 2, east, (PASS, PASS_TAIL)
    )
    pack_east = remote(PACK_EAST, pack.at[0], packs.at[0], {"lon": east})
    pack_west = remote(PACK_WEST, pack.at[1], packs.at[1], {"lon": west})
    send_north = remote(NORTH, sides.at[0], near.at[0], {"lat": band + 1})
    send_south = remote(SOUTH, sides.at[1], near.at[1], {"lat": band - 1})
    second_core = lax.rem(band, 2) == 1
    full = polar & jnp.logical_not(second_core)
    shared = polar & second_core
    middle = (z == 1) | (z == 2)
    gathers = full | (shared & middle)
    helps = shared & middle
    helped = shared & jnp.logical_not(middle)
    early = (
        (send_west, (full & middle) | (shared & (z == 2))),
        (send_east, full & (z == 3)),
        (send_west, shared & (z == 3)),
    )

    for copy, chosen in early:
        @pl.when(chosen)
        def _():
            copy.head.start()

    for other in range(RINGS - 1):
        @pl.when(z > other)
        def _():
            pl.semaphore_signal(ready.at[z], inc=1, device_id={"lon": other}, device_id_type=MESH)

    tails[0, TAIL_SENT - 8 :] = jnp.zeros((TAIL - TAIL_SENT + 8, LANES), jnp.float32)
    load_zonal.wait()
    tails[0, :tail] = zonal[:, :, LANES:].reshape(flat, tail).T
    for copy, chosen in early:
        @pl.when(chosen)
        def _():
            copy.tail.start()

    load_cells.wait()
    tail_lane = lax.broadcasted_iota(jnp.int32, (flat, tail), 1)
    for t in range(count):
        ends = jnp.where(
            tail_lane < tail - 3,
            cells[:, t, 8 : rows + 8, :tail].reshape(flat, tail),
            cells[:, t, 8 : rows + 8, LANES:].reshape(flat, tail),
        ).T
        pack[0, t, 0:3] = ends[tail - 3 :]
        pack[1, t, 0:3] = ends[0:3]
    pack[0, count, 0:1] = tails[0, tail - 1 : tail]

    @pl.when(east < z)
    def _():
        pack_east.start()

    @pl.when(west < z)
    def _():
        pack_west.start()

    @pl.when(shared & (z == 3))
    def _():
        send_across.start()

    load_face.start()
    load_cell.start()

    @pl.when(polar)
    def _():
        load_limit.start()

    @pl.when(gathers)
    def _():
        for copy in load_tables:
            copy.start()

    @pl.when(helps)
    def _():
        for copy in load_far:
            copy.start()

    own[:LANES] = zonal[:, :, :LANES].reshape(flat, LANES).T
    own[LANES:] = tails[0]
    load_merid.wait()
    planes = [(level, t) for level in range(levels) for t in range(count)]
    for k, (level, t) in enumerate(planes):
        sides[0, 3 * k : 3 * k + 3, :cols] = cells[level, t, rows + 5 : rows + 8]
        sides[1, 3 * k : 3 * k + 3, :cols] = cells[level, t, 8:11]
    first_speed = 3 * len(planes)
    for level in range(levels):
        sides[0, first_speed + level, :cols] = merid[level, rows + 7]

    def send_sides(chosen):
        @pl.when(chosen & has_north)
        def _():
            send_north.start()

        @pl.when(chosen & has_south)
        def _():
            send_south.start()

    send_sides(near_ring)
    for slot in range(1, RINGS):
        tails[slot, TAIL_SENT:] = jnp.zeros((TAIL - TAIL_SENT, LANES), jnp.float32)
    border[...] = jnp.zeros_like(border)
    for t in range(count):
        here_out[:, t, :, :LANES] = cells[:, t, 8 : rows + 8, :LANES]
        here_out[:, t, :, LANES:cols] = cells[:, t, 8 : rows + 8, LANES:]
    turned[LANES:, :] = jnp.zeros((LANES, LANES), jnp.float32)

    def signal_beside(semaphore):
        @pl.when(has_south)
        def _():
            pl.semaphore_signal(semaphore, inc=1, device_id={"lat": band - 1}, device_id_type=MESH)

        @pl.when(has_north)
        def _():
            pl.semaphore_signal(semaphore, inc=1, device_id={"lat": band + 1}, device_id_type=MESH)

    def greet(other):
        @pl.when(z < other)
        def _():
            pl.semaphore_wait(ready.at[other], 1)
            for copy, where in ((pack_east, east), (pack_west, west)):
                @pl.when(where == other)
                def _():
                    copy.start()
            for copy, chosen in (
                (send_east, (east == other) & (full | (shared & (z < 2)))),
                (send_west, (west == other) & full),
                (send_across, (across == other) & shared & (z == 0)),
            ):
                @pl.when(chosen)
                def _():
                    copy.start()

    def announce(others):
        for other in others:
            signal_beside(beside_in.at[other])

    def vouch(others):
        for other in others:
            pl.semaphore_wait(beside_in.at[other], beside)
            pl.semaphore_signal(beside_ok, inc=1, device_id={"lon": other}, device_id_type=MESH)

    def block(slot):
        return jnp.concatenate([heads[slot].reshape(flat, LANES).T, tails[slot]], axis=0)

    def forward(slot, values):
        high, low = split_halves(values)
        both = jnp.dot(
            table_hi[slot], jnp.concatenate([high, low], axis=1), preferred_element_type=jnp.float32
        )
        rest_term = jnp.dot(table_lo[slot], high, preferred_element_type=jnp.float32)
        return both[:, :LANES] + (both[:, LANES:] + rest_term)

    greet(1)

    @pl.when(z == 0)
    def _():
        announce((1,))
        vouch((1,))


    @pl.when(full & (z == 3))
    def _():
        send_across.start()
        send_west.start()

    greet(2)

    greet(3)

    @pl.when(z == 1)
    def _():
        pl.semaphore_wait(beside_ok, 1)

    send_sides(z == 1)

    @pl.when(z == 1)
    def _():
        announce((2, 3))

    @pl.when(shared & (z == 1))
    def _():
        send_west.wait_recv()

    @pl.when(full & (z == 1))
    def _():
        send_west.head.wait_recv()
        pass_west.head.start()
        send_west.tail.wait_recv()
        pass_west.tail.start()

    @pl.when(z == 1)
    def _():
        vouch((2, 3))

    @pl.when(polar)
    def _():
        load_limit.wait()

    @pl.when(gathers)
    def _():
        for copy in load_tables:
            copy.wait()
        total[...] = forward(0, own[...])

    @pl.when(helps)
    def _():
        for copy in load_far:
            copy.wait()

    @pl.when(z >= 2)
    def _():
        pl.semaphore_wait(beside_ok, 1)

    send_sides(z >= 2)

    @pl.when(shared & (z == 1))
    def _():
        send_east.wait_recv()

    @pl.when(full & (z == 1))
    def _():
        send_east.head.wait_recv()
        pass_east.head.start()
        send_east.tail.wait_recv()
        pass_east.tail.start()

    @pl.when(shared & (z == 2))
    def _():
        send_east.wait_recv()

    def kept_limit():
        lane = lax.broadcasted_iota(jnp.int32, (8, 2 * LANES), 1)
        spread = jnp.broadcast_to(limit_v[...].reshape(1, bands * rows), (8, bands * rows))
        spread = pltpu.roll(spread, lax.rem((bands - band) * rows, bands * rows), 1)
        limit = jnp.where(lane < rows, spread, 0)
        copies = 1
        while copies < levels:
            limit = limit + pltpu.roll(limit, copies * rows, 1)
            copies *= 2
        return limit[0:1, :LANES]

    send_result = remote(RESULT, result_out, result_in, {"lon": jnp.where(z == 1, 0, RINGS - 1)})

    def wait_second():
        @pl.when(z == 0)
        def _():
            send_east.wait_recv()

        @pl.when(z >= 2)
        def _():
            send_west.wait_recv()

    def last_coefficients(limit):
        wave = lax.broadcasted_iota(jnp.int32, (circle, LANES), 0)
        wave = jnp.where(wave <= circle // 2, wave, wave - circle // 2)
        send_across.wait_recv()
        return jnp.where(wave <= limit, total[...] + forward(2, block(2)), 0.0)

    def inverse(coeff, hi_ref, lo_ref):
        high, low = split_halves(coeff)
        both = jnp.dot(
            hi_ref[...], jnp.concatenate([high, low], axis=1), preferred_element_type=jnp.float32
        )
        rest_term = jnp.dot(lo_ref[...], high, preferred_element_type=jnp.float32)
        return both[:, :LANES] + (both[:, LANES:] + rest_term)

    @pl.when(helps)
    def _():
        limit = kept_limit()
        total[...] += forward(3, block(3))
        wait_second()
        total[...] += forward(1, block(1))
        coeff = last_coefficients(limit)
        result_out[...] = inverse(coeff, far_hi, far_lo)
        send_result.start()
        result_in[...] = inverse(coeff, inv_hi, inv_lo)

    def meridional():
        load_face.wait()
        load_cell.wait()

        @pl.when(has_south)
        def _():
            send_north.wait_recv()
            for k, (level, t) in enumerate(planes):
                cells[level, t, 5:8] = near[0, 3 * k : 3 * k + 3, :cols]
            for level in range(levels):
                merid[level, 7] = near[0, first_speed + level, :cols]

        @pl.when(has_north)
        def _():
            send_south.wait_recv()
            for k, (level, t) in enumerate(planes):
                cells[level, t, rows + 8 : rows + 11] = near[1, 3 * k : 3 * k + 3, :cols]

        @pl.when(jnp.logical_not(has_south))
        def _():
            cells[:, :, 0:8, :] = jnp.zeros((levels, count, 8, cols), jnp.float32)
            merid[:, 0:8, :] = jnp.zeros((levels, 8, cols), jnp.float32)

        @pl.when(jnp.logical_not(has_north))
        def _():
            cells[:, :, rows + 8 :, :] = jnp.zeros((levels, count, 8, cols), jnp.float32)

        for level in range(levels):
            speed = merid[level, 7 : rows + 8]
            by_face, by_edge, by_cell = flux_factors(speed, face_v[7 : rows + 8])
            upward = speed > 0
            inverse_cell = cell_v[...]
            for t in range(count):
                def shifted(offset):
                    return cells[level, t, 7 + offset : 8 + offset + rows, :]

                below, here, above, beyond = shifted(-1), shifted(0), shifted(1), shifted(2)
                edge_here = 7.0 * (below + here) - (shifted(-2) + above)
                edge_face = 7.0 * (here + above) - (below + beyond)
                edge_next = 7.0 * (above + beyond) - (here + shifted(3))
                flux = (
                    by_face * edge_face
                    + by_edge * jnp.where(upward, edge_here, edge_next)
                    + by_cell * jnp.where(upward, here, above)
                )
                change = (flux[1:] - flux[:-1]) * inverse_cell
                rest[level, t] = cells[level, t, 8 : rows + 8, :] - change

    @pl.when((z < 2) | shared)
    def _():
        meridional()

    @pl.when(full & (z == 2))
    def _():
        send_east.head.wait_recv()
        pass_east.head.start()
        send_east.tail.wait_recv()
        pass_east.tail.start()

    @pl.when(full)
    def _():
        @pl.when(z == 0)
        def _():
            send_west.wait_recv()

        @pl.when(z == 3)
        def _():
            send_east.wait_recv()

        slot = jnp.where(z == 0, 1, 3)
        total[...] += forward(slot, block(slot))

    wide_lane = lax.broadcasted_iota(jnp.int32, (levels, rows, LANES), 2)
    pack_east.wait_recv()
    pack_west.wait_recv()
    for t in range(count):
        border[t, tail : tail + 3] = packs[1, t, 0:3]
        border[t, LANES - 3 : LANES] = packs[0, t, 0:3]
        halo = border[t].T.reshape(levels, rows, LANES)
        here_out[:, t, :, LANES:] = jnp.where(wide_lane < tail, here_out[:, t, :, LANES:], halo)

    for level in range(levels):
        here = here_out[level]

        def moved(offset):
            return pltpu.roll(here, (-offset) % (2 * LANES), 2)

        back_two, back_one, ahead_one, ahead_two = moved(-2), moved(-1), moved(1), moved(2)
        next_out[level] = ahead_one
        edge_out[level] = 7.0 * (back_one + here) - (back_two + ahead_one)
        face_out[level] = 7.0 * (here + ahead_one) - (back_one + ahead_two)
        beyond_out[level] = 7.0 * (ahead_one + ahead_two) - (here + moved(3))

    def finish(body_rows, west_row):
        turned[:cols] = body_rows
        turned[2 * LANES - 8 :] = jnp.broadcast_to(west_row, (8, LANES))

    @pl.when(jnp.logical_not(polar))
    def _():
        finish(own[:cols], packs[0, count, 0:1])

    def finish_smooth(smooth, limit):
        kept = limit < circle // 2
        finish(
            jnp.where(kept, smooth[:cols], own[:cols]),
            jnp.where(kept, smooth[DEPTH - 1 :], packs[0, count, 0:1]),
        )

    @pl.when(full)
    def _():
        limit = kept_limit()
        wait_second()
        slot = jnp.where(z == 0, 3, 1)
        total[...] += forward(slot, block(slot))
        coeff = last_coefficients(limit)
        finish_smooth(inverse(coeff, inv_hi, inv_lo), limit)

    @pl.when(shared)
    def _():
        limit = kept_limit()

        @pl.when(jnp.logical_not(middle))
        def _():
            send_result.wait_recv()

        finish_smooth(result_in[...], limit)

    faces[:, :, :LANES] = turned[:LANES].T.reshape(levels, rows, LANES)
    faces[:, :, LANES:] = turned[LANES:].T.reshape(levels, rows, LANES)

    @pl.when((z >= 2) & jnp.logical_not(shared))
    def _():
        meridional()

    pack_east.wait_send()
    pack_west.wait_send()

    for copy, chosen in (
        (send_east, full | (shared & (z < 2))),
        (send_west, full | (shared & (z >= 2))),
        (send_across, (polar & (z == 3)) | (shared & (z == 0))),
        (pass_west, full & (z == 1)),
        (pass_east, full & middle),
        (send_result, helps),
    ):
        @pl.when(chosen)
        def _():
            copy.wait_send()

    @pl.when(has_north)
    def _():
        send_north.wait_send()

    @pl.when(has_south)
    def _():
        send_south.wait_send()


def flux_kernel(
    faces, here, following, edge, face_edge, beyond, rest, updated, filtered, result, smooth, sem
):
    levels, _, _, cols = rest.shape
    smooth[...] = faces[:, :, :cols]
    store = pltpu.make_async_copy(smooth, filtered, sem.at[levels])
    store.start()
    for level in range(levels):
        speed = faces[level]
        by_face, by_edge, by_cell = flux_factors(speed, 1.0)
        eastward = speed > 0
        flux = (
            by_face[None] * face_edge[level]
            + by_edge[None] * jnp.where(eastward[None], edge[level], beyond[level])
            + by_cell[None] * jnp.where(eastward[None], here[level], following[level])
        )
        change = flux - pltpu.roll(flux, 1, 2)
        result[level] = rest[level] - change[:, :, :cols]
        pltpu.make_async_copy(result.at[level], updated.at[level], sem.at[level]).start()
    for level in range(levels):
        pltpu.make_async_copy(result.at[level], updated.at[level], sem.at[level]).wait()
    store.wait()


def ring_body(bands, tracers, courant, cutoffs):
    levels, count, rows, cols = tracers.shape
    circle = cols * RINGS
    sizes = (levels, count, rows, cols, bands, bands // 4, circle)
    ahead_hi, ahead_lo, back_hi, back_lo = filter_tables(circle, cols)
    face_w, cell_w = weight_tables(bands, rows, cols)
    hbm = pl.BlockSpec(memory_space=pltpu.HBM)
    vmem = pl.BlockSpec(memory_space=pltpu.VMEM)
    f32, half = jnp.float32, jnp.bfloat16
    slab = (levels, count, rows)
    strip = -(-(3 * levels * count + levels) // 8) * 8
    wide = jax.ShapeDtypeStruct(slab + (2 * LANES,), f32)
    parts = pl.pallas_call(
        functools.partial(gather_kernel, sizes),
        out_shape=(jax.ShapeDtypeStruct((levels, rows, 2 * LANES), f32),)
        + (wide,) * 5
        + (jax.ShapeDtypeStruct(tracers.shape, f32),),
        in_specs=[hbm] * 9,
        out_specs=(vmem,) * 7,
        scratch_shapes=[
            pltpu.VMEM((levels, rows, cols), f32),
            pltpu.VMEM((levels, count, rows + 16, cols), f32),
            pltpu.VMEM((levels, rows + 8, cols), f32),
            pltpu.VMEM((RINGS, levels, rows, LANES), f32),
            pltpu.VMEM((RINGS, TAIL, LANES), f32),
            pltpu.VMEM((DEPTH, LANES), f32),
            pltpu.VMEM((circle, LANES), f32),
            pltpu.VMEM((RINGS, circle, DEPTH), half),
            pltpu.VMEM((RINGS, circle, DEPTH), half),
            pltpu.VMEM((DEPTH, circle), half),
            pltpu.VMEM((DEPTH, circle), half),
            pltpu.VMEM((DEPTH, circle), half),
            pltpu.VMEM((DEPTH, circle), half),
            pltpu.VMEM((DEPTH, LANES), f32),
            pltpu.VMEM((DEPTH, LANES), f32),
            pltpu.VMEM((bands * rows,), jnp.int32),
            pltpu.VMEM((rows + 8, cols), f32),
            pltpu.VMEM((rows, cols), f32),
            pltpu.VMEM((2, count + 1, 8, LANES), f32),
            pltpu.VMEM((2, count + 1, 8, LANES), f32),
            pltpu.VMEM((2, strip, 2 * LANES), f32),
            pltpu.VMEM((2, strip, 2 * LANES), f32),
            pltpu.VMEM((count, LANES, LANES), f32),
            pltpu.VMEM((2 * LANES, LANES), f32),
            pltpu.SemaphoreType.DMA((12,)),
            pltpu.SemaphoreType.DMA((13,)),
            pltpu.SemaphoreType.DMA((13,)),
            pltpu.SemaphoreType.REGULAR((RINGS,)),
            pltpu.SemaphoreType.REGULAR((RINGS,)),
            pltpu.SemaphoreType.REGULAR,
        ],
        compiler_params=pltpu.CompilerParams(
            collective_id=0, has_side_effects=True, vmem_limit_bytes=24 * 2**20
        ),
    )(
        *(
            pltpu.with_memory_space_constraint(jnp.asarray(operand), pltpu.HBM)
            for operand in (
                tracers, courant, cutoffs, ahead_hi, ahead_lo, back_hi, back_lo, face_w, cell_w
            )
        )
    )
    return pl.pallas_call(
        flux_kernel,
        out_shape=(
            jax.ShapeDtypeStruct(tracers.shape, f32),
            jax.ShapeDtypeStruct((levels, rows, cols), f32),
        ),
        in_specs=[vmem] * 7,
        out_specs=(hbm, hbm),
        scratch_shapes=[
            pltpu.VMEM(tracers.shape, f32),
            pltpu.VMEM((levels, rows, cols), f32),
            pltpu.SemaphoreType.DMA((levels + 1,)),
        ],
        compiler_params=pltpu.CompilerParams(vmem_limit_bytes=16 * 2**20),
    )(*parts)


def body(bands, tracers, courant, cutoffs):
    levels, _, rows, cols = tracers.shape
    fits = (
        lax.axis_size("lon") == RINGS
        and bands % 4 == 0
        and bands * rows == 2 * LANES
        and levels * rows == LANES
        and LANES < cols <= LANES + TAIL_SENT - 4
        and bands % 8 == 0
        and cols % 4 == 0
    )
    if fits:
        return ring_body(bands, tracers, courant, cutoffs)
    return general_body(tracers, courant, cutoffs)


def solution(mesh):
    in_specs = (P(None, None, "lat", "lon"), P(None, None, "lat", "lon"), P())
    out_specs = (P(None, None, "lat", "lon"), P(None, "lat", "lon"))
    return jax.shard_map(
        functools.partial(body, mesh.shape["lat"]),
        mesh=mesh,
        in_specs=in_specs,
        out_specs=out_specs,
        check_vma=False,
    )
```

```python
import functools
import math

import jax
import numpy as np
import jax.numpy as jnp
from jax import lax
from jax.experimental import pallas as pl
from jax.experimental.pallas import tpu as pltpu
from jax.sharding import PartitionSpec as P


def padded(cells, sides, width, closed):
    for axis, dim in sides:
        count = lax.axis_size(axis)
        ends = count if closed else count - 1
        head = lax.slice_in_dim(cells, 0, width, axis=dim)
        tail = lax.slice_in_dim(cells, cells.shape[dim] - width, cells.shape[dim], axis=dim)
        cells = jnp.concatenate(
            [
                lax.ppermute(tail, axis, [(i, (i + 1) % count) for i in range(ends)]),
                cells,
                lax.ppermute(head, axis, [((i + 1) % count, i) for i in range(ends)]),
            ],
            axis=dim,
        )
    return cells


def take_range(values, start, count, axis_index):
    return lax.slice_in_dim(values, start, start + count, axis=axis_index)


def ppm_flux(extended, courant_faces, axis_index):
    cell_count = extended.shape[axis_index] - 6
    edge_values = 7.0 / 12.0 * (
        take_range(extended, 1, cell_count + 3, axis_index)
        + take_range(extended, 2, cell_count + 3, axis_index)
    ) - 1.0 / 12.0 * (
        take_range(extended, 0, cell_count + 3, axis_index)
        + take_range(extended, 3, cell_count + 3, axis_index)
    )
    left_edge = take_range(edge_values, 0, cell_count + 2, axis_index)
    right_edge = take_range(edge_values, 1, cell_count + 2, axis_index)
    centre = take_range(extended, 2, cell_count + 2, axis_index)
    slopes = right_edge - left_edge
    curvature = 6.0 * centre - 3.0 * (left_edge + right_edge)
    upwind = take_range(right_edge, 0, cell_count + 1, axis_index) - 0.5 * courant_faces * (
        take_range(slopes, 0, cell_count + 1, axis_index)
        - (1.0 - courant_faces * (2.0 / 3.0)) * take_range(curvature, 0, cell_count + 1, axis_index)
    )
    downwind = take_range(left_edge, 1, cell_count + 1, axis_index) - 0.5 * courant_faces * (
        take_range(slopes, 1, cell_count + 1, axis_index)
        + (1.0 + courant_faces * (2.0 / 3.0)) * take_range(curvature, 1, cell_count + 1, axis_index)
    )
    return courant_faces * jnp.where(courant_faces > 0, upwind, downwind)


def metric_weights(first_row, row_count, grid_rows):
    faces = first_row + jnp.arange(-1, row_count, dtype=jnp.int32)
    centres = first_row + jnp.arange(row_count, dtype=jnp.int32)
    face_weight = jnp.sin(
        jnp.minimum(faces + 1, grid_rows - 1 - faces).astype(jnp.float32) * (math.pi / grid_rows)
    )
    cell_weight = jnp.sin(
        (jnp.minimum(centres, grid_rows - 1 - centres).astype(jnp.float32) + 0.5)
        * (math.pi / grid_rows)
    )
    return (face_weight, cell_weight)


def angle_table(first_ids, second_ids, period):
    product = first_ids[:, None] * second_ids[None, :] % period
    angles = product.astype(jnp.float32) * (2.0 * math.pi / period)
    return (jnp.cos(angles), jnp.sin(angles))


def spectral_lowpass(row_block, limits, outer_count):
    row_count, circle = row_block.shape
    inner_count = circle // outer_count
    highest = lax.Precision.HIGHEST
    grid_values = row_block.reshape(row_count, outer_count, inner_count)
    outer_ids = jnp.arange(outer_count, dtype=jnp.int32)
    inner_ids = jnp.arange(inner_count, dtype=jnp.int32)
    outer_cos, outer_sin = angle_table(outer_ids, outer_ids, outer_count)
    inner_cos, inner_sin = angle_table(inner_ids, inner_ids, inner_count)
    twiddle_cos, twiddle_sin = angle_table(inner_ids, outer_ids, circle)
    first_real = jnp.einsum("rab,ak->rbk", grid_values, outer_cos, precision=highest)
    first_imag = -jnp.einsum("rab,ak->rbk", grid_values, outer_sin, precision=highest)
    turned_real = first_real * twiddle_cos + first_imag * twiddle_sin
    turned_imag = first_imag * twiddle_cos - first_real * twiddle_sin
    coeff_real = jnp.einsum("rbk,bj->rjk", turned_real, inner_cos, precision=highest) + jnp.einsum(
        "rbk,bj->rjk", turned_imag, inner_sin, precision=highest
    )
    coeff_imag = jnp.einsum("rbk,bj->rjk", turned_imag, inner_cos, precision=highest) - jnp.einsum(
        "rbk,bj->rjk", turned_real, inner_sin, precision=highest
    )
    wavenumber = inner_ids[:, None] * outer_count + outer_ids[None, :]
    folded = jnp.minimum(wavenumber, circle - wavenumber)
    keep_mask = folded[None, :, :] <= limits[:, None, None]
    coeff_real = jnp.where(keep_mask, coeff_real, 0.0)
    coeff_imag = jnp.where(keep_mask, coeff_imag, 0.0)
    back_real = jnp.einsum("rjk,jb->rbk", coeff_real, inner_cos, precision=highest) - jnp.einsum(
        "rjk,jb->rbk", coeff_imag, inner_sin, precision=highest
    )
    back_imag = jnp.einsum("rjk,jb->rbk", coeff_imag, inner_cos, precision=highest) + jnp.einsum(
        "rjk,jb->rbk", coeff_real, inner_sin, precision=highest
    )
    reverted_real = back_real * twiddle_cos - back_imag * twiddle_sin
    reverted_imag = back_imag * twiddle_cos + back_real * twiddle_sin
    signal = jnp.einsum("rbk,ka->rab", reverted_real, outer_cos, precision=highest) - jnp.einsum(
        "rbk,ka->rab", reverted_imag, outer_sin, precision=highest
    )
    return (signal / circle).reshape(row_count, circle)


def general_body(tracers, courant, cutoffs):
    levels, tracer_count, lat_rows, lon_cols = tracers.shape
    lon_groups = lax.axis_size("lon")
    lon_index = lax.axis_index("lon")
    lat_bands = lax.axis_size("lat")
    band_index = lax.axis_index("lat")
    grid_rows = lat_rows * lat_bands
    zonal = courant[0]
    meridional = courant[1]
    lat_stack = jnp.concatenate([tracers, meridional[:, None]], axis=1)
    lat_ext = padded(lat_stack, (("lat", 2),), 3, False)
    flat_count = levels * lat_rows
    flat_zonal = zonal.reshape(flat_count, lon_cols)
    edges = jnp.concatenate([tracers[..., :3], tracers[..., lon_cols - 3 :]], axis=-1)
    west_index = (lon_index + lon_groups - 1) % lon_groups
    east_index = (lon_index + 1) % lon_groups
    local_limits = lax.dynamic_slice_in_dim(cutoffs, band_index * lat_rows, lat_rows)
    limits = jnp.tile(local_limits, levels)
    circle = lon_cols * lon_groups
    gathered = lax.all_gather(flat_zonal, "lon", axis=0)
    gathered_edges = lax.all_gather(edges, "lon", axis=0)
    west = lax.dynamic_index_in_dim(gathered_edges, west_index, 0, keepdims=False)[..., 3:]
    east = lax.dynamic_index_in_dim(gathered_edges, east_index, 0, keepdims=False)[..., :3]
    west_raw = lax.dynamic_index_in_dim(gathered, west_index, 0, keepdims=False)[:, -1:]
    raw_ext = jnp.concatenate([west_raw, flat_zonal], axis=1)
    whole_rows = jnp.transpose(gathered, (1, 0, 2)).reshape(flat_count, circle)
    lowpass = spectral_lowpass(whole_rows, limits, lon_groups)
    lowpass = jnp.concatenate([lowpass[:, -1:], lowpass], axis=1)
    lowpass_ext = lax.dynamic_slice_in_dim(lowpass, lon_index * lon_cols, lon_cols + 1, axis=1)
    lon_ext = jnp.concatenate([west, tracers, east], axis=-1)
    filtered_flat = jnp.where((limits < circle // 2)[:, None], lowpass_ext, raw_ext)
    zonal_faces = filtered_flat.reshape(levels, 1, lat_rows, lon_cols + 1)
    filtered_zonal = zonal_faces[:, 0, :, 1:]
    flux_east = ppm_flux(lon_ext, zonal_faces, 3)
    face_weight, cell_weight = metric_weights(band_index * lat_rows, lat_rows, grid_rows)
    flux_north = (
    ppm_flux(lat_ext[:, :tracer_count], lat_ext[:, tracer_count:, 2 : lat_rows + 3, :], 2)
    * face_weight[None, None, :, None]
    )
    change = (
    flux_east[:, :, :, 1:]
    - flux_east[:, :, :, :-1]
    + (flux_north[:, :, 1:, :] - flux_north[:, :, :-1, :]) / cell_weight[None, None, :, None]
    )
    return (tracers - change, filtered_zonal)


MESH = pl.DeviceIdType.MESH
RINGS = 4
LANES = 128
DEPTH = 192
TAIL = 64
TAIL_SENT = 56
EAST, WEST, ACROSS, EAST_TAIL, WEST_TAIL, ACROSS_TAIL, PACK_EAST, PACK_WEST, NORTH, SOUTH, PASS, PASS_TAIL, RESULT = range(13)


def split_halves(values):
    high = values.astype(jnp.bfloat16)
    low = (values - high.astype(jnp.float32)).astype(jnp.bfloat16)
    return high, low


def filter_tables(circle, cols):
    half = circle // 2
    cells = np.arange(circle, dtype=np.int64)
    cos_ids = np.arange(half + 1, dtype=np.int64)
    sin_ids = np.arange(1, half, dtype=np.int64)

    def waves(ids):
        return np.concatenate(
            [
                np.cos(2.0 * np.pi * ((cos_ids[:, None] * ids[None, :]) % circle) / circle),
                np.sin(2.0 * np.pi * ((sin_ids[:, None] * ids[None, :]) % circle) / circle),
            ],
            axis=0,
        )

    def halves(table):
        high = table.astype(jnp.bfloat16)
        low = (table - high.astype(np.float64)).astype(jnp.bfloat16)
        return high, low

    forward = np.zeros((circle // cols, circle, DEPTH))
    forward[:, :, :cols] = waves(cells).reshape(circle, circle // cols, cols).transpose(1, 0, 2)
    wavenumber = np.concatenate([cos_ids, sin_ids])
    scale = np.where((wavenumber == 0) | (wavenumber == half), 1.0, 2.0) / circle
    inverse = np.zeros((3, DEPTH, circle))
    for index, start in enumerate((0, -cols, cols)):
        inverse[index, :cols] = waves(start + np.arange(cols)).T * scale
        inverse[index, DEPTH - 1] = waves(np.array([start - 1]))[:, 0] * scale
    return halves(forward) + halves(inverse)


def weight_tables(bands, rows, cols):
    grid_rows = bands * rows
    faces = np.arange(bands)[:, None] * rows + np.arange(-8, rows)[None, :]
    cells = np.arange(bands)[:, None] * rows + np.arange(rows)[None, :]
    face = np.sin(np.minimum(faces + 1, grid_rows - 1 - faces) * (np.pi / grid_rows))
    cell = 1.0 / np.sin((np.minimum(cells, grid_rows - 1 - cells) + 0.5) * (np.pi / grid_rows))
    face = np.broadcast_to(face[:, :, None], face.shape + (cols,))
    cell = np.broadcast_to(cell[:, :, None], cell.shape + (cols,))
    return face.astype(np.float32), cell.astype(np.float32)


def flux_factors(courant, scale):
    size = jnp.abs(courant)
    steep = size - size * size
    middle = 3.0 * size - 2.0 * size * size
    scaled = courant * scale
    return (
        scaled * (1.0 + steep - middle) * (1.0 / 12.0),
        scaled * steep * (-1.0 / 12.0),
        scaled * middle,
    )


def gather_kernel(
    sizes,
    tracers, courant, cutoffs, ahead_hi, ahead_lo, back_hi, back_lo, face_w, cell_w,
    faces, here_out, next_out, edge_out, face_out, beyond_out, rest,
    zonal, cells, merid, heads, tails, own, total, table_hi, table_lo, inv_hi, inv_lo, far_hi, far_lo, result_out, result_in, limit_v, face_v, cell_v,
    pack, packs, sides, near, border, turned,
    load_sem, send_sem, recv_sem, ready, beside_in, beside_ok,
):
    levels, count, rows, cols, bands, polar_bands, circle = sizes
    flat = levels * rows
    z = lax.axis_index("lon")
    band = lax.axis_index("lat")
    polar = (band < polar_bands) | (band >= bands - polar_bands)
    has_south = band > 0
    has_north = band < bands - 1
    tail = cols - LANES
    barrier = pltpu.get_barrier_semaphore()

    def load(index, source, target):
        return pltpu.make_async_copy(source, target, load_sem.at[index])

    load_zonal = load(0, courant.at[0], zonal)
    load_cells = load(1, tracers, cells.at[:, :, pl.ds(8, rows), :])
    load_merid = load(2, courant.at[1], merid.at[:, pl.ds(8, rows), :])
    load_limit = load(3, cutoffs, limit_v)
    load_face = load(4, face_w.at[band], face_v)
    load_cell = load(5, cell_w.at[band], cell_v)
    load_tables = [
        load(6, ahead_hi, table_hi),
        load(7, ahead_lo, table_lo),
        load(8, back_hi.at[0], inv_hi),
        load(9, back_lo.at[0], inv_lo),
    ]
    load_far = [load(10, back_hi.at[z], far_hi), load(11, back_lo.at[z], far_lo)]
    load_zonal.start()
    load_cells.start()
    for other in range(1, RINGS):
        @pl.when(z < other)
        def _():
            pl.semaphore_signal(barrier, inc=1, device_id={"lon": other}, device_id_type=MESH)

    near_ring = z == 0

    @pl.when(near_ring & has_south)
    def _():
        pl.semaphore_signal(barrier, inc=1, device_id={"lat": band - 1}, device_id_type=MESH)

    @pl.when(near_ring & has_north)
    def _():
        pl.semaphore_signal(barrier, inc=1, device_id={"lat": band + 1}, device_id_type=MESH)

    beside = has_south.astype(jnp.int32) + has_north.astype(jnp.int32)
    pl.semaphore_wait(barrier, z + jnp.where(near_ring, beside, 0))
    def remote(index, source, target, where, send_index=None):
        return pltpu.make_async_remote_copy(
            src_ref=source,
            dst_ref=target,
            send_sem=send_sem.at[index if send_index is None else send_index],
            recv_sem=recv_sem.at[index],
            device_id=where,
            device_id_type=MESH,
        )

    east = lax.rem(z + 1, RINGS)
    west = lax.rem(z + 3, RINGS)
    across = lax.rem(z + 2, RINGS)
    head = courant.at[0, :, :, pl.ds(0, LANES)]
    tail_rows = pl.ds(0, TAIL_SENT)
    own_tail = tails.at[0, tail_rows]

    class Pair:
        def __init__(self, first, second, sources, slot, where, sends=(None, None)):
            self.head = remote(first, sources[0], heads.at[slot], {"lon": where}, sends[0])
            self.tail = remote(second, sources[1], tails.at[slot, tail_rows], {"lon": where}, sends[1])

        def start(self):
            self.head.start()
            self.tail.start()

        def wait_recv(self):
            self.head.wait_recv()
            self.tail.wait_recv()

        def wait_send(self):
            self.head.wait_send()
            self.tail.wait_send()

    mine = (head, own_tail)
    send_east = Pair(EAST, EAST_TAIL, mine, 3, east)
    send_west = Pair(WEST, WEST_TAIL, mine, 1, west)
    send_across = Pair(ACROSS, ACROSS_TAIL, mine, 2, across)
    pass_west = Pair(ACROSS, ACROSS_TAIL, (heads.at[1], tails.at[1, tail_rows]), 2, west)
    pass_east = Pair(
        ACROSS, ACROSS_TAIL, (heads.at[3], tails.at[3, tail_rows]), 2, east, (PASS, PASS_TAIL)
    )
    pack_east = remote(PACK_EAST, pack.at[0], packs.at[0], {"lon": east})
    pack_west = remote(PACK_WEST, pack.at[1], packs.at[1], {"lon": west})
    send_north = remote(NORTH, sides.at[0], near.at[0], {"lat": band + 1})
    send_south = remote(SOUTH, sides.at[1], near.at[1], {"lat": band - 1})
    second_core = lax.rem(band, 2) == 1
    full = polar & jnp.logical_not(second_core)
    shared = polar & second_core
    middle = (z == 1) | (z == 2)
    gathers = full | (shared & middle)
    helps = shared & middle
    helped = shared & jnp.logical_not(middle)
    early = (
        (send_west, (full & middle) | (shared & (z == 2))),
        (send_east, full & (z == 3)),
        (send_west, shared & (z == 3)),
    )

    for copy, chosen in early:
        @pl.when(chosen)
        def _():
            copy.head.start()

    load_merid.start()
    for other in range(RINGS - 1):
        @pl.when(z > other)
        def _():
            pl.semaphore_signal(ready.at[z], inc=1, device_id={"lon": other}, device_id_type=MESH)

    tails[0, TAIL_SENT - 8 :] = jnp.zeros((TAIL - TAIL_SENT + 8, LANES), jnp.float32)
    load_zonal.wait()
    tails[0, :tail] = zonal[:, :, LANES:].reshape(flat, tail).T
    for copy, chosen in early:
        @pl.when(chosen)
        def _():
            copy.tail.start()

    load_cells.wait()
    tail_lane = lax.broadcasted_iota(jnp.int32, (flat, tail), 1)
    for t in range(count):
        ends = jnp.where(
            tail_lane < tail - 3,
            cells[:, t, 8 : rows + 8, :tail].reshape(flat, tail),
            cells[:, t, 8 : rows + 8, LANES:].reshape(flat, tail),
        ).T
        pack[0, t, 0:3] = ends[tail - 3 :]
        pack[1, t, 0:3] = ends[0:3]
    pack[0, count, 0:1] = tails[0, tail - 1 : tail]

    @pl.when(east < z)
    def _():
        pack_east.start()

    @pl.when(west < z)
    def _():
        pack_west.start()

    @pl.when(shared & (z == 3))
    def _():
        send_across.start()

    load_face.start()
    load_cell.start()

    @pl.when(polar)
    def _():
        load_limit.start()

    @pl.when(gathers)
    def _():
        for copy in load_tables:
            copy.start()

    @pl.when(helps)
    def _():
        for copy in load_far:
            copy.start()

    own[:LANES] = zonal[:, :, :LANES].reshape(flat, LANES).T
    own[LANES:] = tails[0]
    load_merid.wait()
    planes = [(level, t) for level in range(levels) for t in range(count)]
    for k, (level, t) in enumerate(planes):
        sides[0, 3 * k : 3 * k + 3, :cols] = cells[level, t, rows + 5 : rows + 8]
        sides[1, 3 * k : 3 * k + 3, :cols] = cells[level, t, 8:11]
    first_speed = 3 * len(planes)
    for level in range(levels):
        sides[0, first_speed + level, :cols] = merid[level, rows + 7]

    def send_sides(chosen):
        @pl.when(chosen & has_north)
        def _():
            send_north.start()

        @pl.when(chosen & has_south)
        def _():
            send_south.start()

    send_sides(near_ring)
    for slot in range(1, RINGS):
        tails[slot, TAIL_SENT:] = jnp.zeros((TAIL - TAIL_SENT, LANES), jnp.float32)
    border[...] = jnp.zeros_like(border)
    for t in range(count):
        here_out[:, t, :, :LANES] = cells[:, t, 8 : rows + 8, :LANES]
        here_out[:, t, :, LANES:cols] = cells[:, t, 8 : rows + 8, LANES:]
    turned[LANES:, :] = jnp.zeros((LANES, LANES), jnp.float32)

    def signal_beside(semaphore):
        @pl.when(has_south)
        def _():
            pl.semaphore_signal(semaphore, inc=1, device_id={"lat": band - 1}, device_id_type=MESH)

        @pl.when(has_north)
        def _():
            pl.semaphore_signal(semaphore, inc=1, device_id={"lat": band + 1}, device_id_type=MESH)

    def greet(other):
        @pl.when(z < other)
        def _():
            pl.semaphore_wait(ready.at[other], 1)
            for copy, where in ((pack_east, east), (pack_west, west)):
                @pl.when(where == other)
                def _():
                    copy.start()
            for copy, chosen in (
                (send_east, (east == other) & (full | (shared & (z < 2)))),
                (send_west, (west == other) & full),
                (send_across, (across == other) & shared & (z == 0)),
            ):
                @pl.when(chosen)
                def _():
                    copy.start()

    def announce(others):
        for other in others:
            signal_beside(beside_in.at[other])

    def vouch(others):
        for other in others:
            pl.semaphore_wait(beside_in.at[other], beside)
            pl.semaphore_signal(beside_ok, inc=1, device_id={"lon": other}, device_id_type=MESH)

    def block(slot):
        return jnp.concatenate([heads[slot].reshape(flat, LANES).T, tails[slot]], axis=0)

    def forward(slot, values):
        high, low = split_halves(values)
        both = jnp.dot(
            table_hi[slot], jnp.concatenate([high, low], axis=1), preferred_element_type=jnp.float32
        )
        rest_term = jnp.dot(table_lo[slot], high, preferred_element_type=jnp.float32)
        return both[:, :LANES] + (both[:, LANES:] + rest_term)

    greet(1)

    @pl.when(z == 0)
    def _():
        announce((1,))
        vouch((1,))


    @pl.when(full & (z == 3))
    def _():
        send_across.start()
        send_west.start()

    greet(2)

    greet(3)

    @pl.when(z == 1)
    def _():
        pl.semaphore_wait(beside_ok, 1)

    send_sides(z == 1)

    @pl.when(z == 1)
    def _():
        announce((2, 3))

    @pl.when(shared & (z == 1))
    def _():
        send_west.wait_recv()

    @pl.when(full & (z == 1))
    def _():
        send_west.head.wait_recv()
        pass_west.head.start()
        send_west.tail.wait_recv()
        pass_west.tail.start()

    @pl.when(z == 1)
    def _():
        vouch((2, 3))

    @pl.when(polar)
    def _():
        load_limit.wait()

    @pl.when(gathers)
    def _():
        for copy in load_tables:
            copy.wait()
        total[...] = forward(0, own[...])

    @pl.when(helps)
    def _():
        for copy in load_far:
            copy.wait()

    @pl.when(z >= 2)
    def _():
        pl.semaphore_wait(beside_ok, 1)

    send_sides(z >= 2)

    @pl.when(shared & (z == 1))
    def _():
        send_east.wait_recv()

    @pl.when(full & (z == 1))
    def _():
        send_east.head.wait_recv()
        pass_east.head.start()
        send_east.tail.wait_recv()
        pass_east.tail.start()

    @pl.when(shared & (z == 2))
    def _():
        send_east.wait_recv()

    def kept_limit():
        lane = lax.broadcasted_iota(jnp.int32, (8, 2 * LANES), 1)
        spread = jnp.broadcast_to(limit_v[...].reshape(1, bands * rows), (8, bands * rows))
        spread = pltpu.roll(spread, lax.rem((bands - band) * rows, bands * rows), 1)
        limit = jnp.where(lane < rows, spread, 0)
        copies = 1
        while copies < levels:
            limit = limit + pltpu.roll(limit, copies * rows, 1)
            copies *= 2
        return limit[0:1, :LANES]

    send_result = remote(RESULT, result_out, result_in, {"lon": jnp.where(z == 1, 0, RINGS - 1)})

    def wait_second():
        @pl.when(z == 0)
        def _():
            send_east.wait_recv()

        @pl.when(z >= 2)
        def _():
            send_west.wait_recv()

    def last_coefficients(limit):
        wave = lax.broadcasted_iota(jnp.int32, (circle, LANES), 0)
        wave = jnp.where(wave <= circle // 2, wave, wave - circle // 2)
        send_across.wait_recv()
        return jnp.where(wave <= limit, total[...] + forward(2, block(2)), 0.0)

    def inverse(coeff, hi_ref, lo_ref):
        high, low = split_halves(coeff)
        both = jnp.dot(
            hi_ref[...], jnp.concatenate([high, low], axis=1), preferred_element_type=jnp.float32
        )
        rest_term = jnp.dot(lo_ref[...], high, preferred_element_type=jnp.float32)
        return both[:, :LANES] + (both[:, LANES:] + rest_term)

    @pl.when(helps)
    def _():
        limit = kept_limit()
        total[...] += forward(3, block(3))
        wait_second()
        total[...] += forward(1, block(1))
        coeff = last_coefficients(limit)
        result_out[...] = inverse(coeff, far_hi, far_lo)
        send_result.start()
        result_in[...] = inverse(coeff, inv_hi, inv_lo)

    def meridional():
        load_face.wait()
        load_cell.wait()

        @pl.when(has_south)
        def _():
            send_north.wait_recv()
            for k, (level, t) in enumerate(planes):
                cells[level, t, 5:8] = near[0, 3 * k : 3 * k + 3, :cols]
            for level in range(levels):
                merid[level, 7] = near[0, first_speed + level, :cols]

        @pl.when(has_north)
        def _():
            send_south.wait_recv()
            for k, (level, t) in enumerate(planes):
                cells[level, t, rows + 8 : rows + 11] = near[1, 3 * k : 3 * k + 3, :cols]

        @pl.when(jnp.logical_not(has_south))
        def _():
            cells[:, :, 0:8, :] = jnp.zeros((levels, count, 8, cols), jnp.float32)
            merid[:, 0:8, :] = jnp.zeros((levels, 8, cols), jnp.float32)

        @pl.when(jnp.logical_not(has_north))
        def _():
            cells[:, :, rows + 8 :, :] = jnp.zeros((levels, count, 8, cols), jnp.float32)

        for level in range(levels):
            speed = merid[level, 7 : rows + 8]
            by_face, by_edge, by_cell = flux_factors(speed, face_v[7 : rows + 8])
            upward = speed > 0
            inverse_cell = cell_v[...]
            for t in range(count):
                def shifted(offset):
                    return cells[level, t, 7 + offset : 8 + offset + rows, :]

                below, here, above, beyond = shifted(-1), shifted(0), shifted(1), shifted(2)
                edge_here = 7.0 * (below + here) - (shifted(-2) + above)
                edge_face = 7.0 * (here + above) - (below + beyond)
                edge_next = 7.0 * (above + beyond) - (here + shifted(3))
                flux = (
                    by_face * edge_face
                    + by_edge * jnp.where(upward, edge_here, edge_next)
                    + by_cell * jnp.where(upward, here, above)
                )
                change = (flux[1:] - flux[:-1]) * inverse_cell
                rest[level, t] = cells[level, t, 8 : rows + 8, :] - change

    @pl.when((z < 2) | shared)
    def _():
        meridional()

    @pl.when(full & (z == 2))
    def _():
        send_east.head.wait_recv()
        pass_east.head.start()
        send_east.tail.wait_recv()
        pass_east.tail.start()

    @pl.when(full)
    def _():
        @pl.when(z == 0)
        def _():
            send_west.wait_recv()

        @pl.when(z == 3)
        def _():
            send_east.wait_recv()

        slot = jnp.where(z == 0, 1, 3)
        total[...] += forward(slot, block(slot))

    wide_lane = lax.broadcasted_iota(jnp.int32, (levels, rows, LANES), 2)
    pack_east.wait_recv()
    pack_west.wait_recv()
    for t in range(count):
        border[t, tail : tail + 3] = packs[1, t, 0:3]
        border[t, LANES - 3 : LANES] = packs[0, t, 0:3]
        halo = border[t].T.reshape(levels, rows, LANES)
        here_out[:, t, :, LANES:] = jnp.where(wide_lane < tail, here_out[:, t, :, LANES:], halo)

    for level in range(levels):
        here = here_out[level]

        def moved(offset):
            return pltpu.roll(here, (-offset) % (2 * LANES), 2)

        back_two, back_one, ahead_one, ahead_two = moved(-2), moved(-1), moved(1), moved(2)
        next_out[level] = ahead_one
        edge_out[level] = 7.0 * (back_one + here) - (back_two + ahead_one)
        face_out[level] = 7.0 * (here + ahead_one) - (back_one + ahead_two)
        beyond_out[level] = 7.0 * (ahead_one + ahead_two) - (here + moved(3))

    def finish(body_rows, west_row):
        turned[:cols] = body_rows
        turned[2 * LANES - 8 :] = jnp.broadcast_to(west_row, (8, LANES))

    @pl.when(jnp.logical_not(polar))
    def _():
        finish(own[:cols], packs[0, count, 0:1])

    def finish_smooth(smooth, limit):
        kept = limit < circle // 2
        finish(
            jnp.where(kept, smooth[:cols], own[:cols]),
            jnp.where(kept, smooth[DEPTH - 1 :], packs[0, count, 0:1]),
        )

    @pl.when(full)
    def _():
        limit = kept_limit()
        wait_second()
        slot = jnp.where(z == 0, 3, 1)
        total[...] += forward(slot, block(slot))
        coeff = last_coefficients(limit)
        finish_smooth(inverse(coeff, inv_hi, inv_lo), limit)

    @pl.when(shared)
    def _():
        limit = kept_limit()

        @pl.when(jnp.logical_not(middle))
        def _():
            send_result.wait_recv()

        finish_smooth(result_in[...], limit)

    faces[:, :, :LANES] = turned[:LANES].T.reshape(levels, rows, LANES)
    faces[:, :, LANES:] = turned[LANES:].T.reshape(levels, rows, LANES)

    @pl.when((z >= 2) & jnp.logical_not(shared))
    def _():
        meridional()

    pack_east.wait_send()
    pack_west.wait_send()

    for copy, chosen in (
        (send_east, full | (shared & (z < 2))),
        (send_west, full | (shared & (z >= 2))),
        (send_across, (polar & (z == 3)) | (shared & (z == 0))),
        (pass_west, full & (z == 1)),
        (pass_east, full & middle),
        (send_result, helps),
    ):
        @pl.when(chosen)
        def _():
            copy.wait_send()

    @pl.when(has_north)
    def _():
        send_north.wait_send()

    @pl.when(has_south)
    def _():
        send_south.wait_send()


def flux_kernel(
    faces, here, following, edge, face_edge, beyond, rest, updated, filtered, result, smooth, sem
):
    levels, _, _, cols = rest.shape
    smooth[...] = faces[:, :, :cols]
    store = pltpu.make_async_copy(smooth, filtered, sem.at[levels])
    store.start()
    for level in range(levels):
        speed = faces[level]
        by_face, by_edge, by_cell = flux_factors(speed, 1.0)
        eastward = speed > 0
        flux = (
            by_face[None] * face_edge[level]
            + by_edge[None] * jnp.where(eastward[None], edge[level], beyond[level])
            + by_cell[None] * jnp.where(eastward[None], here[level], following[level])
        )
        change = flux - pltpu.roll(flux, 1, 2)
        result[level] = rest[level] - change[:, :, :cols]
        pltpu.make_async_copy(result.at[level], updated.at[level], sem.at[level]).start()
    for level in range(levels):
        pltpu.make_async_copy(result.at[level], updated.at[level], sem.at[level]).wait()
    store.wait()


def ring_body(bands, tracers, courant, cutoffs):
    levels, count, rows, cols = tracers.shape
    circle = cols * RINGS
    sizes = (levels, count, rows, cols, bands, bands // 4, circle)
    ahead_hi, ahead_lo, back_hi, back_lo = filter_tables(circle, cols)
    face_w, cell_w = weight_tables(bands, rows, cols)
    hbm = pl.BlockSpec(memory_space=pltpu.HBM)
    vmem = pl.BlockSpec(memory_space=pltpu.VMEM)
    f32, half = jnp.float32, jnp.bfloat16
    slab = (levels, count, rows)
    strip = -(-(3 * levels * count + levels) // 8) * 8
    wide = jax.ShapeDtypeStruct(slab + (2 * LANES,), f32)
    parts = pl.pallas_call(
        functools.partial(gather_kernel, sizes),
        out_shape=(jax.ShapeDtypeStruct((levels, rows, 2 * LANES), f32),)
        + (wide,) * 5
        + (jax.ShapeDtypeStruct(tracers.shape, f32),),
        in_specs=[hbm] * 9,
        out_specs=(vmem,) * 7,
        scratch_shapes=[
            pltpu.VMEM((levels, rows, cols), f32),
            pltpu.VMEM((levels, count, rows + 16, cols), f32),
            pltpu.VMEM((levels, rows + 8, cols), f32),
            pltpu.VMEM((RINGS, levels, rows, LANES), f32),
            pltpu.VMEM((RINGS, TAIL, LANES), f32),
            pltpu.VMEM((DEPTH, LANES), f32),
            pltpu.VMEM((circle, LANES), f32),
            pltpu.VMEM((RINGS, circle, DEPTH), half),
            pltpu.VMEM((RINGS, circle, DEPTH), half),
            pltpu.VMEM((DEPTH, circle), half),
            pltpu.VMEM((DEPTH, circle), half),
            pltpu.VMEM((DEPTH, circle), half),
            pltpu.VMEM((DEPTH, circle), half),
            pltpu.VMEM((DEPTH, LANES), f32),
            pltpu.VMEM((DEPTH, LANES), f32),
            pltpu.VMEM((bands * rows,), jnp.int32),
            pltpu.VMEM((rows + 8, cols), f32),
            pltpu.VMEM((rows, cols), f32),
            pltpu.VMEM((2, count + 1, 8, LANES), f32),
            pltpu.VMEM((2, count + 1, 8, LANES), f32),
            pltpu.VMEM((2, strip, 2 * LANES), f32),
            pltpu.VMEM((2, strip, 2 * LANES), f32),
            pltpu.VMEM((count, LANES, LANES), f32),
            pltpu.VMEM((2 * LANES, LANES), f32),
            pltpu.SemaphoreType.DMA((12,)),
            pltpu.SemaphoreType.DMA((13,)),
            pltpu.SemaphoreType.DMA((13,)),
            pltpu.SemaphoreType.REGULAR((RINGS,)),
            pltpu.SemaphoreType.REGULAR((RINGS,)),
            pltpu.SemaphoreType.REGULAR,
        ],
        compiler_params=pltpu.CompilerParams(
            collective_id=0, has_side_effects=True, vmem_limit_bytes=24 * 2**20
        ),
    )(
        *(
            pltpu.with_memory_space_constraint(jnp.asarray(operand), pltpu.HBM)
            for operand in (
                tracers, courant, cutoffs, ahead_hi, ahead_lo, back_hi, back_lo, face_w, cell_w
            )
        )
    )
    return pl.pallas_call(
        flux_kernel,
        out_shape=(
            jax.ShapeDtypeStruct(tracers.shape, f32),
            jax.ShapeDtypeStruct((levels, rows, cols), f32),
        ),
        in_specs=[vmem] * 7,
        out_specs=(hbm, hbm),
        scratch_shapes=[
            pltpu.VMEM(tracers.shape, f32),
            pltpu.VMEM((levels, rows, cols), f32),
            pltpu.SemaphoreType.DMA((levels + 1,)),
        ],
        compiler_params=pltpu.CompilerParams(vmem_limit_bytes=16 * 2**20),
    )(*parts)


def body(bands, tracers, courant, cutoffs):
    levels, _, rows, cols = tracers.shape
    fits = (
        lax.axis_size("lon") == RINGS
        and bands % 4 == 0
        and bands * rows == 2 * LANES
        and levels * rows == LANES
        and LANES < cols <= LANES + TAIL_SENT - 4
        and bands % 8 == 0
        and cols % 4 == 0
    )
    if fits:
        return ring_body(bands, tracers, courant, cutoffs)
    return general_body(tracers, courant, cutoffs)


def solution(mesh):
    in_specs = (P(None, None, "lat", "lon"), P(None, None, "lat", "lon"), P())
    out_specs = (P(None, None, "lat", "lon"), P(None, "lat", "lon"))
    return jax.shard_map(
        functools.partial(body, mesh.shape["lat"]),
        mesh=mesh,
        in_specs=in_specs,
        out_specs=out_specs,
        check_vma=False,
    )
```

```python
import functools
import math

import jax
import numpy as np
import jax.numpy as jnp
from jax import lax
from jax.experimental import pallas as pl
from jax.experimental.pallas import tpu as pltpu
from jax.sharding import PartitionSpec as P


def padded(cells, sides, width, closed):
    for axis, dim in sides:
        count = lax.axis_size(axis)
        ends = count if closed else count - 1
        head = lax.slice_in_dim(cells, 0, width, axis=dim)
        tail = lax.slice_in_dim(cells, cells.shape[dim] - width, cells.shape[dim], axis=dim)
        cells = jnp.concatenate(
            [
                lax.ppermute(tail, axis, [(i, (i + 1) % count) for i in range(ends)]),
                cells,
                lax.ppermute(head, axis, [((i + 1) % count, i) for i in range(ends)]),
            ],
            axis=dim,
        )
    return cells


def take_range(values, start, count, axis_index):
    return lax.slice_in_dim(values, start, start + count, axis=axis_index)


def ppm_flux(extended, courant_faces, axis_index):
    cell_count = extended.shape[axis_index] - 6
    edge_values = 7.0 / 12.0 * (
        take_range(extended, 1, cell_count + 3, axis_index)
        + take_range(extended, 2, cell_count + 3, axis_index)
    ) - 1.0 / 12.0 * (
        take_range(extended, 0, cell_count + 3, axis_index)
        + take_range(extended, 3, cell_count + 3, axis_index)
    )
    left_edge = take_range(edge_values, 0, cell_count + 2, axis_index)
    right_edge = take_range(edge_values, 1, cell_count + 2, axis_index)
    centre = take_range(extended, 2, cell_count + 2, axis_index)
    slopes = right_edge - left_edge
    curvature = 6.0 * centre - 3.0 * (left_edge + right_edge)
    upwind = take_range(right_edge, 0, cell_count + 1, axis_index) - 0.5 * courant_faces * (
        take_range(slopes, 0, cell_count + 1, axis_index)
        - (1.0 - courant_faces * (2.0 / 3.0)) * take_range(curvature, 0, cell_count + 1, axis_index)
    )
    downwind = take_range(left_edge, 1, cell_count + 1, axis_index) - 0.5 * courant_faces * (
        take_range(slopes, 1, cell_count + 1, axis_index)
        + (1.0 + courant_faces * (2.0 / 3.0)) * take_range(curvature, 1, cell_count + 1, axis_index)
    )
    return courant_faces * jnp.where(courant_faces > 0, upwind, downwind)


def metric_weights(first_row, row_count, grid_rows):
    faces = first_row + jnp.arange(-1, row_count, dtype=jnp.int32)
    centres = first_row + jnp.arange(row_count, dtype=jnp.int32)
    face_weight = jnp.sin(
        jnp.minimum(faces + 1, grid_rows - 1 - faces).astype(jnp.float32) * (math.pi / grid_rows)
    )
    cell_weight = jnp.sin(
        (jnp.minimum(centres, grid_rows - 1 - centres).astype(jnp.float32) + 0.5)
        * (math.pi / grid_rows)
    )
    return (face_weight, cell_weight)


def angle_table(first_ids, second_ids, period):
    product = first_ids[:, None] * second_ids[None, :] % period
    angles = product.astype(jnp.float32) * (2.0 * math.pi / period)
    return (jnp.cos(angles), jnp.sin(angles))


def spectral_lowpass(row_block, limits, outer_count):
    row_count, circle = row_block.shape
    inner_count = circle // outer_count
    highest = lax.Precision.HIGHEST
    grid_values = row_block.reshape(row_count, outer_count, inner_count)
    outer_ids = jnp.arange(outer_count, dtype=jnp.int32)
    inner_ids = jnp.arange(inner_count, dtype=jnp.int32)
    outer_cos, outer_sin = angle_table(outer_ids, outer_ids, outer_count)
    inner_cos, inner_sin = angle_table(inner_ids, inner_ids, inner_count)
    twiddle_cos, twiddle_sin = angle_table(inner_ids, outer_ids, circle)
    first_real = jnp.einsum("rab,ak->rbk", grid_values, outer_cos, precision=highest)
    first_imag = -jnp.einsum("rab,ak->rbk", grid_values, outer_sin, precision=highest)
    turned_real = first_real * twiddle_cos + first_imag * twiddle_sin
    turned_imag = first_imag * twiddle_cos - first_real * twiddle_sin
    coeff_real = jnp.einsum("rbk,bj->rjk", turned_real, inner_cos, precision=highest) + jnp.einsum(
        "rbk,bj->rjk", turned_imag, inner_sin, precision=highest
    )
    coeff_imag = jnp.einsum("rbk,bj->rjk", turned_imag, inner_cos, precision=highest) - jnp.einsum(
        "rbk,bj->rjk", turned_real, inner_sin, precision=highest
    )
    wavenumber = inner_ids[:, None] * outer_count + outer_ids[None, :]
    folded = jnp.minimum(wavenumber, circle - wavenumber)
    keep_mask = folded[None, :, :] <= limits[:, None, None]
    coeff_real = jnp.where(keep_mask, coeff_real, 0.0)
    coeff_imag = jnp.where(keep_mask, coeff_imag, 0.0)
    back_real = jnp.einsum("rjk,jb->rbk", coeff_real, inner_cos, precision=highest) - jnp.einsum(
        "rjk,jb->rbk", coeff_imag, inner_sin, precision=highest
    )
    back_imag = jnp.einsum("rjk,jb->rbk", coeff_imag, inner_cos, precision=highest) + jnp.einsum(
        "rjk,jb->rbk", coeff_real, inner_sin, precision=highest
    )
    reverted_real = back_real * twiddle_cos - back_imag * twiddle_sin
    reverted_imag = back_imag * twiddle_cos + back_real * twiddle_sin
    signal = jnp.einsum("rbk,ka->rab", reverted_real, outer_cos, precision=highest) - jnp.einsum(
        "rbk,ka->rab", reverted_imag, outer_sin, precision=highest
    )
    return (signal / circle).reshape(row_count, circle)


def general_body(tracers, courant, cutoffs):
    levels, tracer_count, lat_rows, lon_cols = tracers.shape
    lon_groups = lax.axis_size("lon")
    lon_index = lax.axis_index("lon")
    lat_bands = lax.axis_size("lat")
    band_index = lax.axis_index("lat")
    grid_rows = lat_rows * lat_bands
    zonal = courant[0]
    meridional = courant[1]
    lat_stack = jnp.concatenate([tracers, meridional[:, None]], axis=1)
    lat_ext = padded(lat_stack, (("lat", 2),), 3, False)
    flat_count = levels * lat_rows
    flat_zonal = zonal.reshape(flat_count, lon_cols)
    edges = jnp.concatenate([tracers[..., :3], tracers[..., lon_cols - 3 :]], axis=-1)
    west_index = (lon_index + lon_groups - 1) % lon_groups
    east_index = (lon_index + 1) % lon_groups
    local_limits = lax.dynamic_slice_in_dim(cutoffs, band_index * lat_rows, lat_rows)
    limits = jnp.tile(local_limits, levels)
    circle = lon_cols * lon_groups
    gathered = lax.all_gather(flat_zonal, "lon", axis=0)
    gathered_edges = lax.all_gather(edges, "lon", axis=0)
    west = lax.dynamic_index_in_dim(gathered_edges, west_index, 0, keepdims=False)[..., 3:]
    east = lax.dynamic_index_in_dim(gathered_edges, east_index, 0, keepdims=False)[..., :3]
    west_raw = lax.dynamic_index_in_dim(gathered, west_index, 0, keepdims=False)[:, -1:]
    raw_ext = jnp.concatenate([west_raw, flat_zonal], axis=1)
    whole_rows = jnp.transpose(gathered, (1, 0, 2)).reshape(flat_count, circle)
    lowpass = spectral_lowpass(whole_rows, limits, lon_groups)
    lowpass = jnp.concatenate([lowpass[:, -1:], lowpass], axis=1)
    lowpass_ext = lax.dynamic_slice_in_dim(lowpass, lon_index * lon_cols, lon_cols + 1, axis=1)
    lon_ext = jnp.concatenate([west, tracers, east], axis=-1)
    filtered_flat = jnp.where((limits < circle // 2)[:, None], lowpass_ext, raw_ext)
    zonal_faces = filtered_flat.reshape(levels, 1, lat_rows, lon_cols + 1)
    filtered_zonal = zonal_faces[:, 0, :, 1:]
    flux_east = ppm_flux(lon_ext, zonal_faces, 3)
    face_weight, cell_weight = metric_weights(band_index * lat_rows, lat_rows, grid_rows)
    flux_north = (
    ppm_flux(lat_ext[:, :tracer_count], lat_ext[:, tracer_count:, 2 : lat_rows + 3, :], 2)
    * face_weight[None, None, :, None]
    )
    change = (
    flux_east[:, :, :, 1:]
    - flux_east[:, :, :, :-1]
    + (flux_north[:, :, 1:, :] - flux_north[:, :, :-1, :]) / cell_weight[None, None, :, None]
    )
    return (tracers - change, filtered_zonal)


MESH = pl.DeviceIdType.MESH
RINGS = 4
LANES = 128
DEPTH = 192
TAIL = 64
TAIL_SENT = 56
EAST, WEST, ACROSS, EAST_TAIL, WEST_TAIL, ACROSS_TAIL, PACK_EAST, PACK_WEST, NORTH, SOUTH, PASS, PASS_TAIL, RESULT = range(13)


def split_halves(values):
    high = values.astype(jnp.bfloat16)
    low = (values - high.astype(jnp.float32)).astype(jnp.bfloat16)
    return high, low


def filter_tables(circle, cols):
    half = circle // 2
    cells = np.arange(circle, dtype=np.int64)
    cos_ids = np.arange(half + 1, dtype=np.int64)
    sin_ids = np.arange(1, half, dtype=np.int64)

    def waves(ids):
        return np.concatenate(
            [
                np.cos(2.0 * np.pi * ((cos_ids[:, None] * ids[None, :]) % circle) / circle),
                np.sin(2.0 * np.pi * ((sin_ids[:, None] * ids[None, :]) % circle) / circle),
            ],
            axis=0,
        )

    def halves(table):
        high = table.astype(jnp.bfloat16)
        low = (table - high.astype(np.float64)).astype(jnp.bfloat16)
        return high, low

    forward = np.zeros((circle // cols, circle, DEPTH))
    forward[:, :, :cols] = waves(cells).reshape(circle, circle // cols, cols).transpose(1, 0, 2)
    wavenumber = np.concatenate([cos_ids, sin_ids])
    scale = np.where((wavenumber == 0) | (wavenumber == half), 1.0, 2.0) / circle
    inverse = np.zeros((3, DEPTH, circle))
    for index, start in enumerate((0, -cols, cols)):
        inverse[index, :cols] = waves(start + np.arange(cols)).T * scale
        inverse[index, DEPTH - 1] = waves(np.array([start - 1]))[:, 0] * scale
    return halves(forward) + halves(inverse)


def weight_tables(bands, rows, cols):
    grid_rows = bands * rows
    faces = np.arange(bands)[:, None] * rows + np.arange(-8, rows)[None, :]
    cells = np.arange(bands)[:, None] * rows + np.arange(rows)[None, :]
    face = np.sin(np.minimum(faces + 1, grid_rows - 1 - faces) * (np.pi / grid_rows))
    cell = 1.0 / np.sin((np.minimum(cells, grid_rows - 1 - cells) + 0.5) * (np.pi / grid_rows))
    face = np.broadcast_to(face[:, :, None], face.shape + (cols,))
    cell = np.broadcast_to(cell[:, :, None], cell.shape + (cols,))
    return face.astype(np.float32), cell.astype(np.float32)


def flux_factors(courant, scale):
    size = jnp.abs(courant)
    steep = size - size * size
    middle = 3.0 * size - 2.0 * size * size
    scaled = courant * scale
    return (
        scaled * (1.0 + steep - middle) * (1.0 / 12.0),
        scaled * steep * (-1.0 / 12.0),
        scaled * middle,
    )


def gather_kernel(
    sizes,
    tracers, courant, cutoffs, ahead_hi, ahead_lo, back_hi, back_lo, face_w, cell_w,
    faces, here_out, next_out, edge_out, face_out, beyond_out, rest,
    zonal, cells, merid, heads, tails, own, total, table_hi, table_lo, inv_hi, inv_lo, far_hi, far_lo, result_out, result_in, limit_v, face_v, cell_v,
    pack, packs, sides, near, border, turned,
    load_sem, send_sem, recv_sem, ready, beside_in, beside_ok,
):
    levels, count, rows, cols, bands, polar_bands, circle = sizes
    flat = levels * rows
    z = lax.axis_index("lon")
    band = lax.axis_index("lat")
    polar = (band < polar_bands) | (band >= bands - polar_bands)
    has_south = band > 0
    has_north = band < bands - 1
    tail = cols - LANES
    barrier = pltpu.get_barrier_semaphore()

    def load(index, source, target):
        return pltpu.make_async_copy(source, target, load_sem.at[index])

    load_zonal = load(0, courant.at[0], zonal)
    load_cells = load(1, tracers, cells.at[:, :, pl.ds(8, rows), :])
    load_merid = load(2, courant.at[1], merid.at[:, pl.ds(8, rows), :])
    load_limit = load(3, cutoffs, limit_v)
    load_face = load(4, face_w.at[band], face_v)
    load_cell = load(5, cell_w.at[band], cell_v)
    load_tables = [
        load(6, ahead_hi, table_hi),
        load(7, ahead_lo, table_lo),
        load(8, back_hi.at[0], inv_hi),
        load(9, back_lo.at[0], inv_lo),
    ]
    load_far = [load(10, back_hi.at[z], far_hi), load(11, back_lo.at[z], far_lo)]
    load_zonal.start()
    load_cells.start()
    for other in range(1, RINGS):
        @pl.when(z < other)
        def _():
            pl.semaphore_signal(barrier, inc=1, device_id={"lon": other}, device_id_type=MESH)

    near_ring = z == 0

    @pl.when(near_ring & has_south)
    def _():
        pl.semaphore_signal(barrier, inc=1, device_id={"lat": band - 1}, device_id_type=MESH)

    @pl.when(near_ring & has_north)
    def _():
        pl.semaphore_signal(barrier, inc=1, device_id={"lat": band + 1}, device_id_type=MESH)

    beside = has_south.astype(jnp.int32) + has_north.astype(jnp.int32)
    pl.semaphore_wait(barrier, z + jnp.where(near_ring, beside, 0))
    def remote(index, source, target, where, send_index=None):
        return pltpu.make_async_remote_copy(
            src_ref=source,
            dst_ref=target,
            send_sem=send_sem.at[index if send_index is None else send_index],
            recv_sem=recv_sem.at[index],
            device_id=where,
            device_id_type=MESH,
        )

    east = lax.rem(z + 1, RINGS)
    west = lax.rem(z + 3, RINGS)
    across = lax.rem(z + 2, RINGS)
    head = courant.at[0, :, :, pl.ds(0, LANES)]
    tail_rows = pl.ds(0, TAIL_SENT)
    own_tail = tails.at[0, tail_rows]

    class Pair:
        def __init__(self, first, second, sources, slot, where, sends=(None, None)):
            self.head = remote(first, sources[0], heads.at[slot], {"lon": where}, sends[0])
            self.tail = remote(second, sources[1], tails.at[slot, tail_rows], {"lon": where}, sends[1])

        def start(self):
            self.head.start()
            self.tail.start()

        def wait_recv(self):
            self.head.wait_recv()
            self.tail.wait_recv()

        def wait_send(self):
            self.head.wait_send()
            self.tail.wait_send()

    mine = (head, own_tail)
    send_east = Pair(EAST, EAST_TAIL, mine, 3, east)
    send_west = Pair(WEST, WEST_TAIL, mine, 1, west)
    send_across = Pair(ACROSS, ACROSS_TAIL, mine, 2, across)
    pass_west = Pair(ACROSS, ACROSS_TAIL, (heads.at[1], tails.at[1, tail_rows]), 2, west)
    pass_east = Pair(
        ACROSS, ACROSS_TAIL, (heads.at[3], tails.at[3, tail_rows]), 2, east, (PASS, PASS_TAIL)
    )
    pack_east = remote(PACK_EAST, pack.at[0], packs.at[0], {"lon": east})
    pack_west = remote(PACK_WEST, pack.at[1], packs.at[1], {"lon": west})
    send_north = remote(NORTH, sides.at[0], near.at[0], {"lat": band + 1})
    send_south = remote(SOUTH, sides.at[1], near.at[1], {"lat": band - 1})
    second_core = lax.rem(band, 2) == 1
    full = polar & jnp.logical_not(second_core)
    shared = polar & second_core
    middle = (z == 1) | (z == 2)
    gathers = full | (shared & middle)
    helps = shared & middle
    helped = shared & jnp.logical_not(middle)
    early = (
        (send_west, (full & middle) | (shared & (z == 2))),
        (send_east, full & (z == 3)),
        (send_west, shared & (z == 3)),
    )

    for copy, chosen in early:
        @pl.when(chosen)
        def _():
            copy.head.start()

    load_merid.start()
    for other in range(RINGS - 1):
        @pl.when(z > other)
        def _():
            pl.semaphore_signal(ready.at[z], inc=1, device_id={"lon": other}, device_id_type=MESH)

    tails[0, TAIL_SENT - 8 :] = jnp.zeros((TAIL - TAIL_SENT + 8, LANES), jnp.float32)
    load_zonal.wait()
    tails[0, :tail] = zonal[:, :, LANES:].reshape(flat, tail).T
    for copy, chosen in early:
        @pl.when(chosen)
        def _():
            copy.tail.start()

    load_cells.wait()
    tail_lane = lax.broadcasted_iota(jnp.int32, (flat, tail), 1)
    for t in range(count):
        ends = jnp.where(
            tail_lane < tail - 3,
            cells[:, t, 8 : rows + 8, :tail].reshape(flat, tail),
            cells[:, t, 8 : rows + 8, LANES:].reshape(flat, tail),
        ).T
        pack[0, t, 0:3] = ends[tail - 3 :]
        pack[1, t, 0:3] = ends[0:3]
    pack[0, count, 0:1] = tails[0, tail - 1 : tail]

    @pl.when(east < z)
    def _():
        pack_east.start()

    @pl.when(west < z)
    def _():
        pack_west.start()

    @pl.when(shared & (z == 3))
    def _():
        send_across.start()

    load_face.start()
    load_cell.start()

    @pl.when(polar)
    def _():
        load_limit.start()

    @pl.when(gathers)
    def _():
        for copy in load_tables:
            copy.start()

    @pl.when(helps)
    def _():
        for copy in load_far:
            copy.start()

    own[:LANES] = zonal[:, :, :LANES].reshape(flat, LANES).T
    own[LANES:] = tails[0]
    load_merid.wait()
    planes = [(level, t) for level in range(levels) for t in range(count)]
    for k, (level, t) in enumerate(planes):
        sides[0, 3 * k : 3 * k + 3, :cols] = cells[level, t, rows + 5 : rows + 8]
        sides[1, 3 * k : 3 * k + 3, :cols] = cells[level, t, 8:11]
    first_speed = 3 * len(planes)
    for level in range(levels):
        sides[0, first_speed + level, :cols] = merid[level, rows + 7]

    def send_sides(chosen):
        @pl.when(chosen & has_north)
        def _():
            send_north.start()

        @pl.when(chosen & has_south)
        def _():
            send_south.start()

    send_sides(near_ring)
    for slot in range(1, RINGS):
        tails[slot, TAIL_SENT:] = jnp.zeros((TAIL - TAIL_SENT, LANES), jnp.float32)
    border[...] = jnp.zeros_like(border)
    for t in range(count):
        here_out[:, t, :, :LANES] = cells[:, t, 8 : rows + 8, :LANES]
        here_out[:, t, :, LANES:cols] = cells[:, t, 8 : rows + 8, LANES:]
    turned[LANES:, :] = jnp.zeros((LANES, LANES), jnp.float32)

    def signal_beside(semaphore):
        @pl.when(has_south)
        def _():
            pl.semaphore_signal(semaphore, inc=1, device_id={"lat": band - 1}, device_id_type=MESH)

        @pl.when(has_north)
        def _():
            pl.semaphore_signal(semaphore, inc=1, device_id={"lat": band + 1}, device_id_type=MESH)

    def greet(other):
        @pl.when(z < other)
        def _():
            pl.semaphore_wait(ready.at[other], 1)
            for copy, where in ((pack_east, east), (pack_west, west)):
                @pl.when(where == other)
                def _():
                    copy.start()
            for copy, chosen in (
                (send_east, (east == other) & (full | (shared & (z < 2)))),
                (send_west, (west == other) & full),
                (send_across, (across == other) & shared & (z == 0)),
            ):
                @pl.when(chosen)
                def _():
                    copy.start()

    def announce(others):
        for other in others:
            signal_beside(beside_in.at[other])

    def vouch(others):
        for other in others:
            pl.semaphore_wait(beside_in.at[other], beside)
            pl.semaphore_signal(beside_ok, inc=1, device_id={"lon": other}, device_id_type=MESH)

    def block(slot):
        return jnp.concatenate([heads[slot].reshape(flat, LANES).T, tails[slot]], axis=0)

    def forward(slot, values):
        high, low = split_halves(values)
        both = jnp.dot(
            table_hi[slot], jnp.concatenate([high, low], axis=1), preferred_element_type=jnp.float32
        )
        rest_term = jnp.dot(table_lo[slot], high, preferred_element_type=jnp.float32)
        return both[:, :LANES] + (both[:, LANES:] + rest_term)

    greet(1)

    @pl.when(z == 0)
    def _():
        announce((1,))
        vouch((1,))


    @pl.when(full & (z == 3))
    def _():
        send_across.start()
        send_west.start()

    greet(2)

    greet(3)

    @pl.when(z == 1)
    def _():
        pl.semaphore_wait(beside_ok, 1)

    send_sides(z == 1)

    @pl.when(z == 1)
    def _():
        announce((2, 3))

    @pl.when(shared & (z == 1))
    def _():
        send_west.wait_recv()

    @pl.when(full & (z == 1))
    def _():
        send_west.head.wait_recv()
        pass_west.head.start()
        send_west.tail.wait_recv()
        pass_west.tail.start()

    @pl.when(z == 1)
    def _():
        vouch((2, 3))

    @pl.when(polar)
    def _():
        load_limit.wait()

    @pl.when(gathers)
    def _():
        for copy in load_tables:
            copy.wait()
        total[...] = forward(0, own[...])

    @pl.when(helps)
    def _():
        for copy in load_far:
            copy.wait()

    @pl.when(z >= 2)
    def _():
        pl.semaphore_wait(beside_ok, 1)

    send_sides(z >= 2)

    @pl.when(shared & (z == 1))
    def _():
        send_east.wait_recv()

    @pl.when(full & (z == 1))
    def _():
        send_east.head.wait_recv()
        pass_east.head.start()
        send_east.tail.wait_recv()
        pass_east.tail.start()

    @pl.when(shared & (z == 2))
    def _():
        send_east.wait_recv()

    def kept_limit():
        lane = lax.broadcasted_iota(jnp.int32, (8, 2 * LANES), 1)
        spread = jnp.broadcast_to(limit_v[...].reshape(1, bands * rows), (8, bands * rows))
        spread = pltpu.roll(spread, lax.rem((bands - band) * rows, bands * rows), 1)
        limit = jnp.where(lane < rows, spread, 0)
        copies = 1
        while copies < levels:
            limit = limit + pltpu.roll(limit, copies * rows, 1)
            copies *= 2
        return limit[0:1, :LANES]

    send_result = remote(RESULT, result_out, result_in, {"lon": jnp.where(z == 1, 0, RINGS - 1)})

    def wait_second():
        @pl.when(z == 0)
        def _():
            send_east.wait_recv()

        @pl.when(z >= 2)
        def _():
            send_west.wait_recv()

    def last_coefficients(limit, slot):
        wave = lax.broadcasted_iota(jnp.int32, (circle, LANES), 0)
        wave = jnp.where(wave <= circle // 2, wave, wave - circle // 2)
        return jnp.where(wave <= limit, total[...] + forward(slot, block(slot)), 0.0)

    def inverse(coeff, hi_ref, lo_ref):
        high, low = split_halves(coeff)
        both = jnp.dot(
            hi_ref[...], jnp.concatenate([high, low], axis=1), preferred_element_type=jnp.float32
        )
        rest_term = jnp.dot(lo_ref[...], high, preferred_element_type=jnp.float32)
        return both[:, :LANES] + (both[:, LANES:] + rest_term)

    @pl.when(helps)
    def _():
        limit = kept_limit()
        total[...] += forward(3, block(3))
        wait_second()
        total[...] += forward(1, block(1))
        send_across.wait_recv()
        coeff = last_coefficients(limit, 2)
        result_out[...] = inverse(coeff, far_hi, far_lo)
        send_result.start()
        result_in[...] = inverse(coeff, inv_hi, inv_lo)

    def meridional():
        load_face.wait()
        load_cell.wait()

        @pl.when(has_south)
        def _():
            send_north.wait_recv()
            for k, (level, t) in enumerate(planes):
                cells[level, t, 5:8] = near[0, 3 * k : 3 * k + 3, :cols]
            for level in range(levels):
                merid[level, 7] = near[0, first_speed + level, :cols]

        @pl.when(has_north)
        def _():
            send_south.wait_recv()
            for k, (level, t) in enumerate(planes):
                cells[level, t, rows + 8 : rows + 11] = near[1, 3 * k : 3 * k + 3, :cols]

        @pl.when(jnp.logical_not(has_south))
        def _():
            cells[:, :, 0:8, :] = jnp.zeros((levels, count, 8, cols), jnp.float32)
            merid[:, 0:8, :] = jnp.zeros((levels, 8, cols), jnp.float32)

        @pl.when(jnp.logical_not(has_north))
        def _():
            cells[:, :, rows + 8 :, :] = jnp.zeros((levels, count, 8, cols), jnp.float32)

        for level in range(levels):
            speed = merid[level, 7 : rows + 8]
            by_face, by_edge, by_cell = flux_factors(speed, face_v[7 : rows + 8])
            upward = speed > 0
            inverse_cell = cell_v[...]
            for t in range(count):
                def shifted(offset):
                    return cells[level, t, 7 + offset : 8 + offset + rows, :]

                below, here, above, beyond = shifted(-1), shifted(0), shifted(1), shifted(2)
                edge_here = 7.0 * (below + here) - (shifted(-2) + above)
                edge_face = 7.0 * (here + above) - (below + beyond)
                edge_next = 7.0 * (above + beyond) - (here + shifted(3))
                flux = (
                    by_face * edge_face
                    + by_edge * jnp.where(upward, edge_here, edge_next)
                    + by_cell * jnp.where(upward, here, above)
                )
                change = (flux[1:] - flux[:-1]) * inverse_cell
                rest[level, t] = cells[level, t, 8 : rows + 8, :] - change

    @pl.when((z < 2) | shared)
    def _():
        meridional()

    @pl.when(full & (z == 2))
    def _():
        send_east.head.wait_recv()
        pass_east.head.start()
        send_east.tail.wait_recv()
        pass_east.tail.start()

    @pl.when(full)
    def _():
        @pl.when(z == 0)
        def _():
            send_west.wait_recv()

        @pl.when(z == 3)
        def _():
            send_east.wait_recv()

        slot = jnp.where(z == 0, 1, 3)
        total[...] += forward(slot, block(slot))

    wide_lane = lax.broadcasted_iota(jnp.int32, (levels, rows, LANES), 2)
    pack_east.wait_recv()
    pack_west.wait_recv()
    for t in range(count):
        border[t, tail : tail + 3] = packs[1, t, 0:3]
        border[t, LANES - 3 : LANES] = packs[0, t, 0:3]
        halo = border[t].T.reshape(levels, rows, LANES)
        here_out[:, t, :, LANES:] = jnp.where(wide_lane < tail, here_out[:, t, :, LANES:], halo)

    for level in range(levels):
        here = here_out[level]

        def moved(offset):
            return pltpu.roll(here, (-offset) % (2 * LANES), 2)

        back_two, back_one, ahead_one, ahead_two = moved(-2), moved(-1), moved(1), moved(2)
        next_out[level] = ahead_one
        edge_out[level] = 7.0 * (back_one + here) - (back_two + ahead_one)
        face_out[level] = 7.0 * (here + ahead_one) - (back_one + ahead_two)
        beyond_out[level] = 7.0 * (ahead_one + ahead_two) - (here + moved(3))

    def finish(body_rows, west_row):
        turned[:cols] = body_rows
        turned[2 * LANES - 8 :] = jnp.broadcast_to(west_row, (8, LANES))

    @pl.when(jnp.logical_not(polar))
    def _():
        finish(own[:cols], packs[0, count, 0:1])

    def finish_smooth(smooth, limit):
        kept = limit < circle // 2
        finish(
            jnp.where(kept, smooth[:cols], own[:cols]),
            jnp.where(kept, smooth[DEPTH - 1 :], packs[0, count, 0:1]),
        )

    @pl.when(full)
    def _():
        limit = kept_limit()

        @pl.when(z == 0)
        def _():
            send_across.wait_recv()

        @pl.when(z > 0)
        def _():
            wait_second()

        slot = jnp.where(z == 0, 2, 1)
        total[...] += forward(slot, block(slot))

        @pl.when(z == 0)
        def _():
            wait_second()

        @pl.when(z > 0)
        def _():
            send_across.wait_recv()

        coeff = last_coefficients(limit, jnp.where(z == 0, 3, 2))
        finish_smooth(inverse(coeff, inv_hi, inv_lo), limit)

    @pl.when(shared)
    def _():
        limit = kept_limit()

        @pl.when(jnp.logical_not(middle))
        def _():
            send_result.wait_recv()

        finish_smooth(result_in[...], limit)

    faces[:, :, :LANES] = turned[:LANES].T.reshape(levels, rows, LANES)
    faces[:, :, LANES:] = turned[LANES:].T.reshape(levels, rows, LANES)

    @pl.when((z >= 2) & jnp.logical_not(shared))
    def _():
        meridional()

    pack_east.wait_send()
    pack_west.wait_send()

    for copy, chosen in (
        (send_east, full | (shared & (z < 2))),
        (send_west, full | (shared & (z >= 2))),
        (send_across, (polar & (z == 3)) | (shared & (z == 0))),
        (pass_west, full & (z == 1)),
        (pass_east, full & middle),
        (send_result, helps),
    ):
        @pl.when(chosen)
        def _():
            copy.wait_send()

    @pl.when(has_north)
    def _():
        send_north.wait_send()

    @pl.when(has_south)
    def _():
        send_south.wait_send()


def flux_kernel(
    faces, here, following, edge, face_edge, beyond, rest, updated, filtered, result, smooth, sem
):
    levels, _, _, cols = rest.shape
    smooth[...] = faces[:, :, :cols]
    store = pltpu.make_async_copy(smooth, filtered, sem.at[levels])
    store.start()
    for level in range(levels):
        speed = faces[level]
        by_face, by_edge, by_cell = flux_factors(speed, 1.0)
        eastward = speed > 0
        flux = (
            by_face[None] * face_edge[level]
            + by_edge[None] * jnp.where(eastward[None], edge[level], beyond[level])
            + by_cell[None] * jnp.where(eastward[None], here[level], following[level])
        )
        change = flux - pltpu.roll(flux, 1, 2)
        result[level] = rest[level] - change[:, :, :cols]
        pltpu.make_async_copy(result.at[level], updated.at[level], sem.at[level]).start()
    for level in range(levels):
        pltpu.make_async_copy(result.at[level], updated.at[level], sem.at[level]).wait()
    store.wait()


def ring_body(bands, tracers, courant, cutoffs):
    levels, count, rows, cols = tracers.shape
    circle = cols * RINGS
    sizes = (levels, count, rows, cols, bands, bands // 4, circle)
    ahead_hi, ahead_lo, back_hi, back_lo = filter_tables(circle, cols)
    face_w, cell_w = weight_tables(bands, rows, cols)
    hbm = pl.BlockSpec(memory_space=pltpu.HBM)
    vmem = pl.BlockSpec(memory_space=pltpu.VMEM)
    f32, half = jnp.float32, jnp.bfloat16
    slab = (levels, count, rows)
    strip = -(-(3 * levels * count + levels) // 8) * 8
    wide = jax.ShapeDtypeStruct(slab + (2 * LANES,), f32)
    parts = pl.pallas_call(
        functools.partial(gather_kernel, sizes),
        out_shape=(jax.ShapeDtypeStruct((levels, rows, 2 * LANES), f32),)
        + (wide,) * 5
        + (jax.ShapeDtypeStruct(tracers.shape, f32),),
        in_specs=[hbm] * 9,
        out_specs=(vmem,) * 7,
        scratch_shapes=[
            pltpu.VMEM((levels, rows, cols), f32),
            pltpu.VMEM((levels, count, rows + 16, cols), f32),
            pltpu.VMEM((levels, rows + 8, cols), f32),
            pltpu.VMEM((RINGS, levels, rows, LANES), f32),
            pltpu.VMEM((RINGS, TAIL, LANES), f32),
            pltpu.VMEM((DEPTH, LANES), f32),
            pltpu.VMEM((circle, LANES), f32),
            pltpu.VMEM((RINGS, circle, DEPTH), half),
            pltpu.VMEM((RINGS, circle, DEPTH), half),
            pltpu.VMEM((DEPTH, circle), half),
            pltpu.VMEM((DEPTH, circle), half),
            pltpu.VMEM((DEPTH, circle), half),
            pltpu.VMEM((DEPTH, circle), half),
            pltpu.VMEM((DEPTH, LANES), f32),
            pltpu.VMEM((DEPTH, LANES), f32),
            pltpu.VMEM((bands * rows,), jnp.int32),
            pltpu.VMEM((rows + 8, cols), f32),
            pltpu.VMEM((rows, cols), f32),
            pltpu.VMEM((2, count + 1, 8, LANES), f32),
            pltpu.VMEM((2, count + 1, 8, LANES), f32),
            pltpu.VMEM((2, strip, 2 * LANES), f32),
            pltpu.VMEM((2, strip, 2 * LANES), f32),
            pltpu.VMEM((count, LANES, LANES), f32),
            pltpu.VMEM((2 * LANES, LANES), f32),
            pltpu.SemaphoreType.DMA((12,)),
            pltpu.SemaphoreType.DMA((13,)),
            pltpu.SemaphoreType.DMA((13,)),
            pltpu.SemaphoreType.REGULAR((RINGS,)),
            pltpu.SemaphoreType.REGULAR((RINGS,)),
            pltpu.SemaphoreType.REGULAR,
        ],
        compiler_params=pltpu.CompilerParams(
            collective_id=0, has_side_effects=True, vmem_limit_bytes=24 * 2**20
        ),
    )(
        *(
            pltpu.with_memory_space_constraint(jnp.asarray(operand), pltpu.HBM)
            for operand in (
                tracers, courant, cutoffs, ahead_hi, ahead_lo, back_hi, back_lo, face_w, cell_w
            )
        )
    )
    return pl.pallas_call(
        flux_kernel,
        out_shape=(
            jax.ShapeDtypeStruct(tracers.shape, f32),
            jax.ShapeDtypeStruct((levels, rows, cols), f32),
        ),
        in_specs=[vmem] * 7,
        out_specs=(hbm, hbm),
        scratch_shapes=[
            pltpu.VMEM(tracers.shape, f32),
            pltpu.VMEM((levels, rows, cols), f32),
            pltpu.SemaphoreType.DMA((levels + 1,)),
        ],
        compiler_params=pltpu.CompilerParams(vmem_limit_bytes=16 * 2**20),
    )(*parts)


def body(bands, tracers, courant, cutoffs):
    levels, _, rows, cols = tracers.shape
    fits = (
        lax.axis_size("lon") == RINGS
        and bands % 4 == 0
        and bands * rows == 2 * LANES
        and levels * rows == LANES
        and LANES < cols <= LANES + TAIL_SENT - 4
        and bands % 8 == 0
        and cols % 4 == 0
    )
    if fits:
        return ring_body(bands, tracers, courant, cutoffs)
    return general_body(tracers, courant, cutoffs)


def solution(mesh):
    in_specs = (P(None, None, "lat", "lon"), P(None, None, "lat", "lon"), P())
    out_specs = (P(None, None, "lat", "lon"), P(None, "lat", "lon"))
    return jax.shard_map(
        functools.partial(body, mesh.shape["lat"]),
        mesh=mesh,
        in_specs=in_specs,
        out_specs=out_specs,
        check_vma=False,
    )
```
